32 devices in a mesh: tok: 8 (over y, x, core), head: 4 (over z).
Axes of the slice: x: 2, y: 2, z: 4, core: 2. Of those that a mesh axis runs over, the one named last changes fastest.
Arguments:
- pre_tokens: bfloat16 [8192, 2048], P('tok'), may hold values from -6 to 6
- dec_tokens: bfloat16 [16, 2048], P('tok'), may hold values from -6 to 6
- attn_gain: float32 [2048], replicated, may hold values from 0.1 to 1.9
- mlp_gain: float32 [2048], replicated, may hold values from 0.1 to 1.9
- w_qkv: bfloat16 [3, 2048, 2048], P(None, 'head', 'tok'), may hold values from -0.125 to 0.125
- w_out: bfloat16 [2048, 2048], P('tok', 'head'), may hold values from -0.125 to 0.125
- w_gate_up: bfloat16 [2, 8192, 2048], P(None, 'head', 'tok'), may hold values from -0.125 to 0.125
- w_down: bfloat16 [2048, 8192], P('tok', 'head'), may hold values from -0.0625 to 0.0625
- pre_cache: bfloat16 [8, 2, 2048, 2048], P('tok', None, None, 'head'), may hold values from -60 to 60
- dec_cache: bfloat16 [16, 2, 4096, 2048], P('tok', None, None, 'head'), may hold values from -60 to 60
- pre_order: int32 [8], replicated, may hold values from 0 to 7, each once
- dec_order: int32 [16], replicated, may hold values from 0 to 15, each once
- pre_offsets: int32 [8], P('tok'), may hold values from 2 to 2048, as said below
- dec_lengths: int32 [16], P('tok'), may hold values from 2 to 4096, as said below
Outputs:
- pre_out: bfloat16 [8192, 2048], P('tok')
- dec_out: bfloat16 [16, 2048], P('tok')
The draws below stay inside these ranges and needn't reach their ends.
Inputs may be any that keep to these rules, and one draw needn't show every extreme that they name: `pre_order`: the prefill request at position k is handled with the caches of position k, which lie on index k of tok. `dec_order`: positions k of one index of tok are those with k // 2 equal to it. `pre_offsets`: some position reaches 2048. `dec_lengths`: some position reaches 4096.
All inputs are finite; a program needn't handle non-finite values.
Results may differ from the reference program's by a relative error of at most 0.013.
Values may be sent and summed in bfloat16 or wider, within the bound.
A program may use at most 192 MiB of HBM per device.

```python
import jax
import jax.numpy as jnp
from jax import lax

D = 2048
HEADS = 32
HD = 64
FF = 8192
SPAN = 1024
PREFIX = 2048
CACHE = 4096
PF = 8
DEC = 16
N_TOK = 8


def cache_draw(key, count, length):
    first_key = jax.random.fold_in(jax.random.fold_in(key, 7), 0)
    shape = (count, 2, length, HEADS * HD)
    return jnp.clip(jax.random.normal(first_key, shape, jnp.float32), -6.0, 6.0)


def draw_pre_cache(key, part):
    return cache_draw(key, PF, PREFIX).astype(jnp.bfloat16)


def draw_dec_cache(key, part):
    return cache_draw(key, DEC, CACHE).astype(jnp.bfloat16)


def bounded_counts(key, count, largest):
    first_key, second_key = jax.random.split(jax.random.fold_in(key, 11))
    values = jax.random.randint(first_key, (count,), 2, largest + 1)
    chosen = jax.random.randint(second_key, (), 0, count)
    return jnp.where(jnp.arange(count) == chosen, largest, values).astype(jnp.int32)


def draw_pre_offsets(key, part):
    return bounded_counts(key, PF, PREFIX)


def draw_dec_lengths(key, part):
    return bounded_counts(key, DEC, CACHE)


def level_of(stream_key, extent, cuts, smallest, top_value):
    loudness, own = 1.0, jax.random.fold_in(stream_key, 6)
    for axis_at, shards_of in cuts:
        heights = jnp.exp(jax.random.uniform(jax.random.fold_in(own, axis_at), (shards_of,), jnp.float32, smallest / len(cuts), top_value / len(cuts)))
        loudness = loudness * jnp.repeat(heights, extent[axis_at] // shards_of).reshape([-1 if axis == axis_at else 1 for axis in range(len(extent))])
    return loudness


def centred(own_key, shape, scale, bound, cuts=(), held_as=jnp.bfloat16):
    result = scale * jax.random.normal(own_key, shape, jnp.float32)
    if cuts:
        result = result * level_of(own_key, shape, cuts, -0.22, 0.18)
    return jnp.clip(result, -bound, bound).astype(held_as)


def setup_inputs(seed: int = 0) -> dict:
    keys = jax.random.split(jax.random.key(seed), 15)
    return {
        "pre_tokens": centred(keys[0], (PF * SPAN, D), 1.0, 6.0, ((0, 8),)),
        "dec_tokens": centred(keys[1], (DEC, D), 1.0, 6.0, ((0, 8),)),
        "attn_gain": jnp.clip(1.0 + 0.18 * jax.random.normal(keys[2], (D,), jnp.float32), 0.1, 1.9),
        "mlp_gain": jnp.clip(1.0 + 0.18 * jax.random.normal(keys[3], (D,), jnp.float32), 0.1, 1.9),
        "w_qkv": centred(keys[4], (3, HEADS * HD, D), D ** -0.5, 0.125, ((1, 4), (2, 8))),
        "w_out": centred(keys[5], (D, HEADS * HD), (HEADS * HD) ** -0.5, 0.125, ((0, 8), (1, 4))),
        "w_gate_up": centred(keys[6], (2, FF, D), D ** -0.5, 0.125, ((1, 4), (2, 8))),
        "w_down": centred(keys[7], (D, FF), FF ** -0.5, 0.0625, ((0, 8), (1, 4))),
        "pre_cache": draw_pre_cache(jax.random.fold_in(keys[14], 71), 0),
        "dec_cache": draw_dec_cache(jax.random.fold_in(keys[14], 71), 0),
        "pre_order": jax.random.permutation(keys[10], PF).astype(jnp.int32),
        "dec_order": jax.random.permutation(keys[11], DEC).astype(jnp.int32),
        "pre_offsets": draw_pre_offsets(jax.random.fold_in(keys[14], 71), 0),
        "dec_lengths": draw_dec_lengths(jax.random.fold_in(keys[14], 71), 0),
    }


rope_base = 130000.0
norm_eps = 1e-05

def rotate(values, positions):
    width = values.shape[-1]
    half = width // 2
    freqs = rope_base ** (-(jnp.arange(half, dtype=jnp.float32) * 2.0 / width))
    angles = positions.astype(jnp.float32)[:, None] * freqs[None, :]
    cosine = jnp.cos(angles)[:, None, :]
    sine = jnp.sin(angles)[:, None, :]
    first = values[..., :half]
    second = values[..., half:]
    return jnp.concatenate([first * cosine - second * sine, second * cosine + first * sine], axis=-1)

def rms_norm(rows, gain):
    rows = rows.astype(jnp.float32)
    factor = lax.rsqrt(lax.optimization_barrier(jnp.mean(rows * rows, axis=-1, keepdims=True)) + norm_eps)
    return (rows * factor * gain).astype(jnp.bfloat16)

def attend(query, keys_new, values_new, cache, limit, positions, self_mask):
    rows_q = query.shape[0]
    heads = query.shape[1]
    size = query.shape[2]
    q_rot = rotate(query.astype(jnp.float32), positions).astype(jnp.bfloat16)
    k_rot = rotate(keys_new.astype(jnp.float32), positions).astype(jnp.bfloat16)
    length = cache.shape[1]
    cached_keys = cache[0].reshape(length, heads, size)
    cached_values = cache[1].reshape(length, heads, size)
    all_keys = jnp.concatenate([cached_keys, k_rot], axis=0)
    all_values = jnp.concatenate([cached_values, values_new], axis=0)
    scores = jnp.einsum('qhd,khd->hqk', q_rot.astype(jnp.float32), all_keys.astype(jnp.float32)) / jnp.sqrt(jnp.float32(size))
    cache_live = jnp.broadcast_to(jnp.arange(length, dtype=jnp.int32)[None, :] < limit, (rows_q, length))
    valid = jnp.concatenate([cache_live, self_mask], axis=1)
    scores = jnp.where(valid[None], scores, -jnp.inf)
    top = lax.optimization_barrier(jnp.max(scores, axis=-1, keepdims=True))
    weights = jnp.exp(scores - top)
    total = lax.optimization_barrier(jnp.sum(weights, axis=-1))
    mixed = jnp.einsum('hqk,khd->qhd', weights.astype(jnp.bfloat16).astype(jnp.float32), all_values.astype(jnp.float32))
    mixed = mixed / jnp.transpose(total)[:, :, None]
    return mixed.astype(jnp.bfloat16).reshape(rows_q, heads * size)

def inverse_of(order, count):
    return jnp.zeros((count,), jnp.int32).at[order].set(jnp.arange(count, dtype=jnp.int32))

def reference(pre_tokens, dec_tokens, attn_gain, mlp_gain, w_qkv, w_out, w_gate_up, w_down, pre_cache, dec_cache, pre_order, dec_order, pre_offsets, dec_lengths):
    piece_len = SPAN // N_TOK
    width = HEADS * HD
    rows = jnp.concatenate([pre_tokens, dec_tokens], axis=0)
    normed = rms_norm(rows, attn_gain)
    projected = jnp.dot(normed, w_qkv.reshape(3 * width, D).T, preferred_element_type=jnp.float32).astype(jnp.bfloat16)
    projected = projected.reshape(-1, 3, HEADS, HD)
    pre_part = projected[:PF * SPAN].reshape(N_TOK, PF, piece_len, 3, HEADS, HD)
    pre_part = jnp.transpose(pre_part, (1, 0, 2, 3, 4, 5)).reshape(PF, SPAN, 3, HEADS, HD)
    by_position = pre_part[pre_order]
    causal = jnp.arange(SPAN, dtype=jnp.int32)[None, :] <= jnp.arange(SPAN, dtype=jnp.int32)[:, None]

    def prefill_one(item):
        block, cache, offset = item
        positions = offset + jnp.arange(SPAN, dtype=jnp.int32)
        return attend(block[:, 0], block[:, 1], block[:, 2], cache, offset, positions, causal)
    pre_att = lax.map(prefill_one, (by_position, pre_cache, pre_offsets))
    pre_att = pre_att[inverse_of(pre_order, PF)]
    pre_att = jnp.transpose(pre_att.reshape(PF, N_TOK, piece_len, width), (1, 0, 2, 3)).reshape(PF * SPAN, width)
    dec_part = projected[PF * SPAN:][dec_order]
    self_only = jnp.ones((1, 1), jnp.bool_)

    def decode_one(item):
        block, cache, length = item
        positions = jnp.reshape(length, (1,))
        return attend(block[None, 0], block[None, 1], block[None, 2], cache, length, positions, self_only)
    dec_att = lax.map(decode_one, (dec_part, dec_cache, dec_lengths)).reshape(DEC, width)
    dec_att = dec_att[inverse_of(dec_order, DEC)]
    attended = jnp.concatenate([pre_att, dec_att], axis=0)
    resid = rows.astype(jnp.float32) + jnp.dot(attended, w_out.T, preferred_element_type=jnp.float32)
    mlp_in = rms_norm(resid, mlp_gain)
    gate_up = jnp.dot(mlp_in, w_gate_up.reshape(2 * FF, D).T, preferred_element_type=jnp.float32)
    hidden = (jax.nn.silu(gate_up[:, :FF]) * gate_up[:, FF:]).astype(jnp.bfloat16)
    final = (resid + jnp.dot(hidden, w_down.T, preferred_element_type=jnp.float32)).astype(jnp.bfloat16)
    return (final[:PF * SPAN], final[PF * SPAN:])
```

```python
import functools

import jax
import jax.numpy as jnp
from jax import lax
from jax.experimental import pallas as pl
from jax.experimental.pallas import tpu as pltpu
from jax.sharding import PartitionSpec as P

HD = 64
Q_ROWS = 512
K_ROWS = 512
DEC_ROWS = 1024
DEC_PAD = 16


rope_base = 130000.0
norm_eps = 1e-05
masked_score = -1e30


def rotate(values, positions):
    width = values.shape[-1]
    half = width // 2
    freqs = rope_base ** (-(jnp.arange(half, dtype=jnp.float32) * 2.0 / width))
    angles = positions.astype(jnp.float32)[:, None] * freqs[None, :]
    cosine = jnp.cos(angles)[:, None, :]
    sine = jnp.sin(angles)[:, None, :]
    first = values[..., :half]
    second = values[..., half:]
    return jnp.concatenate(
        [first * cosine - second * sine, second * cosine + first * sine], axis=-1
    )


def rms_norm(rows, gain):
    rows = rows.astype(jnp.float32)
    factor = lax.rsqrt(jnp.mean(rows * rows, axis=-1, keepdims=True) + norm_eps)
    return (rows * factor * gain).astype(jnp.bfloat16)


def fold_rows(inputs, weights):
    return jnp.einsum("td,kcd->ktc", inputs, weights, preferred_element_type=jnp.float32)


def map_rows(inputs, weights):
    return jnp.einsum("tc,dc->td", inputs, weights, preferred_element_type=jnp.float32)


def whole(weights, axis):
    return lax.all_gather(weights, "tok", axis=axis, tiled=True)


def to_heads(blocks):
    return lax.all_to_all(blocks, "head", split_axis=0, concat_axis=0, tiled=True)


def from_heads(rows):
    return lax.all_gather(rows, "head", axis=0, tiled=True)


def sum_heads(partial_value):
    return lax.psum_scatter(
        partial_value.astype(jnp.bfloat16), "head", scatter_dimension=0, tiled=True
    )


def after(first, second):
    return lax.optimization_barrier((first, second))


def rope_tables(positions, width):
    half = HD // 2
    freqs = rope_base ** (-(jnp.arange(half, dtype=jnp.float32) * 2.0 / HD))
    angles = positions.astype(jnp.float32)[:, None] * freqs[None, :]
    cosine = jnp.cos(angles)
    sine = jnp.sin(angles)
    copies = width // HD
    return (
        jnp.tile(jnp.concatenate([cosine, cosine], axis=1), (1, copies)),
        jnp.tile(jnp.concatenate([-sine, sine], axis=1), (1, copies)),
    )


def swap_halves(values):
    half = HD // 2
    width = values.shape[-1]
    lane = lax.broadcasted_iota(jnp.int32, values.shape, values.ndim - 1)
    axis = values.ndim - 1
    return jnp.where(
        lane % HD < half,
        pltpu.roll(values, width - half, axis),
        pltpu.roll(values, half, axis),
    )


def prefill_kernel(
    limit_ref, q_ref, k_ref, v_ref, cos_ref, sin_ref, cache_ref, out_ref, q_rot, k_rot, v_ext, c_ext
):
    span = q_ref.shape[1]
    length = cache_ref.shape[2]
    pair = q_ref.shape[2]
    limit = limit_ref[0]
    cosine = cos_ref[...]
    sine = sin_ref[...]
    lane = lax.broadcasted_iota(jnp.int32, (1, pair), 1)
    halves = (lane < HD, lane >= HD)

    key = k_ref[0].astype(jnp.float32)
    k_rot[...] = (key * cosine + swap_halves(key) * sine).astype(jnp.bfloat16)
    query = q_ref[0].astype(jnp.float32)
    query = (query * cosine + swap_halves(query) * sine).astype(jnp.bfloat16)
    query = query * jnp.bfloat16(HD**-0.5)
    one = jnp.ones((), jnp.bfloat16)
    zero = jnp.zeros((), jnp.bfloat16)
    for side in range(2):
        q_rot[side] = jnp.where(halves[side], query, zero)
        v_ext[side] = jnp.where(halves[side], v_ref[0], one)
        c_ext[side] = jnp.where(halves[side], cache_ref[0, 1], one)

    def score(rows, keys):
        return lax.dot_general(
            rows, keys, (((1,), (1,)), ((), ())), preferred_element_type=jnp.float32
        )

    def fold(state, scores, values):
        top, mixed = state
        new_top = jnp.maximum(top, jnp.max(scores, axis=-1, keepdims=True))
        weights = jnp.exp(scores - new_top).astype(jnp.bfloat16)
        factor = jnp.exp(top - new_top)
        return new_top, mixed * factor + jnp.dot(
            weights, values, preferred_element_type=jnp.float32
        )

    for block in range(span // Q_ROWS):
        start = block * Q_ROWS
        rows = [q_rot[side, start : start + Q_ROWS, :] for side in range(2)]
        keys = k_rot[start : start + Q_ROWS, :]
        shape = (Q_ROWS, Q_ROWS)
        seen = lax.broadcasted_iota(jnp.int32, shape, 1) <= lax.broadcasted_iota(
            jnp.int32, shape, 0
        )
        states = []
        for side in range(2):
            scores = jnp.where(seen, score(rows[side], keys), masked_score)
            top = jnp.max(scores, axis=-1, keepdims=True)
            weights = jnp.exp(scores - top).astype(jnp.bfloat16)
            mixed = jnp.dot(
                weights,
                v_ext[side, start : start + Q_ROWS, :],
                preferred_element_type=jnp.float32,
            )
            states.append((top, mixed))
        for earlier in range(block):
            begin = earlier * Q_ROWS
            keys = k_rot[begin : begin + Q_ROWS, :]
            for side in range(2):
                states[side] = fold(
                    states[side],
                    score(rows[side], keys),
                    v_ext[side, begin : begin + Q_ROWS, :],
                )

        def cached(index, state, masked):
            begin = pl.multiple_of(index * K_ROWS, K_ROWS)
            keys_now = cache_ref[0, 0, pl.ds(begin, K_ROWS), :]
            result = []
            for side in range(2):
                scores = score(rows[side], keys_now)
                if masked:
                    spot = begin + lax.broadcasted_iota(jnp.int32, (1, K_ROWS), 1)
                    scores = jnp.where(spot < limit, scores, masked_score)
                result.append(
                    fold(state[side], scores, c_ext[side, pl.ds(begin, K_ROWS), :])
                )
            return tuple(result)

        full = limit // K_ROWS
        every = (limit + K_ROWS - 1) // K_ROWS
        states = lax.fori_loop(0, full, lambda i, s: cached(i, s, False), tuple(states))
        states = lax.fori_loop(full, every, lambda i, s: cached(i, s, True), states)
        parts = []
        for side in range(2):
            mixed = states[side][1]
            total = pltpu.roll(mixed, HD, 1)
            parts.append(mixed / total)
        out_ref[start : start + Q_ROWS, :] = jnp.where(halves[0], parts[0], parts[1]).astype(
            jnp.bfloat16
        )


def prefill_attend(qkv, offset, cache):
    _, span, width = qkv.shape
    length = cache.shape[2]
    pair = 2 * HD
    cosine, sine = rope_tables(offset + jnp.arange(span, dtype=jnp.int32), pair)
    part = lambda which: pl.BlockSpec((1, span, pair), lambda p, limit: (which, 0, p))
    table = pl.BlockSpec((span, pair), lambda p, limit: (0, 0))
    return pl.pallas_call(
        prefill_kernel,
        out_shape=jax.ShapeDtypeStruct((span, width), jnp.bfloat16),
        grid_spec=pltpu.PrefetchScalarGridSpec(
            num_scalar_prefetch=1,
            grid=(width // pair,),
            in_specs=[
                part(0),
                part(1),
                part(2),
                table,
                table,
                pl.BlockSpec((1, 2, length, pair), lambda p, limit: (0, 0, 0, p)),
            ],
            out_specs=pl.BlockSpec((span, pair), lambda p, limit: (0, p)),
            scratch_shapes=[
                pltpu.VMEM((2, span, pair), jnp.bfloat16),
                pltpu.VMEM((span, pair), jnp.bfloat16),
                pltpu.VMEM((2, span, pair), jnp.bfloat16),
                pltpu.VMEM((2, length, pair), jnp.bfloat16),
            ],
        ),
        compiler_params=pltpu.CompilerParams(vmem_limit_bytes=40 * 1024 * 1024),
        cost_estimate=pl.CostEstimate(
            flops=16 * span * 3 * span * width,
            bytes_accessed=4 * length * width + 8 * span * width,
            transcendentals=span * 3 * span * width // HD,
        ),
        name="prefill_attend",
    )(offset[None], qkv, qkv, qkv, cosine, sine, cache)


def decode_kernel(limits_ref, q_ref, k_ref, v_ref, cache_ref, out_ref, top_ref, total_ref, mixed_ref):
    request = pl.program_id(0)
    index = pl.program_id(1)
    limit = limits_ref[request]
    heads, width = q_ref.shape[1:]
    block = cache_ref.shape[2]

    @pl.when(index == 0)
    def _():
        own = q_ref[0].astype(jnp.float32) * k_ref[0].astype(jnp.float32)
        top_ref[...] = jnp.sum(own, axis=-1, keepdims=True)
        total_ref[...] = jnp.ones_like(total_ref)
        mixed_ref[...] = jnp.broadcast_to(v_ref[0].astype(jnp.float32), (heads, width))

    @pl.when(index * block < limit)
    def _():
        scores = lax.dot_general(
            q_ref[0],
            cache_ref[0, 0],
            (((1,), (1,)), ((), ())),
            preferred_element_type=jnp.float32,
        )
        spot = index * block + lax.broadcasted_iota(jnp.int32, (1, block), 1)
        scores = jnp.where(spot < limit, scores, masked_score)
        top = top_ref[...]
        new_top = jnp.maximum(top, jnp.max(scores, axis=-1, keepdims=True))
        weights = jnp.exp(scores - new_top)
        factor = jnp.exp(top - new_top)
        top_ref[...] = new_top
        total_ref[...] = total_ref[...] * factor + jnp.sum(weights, axis=-1, keepdims=True)
        mixed_ref[...] = mixed_ref[...] * factor + jnp.dot(
            weights.astype(jnp.bfloat16), cache_ref[0, 1], preferred_element_type=jnp.float32
        )

    @pl.when(index == pl.num_programs(1) - 1)
    def _():
        shape = (heads, width)
        mine = lax.broadcasted_iota(jnp.int32, shape, 1) // HD == lax.broadcasted_iota(
            jnp.int32, shape, 0
        )
        value = jnp.where(mine, mixed_ref[...] / total_ref[...], 0.0)
        out_ref[0] = jnp.sum(value, axis=0, keepdims=True).astype(jnp.bfloat16)


def decode_attend(qkv, lengths, cache):
    _, count, width = qkv.shape
    heads = width // HD
    block = min(DEC_ROWS, cache.shape[2])
    split = qkv.reshape(3, count, heads, HD)
    q_rot = rotate(split[0].astype(jnp.float32), lengths).astype(jnp.bfloat16)
    k_rot = rotate(split[1].astype(jnp.float32), lengths).astype(jnp.bfloat16)
    q_rot = q_rot * jnp.bfloat16(HD**-0.5)
    spread = jnp.where(
        jnp.eye(heads, dtype=jnp.bool_)[None, :, :, None], q_rot[:, None], jnp.bfloat16(0)
    ).reshape(count, heads, width)

    def cache_at(request, index, limits):
        last = (limits[request] - 1) // block
        return (request, 0, jnp.minimum(index, last), 0)

    row = pl.BlockSpec((1, 1, width), lambda request, index, limits: (request, 0, 0))
    return pl.pallas_call(
        decode_kernel,
        out_shape=jax.ShapeDtypeStruct((count, 1, width), jnp.bfloat16),
        grid_spec=pltpu.PrefetchScalarGridSpec(
            num_scalar_prefetch=1,
            grid=(count, cache.shape[2] // block),
            in_specs=[
                pl.BlockSpec((1, heads, width), lambda request, index, limits: (request, 0, 0)),
                row,
                row,
                pl.BlockSpec((1, 2, block, width), cache_at),
            ],
            out_specs=row,
            scratch_shapes=[
                pltpu.VMEM((heads, 1), jnp.float32),
                pltpu.VMEM((heads, 1), jnp.float32),
                pltpu.VMEM((heads, width), jnp.float32),
            ],
        ),
        compiler_params=pltpu.CompilerParams(vmem_limit_bytes=32 * 1024 * 1024),
        cost_estimate=pl.CostEstimate(
            flops=4 * count * heads * cache.shape[2] * width,
            bytes_accessed=4 * count * cache.shape[2] * width,
            transcendentals=count * cache.shape[2] * heads,
        ),
        name="decode_attend",
    )(lengths, spread, k_rot.reshape(count, 1, width), qkv[2].reshape(count, 1, width), cache)[:, 0]


MESH = pl.DeviceIdType.MESH
CHUNK = 64
TILE = 512


def nt_dot(rows, weights):
    return lax.dot_general(
        rows, weights, (((1,), (1,)), ((), ())), preferred_element_type=jnp.float32
    )


def tiles_of(extent):
    tile = min(TILE, extent)
    return tile, extent // tile


def mlp_kernel(
    head_count,
    att_ref,
    rows_ref,
    dec_att_ref,
    dec_rows_ref,
    gain_ref,
    w_out_ref,
    w_gu_ref,
    w_down_ref,
    out_ref,
    dec_out_ref,
    x_v,
    r_v,
    w_out_v,
    w_gu_v,
    w_down_v,
    resid,
    mlp_in,
    hidden,
    partial,
    dec_resid,
    slots,
    dec_slots,
    in_sem,
    load_sem,
    rs_send,
    rs_recv,
    ag_send,
    ag_recv,
    keep_sem,
    dec_send,
    dec_recv,
):
    last = head_count - 1
    me = lax.axis_index("head")
    span, width = att_ref.shape
    half = span // 2
    count = half // CHUNK
    wide = 2 * CHUNK
    pieces, _, units, piece = w_gu_ref.shape
    dec = dec_att_ref.shape[0]

    loads = [
        pltpu.make_async_copy(w_out_ref, w_out_v, load_sem.at[0]),
        pltpu.make_async_copy(w_gu_ref, w_gu_v, load_sem.at[1]),
        pltpu.make_async_copy(w_down_ref, w_down_v, load_sem.at[2]),
    ]

    def inputs(step, slot):
        copies = []
        for which, (source, target) in enumerate(((att_ref, x_v), (rows_ref, r_v))):
            for side in range(2):
                begin = pl.multiple_of(side * half + step * CHUNK, CHUNK)
                copies.append(
                    pltpu.make_async_copy(
                        source.at[pl.ds(begin, CHUNK)],
                        target.at[slot, pl.ds(side * CHUNK, CHUNK)],
                        in_sem.at[slot, which, side],
                    )
                )
        return copies

    for copy in inputs(0, 0):
        copy.start()
    for copy in loads:
        copy.start()
    for slot in range(2):
        x_v[slot, wide:, :] = dec_att_ref[...]
        r_v[slot, wide:, :] = dec_rows_ref[...]

    barrier = pltpu.get_barrier_semaphore()
    for offset in range(1, head_count):
        pl.semaphore_signal(
            barrier,
            inc=1,
            device_id={"head": lax.rem(me + offset, head_count)},
            device_id_type=MESH,
        )
    pl.semaphore_wait(barrier, head_count - 1)

    spot = lax.broadcasted_iota(jnp.int32, (wide, 1), 0)
    owner = jnp.where(spot < CHUNK, 0, last)
    owned = jnp.where(owner == me, 1.0, 0.0).astype(jnp.float32)

    def compute(step):
        slot = lax.rem(step, 2)

        @pl.when(step + 1 < count)
        def _():
            for copy in inputs(step + 1, lax.rem(step + 1, 2)):
                copy.start()

        for copy in inputs(step, slot):
            copy.wait()

        @pl.when(step == 0)
        def _():
            loads[0].wait()

        out_tile, out_tiles = tiles_of(width)

        def project(index, squares):
            begin = pl.multiple_of(index * out_tile, out_tile)
            value = nt_dot(x_v[slot], w_out_v[pl.ds(begin, out_tile), :])
            value = value + r_v[slot, :, pl.ds(begin, out_tile)].astype(jnp.float32)
            resid[:, pl.ds(begin, out_tile)] = value
            return squares + jnp.sum(value * value, axis=-1, keepdims=True)

        squares = lax.fori_loop(
            0, out_tiles, project, jnp.zeros((wide + dec, 1), jnp.float32)
        )
        factor = lax.rsqrt(squares / width + norm_eps)
        mlp_in[...] = (resid[...] * factor * gain_ref[...]).astype(jnp.bfloat16)

        @pl.when(step == 0)
        def _():
            loads[1].wait()

        unit_tile, unit_tiles = tiles_of(units)

        def gate_up(index, carry):
            begin = pl.multiple_of(index * unit_tile, unit_tile)
            sums = [None, None]
            for which in range(2):
                for part in range(pieces):
                    term = nt_dot(
                        mlp_in[:, part * piece : (part + 1) * piece],
                        w_gu_v[part, which, pl.ds(begin, unit_tile), :],
                    )
                    sums[which] = term if part == 0 else sums[which] + term
            gate, up = sums
            hidden[:, pl.ds(begin, unit_tile)] = (
                gate / (1.0 + jnp.exp(-gate)) * up
            ).astype(jnp.bfloat16)
            return carry

        lax.fori_loop(0, unit_tiles, gate_up, 0)

        @pl.when(step == 0)
        def _():
            loads[2].wait()

        def down(index, carry):
            begin = pl.multiple_of(index * out_tile, out_tile)
            value = nt_dot(hidden[...], w_down_v[pl.ds(begin, out_tile), :])
            columns = pl.ds(begin, out_tile)
            partial[step, :, columns] = value[:wide] + resid[:wide, columns] * owned

            @pl.when(step == 0)
            def _():
                dec_slots[me, :, columns] = value[wide:].astype(jnp.bfloat16)

            return carry

        lax.fori_loop(0, out_tiles, down, 0)

        @pl.when(step == 0)
        def _():
            dec_resid[...] = resid[wide:, :]
            for offset in range(1, head_count):
                dec_copy(offset).start()

    def dec_copy(offset):
        return pltpu.make_async_remote_copy(
            src_ref=dec_slots.at[me],
            dst_ref=dec_slots.at[me],
            send_sem=dec_send.at[offset],
            recv_sem=dec_recv.at[offset],
            device_id={"head": lax.rem(me + offset, head_count)},
            device_id_type=MESH,
        )

    def out_rows(side, index):
        return out_ref.at[pl.ds(pl.multiple_of(side * half + index * CHUNK, CHUNK), CHUNK)]

    def next_of(side):
        return jnp.maximum(me - 1, 0) if side == 0 else jnp.minimum(me + 1, last)

    def before_of(side):
        return next_of(1 - side)

    def sum_copy(side, index):
        return pltpu.make_async_remote_copy(
            src_ref=slots.at[side, index],
            dst_ref=slots.at[side, index],
            send_sem=rs_send.at[side, index],
            recv_sem=rs_recv.at[side, index],
            device_id={"head": next_of(side)},
            device_id_type=MESH,
        )

    def final_copy(side, index, source):
        return pltpu.make_async_remote_copy(
            src_ref=source,
            dst_ref=out_rows(side, index),
            send_sem=ag_send.at[side, index],
            recv_sem=ag_recv.at[side, index],
            device_id={"head": before_of(side)},
            device_id_type=MESH,
        )

    def keep_copy(side, index):
        return pltpu.make_async_copy(
            slots.at[side, index], out_rows(side, index), keep_sem.at[side, index]
        )

    hops = [last - me, me]
    to_end = [me, last - me]

    def combine(side, index):
        mine = partial.at[index, pl.ds(side * CHUNK, CHUNK)]

        @pl.when(hops[side] == 0)
        def _():
            slots[side, index] = mine[...].astype(jnp.bfloat16)

        @pl.when(hops[side] > 0)
        def _():
            sum_copy(side, index).wait_recv()
            slots[side, index] = (
                mine[...] + slots[side, index].astype(jnp.float32)
            ).astype(jnp.bfloat16)

        @pl.when(to_end[side] > 0)
        def _():
            sum_copy(side, index).start()

        @pl.when(to_end[side] == 0)
        def _():
            final_copy(side, index, slots.at[side, index]).start()
            keep_copy(side, index).start()

    def forward(side, index):
        final_copy(side, index, out_rows(side, index)).wait_recv()

        @pl.when(hops[side] > 0)
        def _():
            final_copy(side, index, out_rows(side, index)).start()

    def tick(step, carry):
        @pl.when(step < count)
        def _():
            compute(step)

        for side in range(2):
            index = step - hops[side]

            @pl.when(jnp.logical_and(index >= 0, index < count))
            def _():
                combine(side, index)

        for side in range(2):
            spread = step - last - to_end[side]

            @pl.when(
                jnp.logical_and(
                    to_end[side] > 0, jnp.logical_and(spread >= 0, spread < count)
                )
            )
            def _():
                forward(side, spread)

        return carry

    lax.fori_loop(0, count + 2 * last, tick, 0)

    for offset in range(1, head_count):
        dec_copy(offset).wait()
    total = dec_resid[...]
    for index in range(head_count):
        total = total + dec_slots[index].astype(jnp.float32)
    dec_out_ref[...] = total.astype(jnp.bfloat16)

    def drain(index, carry):
        for side in range(2):

            @pl.when(to_end[side] > 0)
            def _():
                sum_copy(side, index).wait_send()

            @pl.when(to_end[side] == 0)
            def _():
                keep_copy(side, index).wait()

            @pl.when(hops[side] > 0)
            def _():
                final_copy(side, index, out_rows(side, index)).wait_send()

        return carry

    lax.fori_loop(0, count, drain, 0)


def mlp_layer(att, rows, dec_att, dec_rows, gain, w_out, w_gu, w_down):
    head_count = lax.axis_size("head")
    span, width = att.shape
    pieces, _, units, piece = w_gu.shape
    count = span // 2 // CHUNK
    dec = dec_att.shape[0]
    wide = 2 * CHUNK + dec
    any_space = pl.BlockSpec(memory_space=pl.ANY)
    in_vmem = pl.BlockSpec(memory_space=pltpu.VMEM)
    both = pltpu.SemaphoreType.DMA((2, count))
    return pl.pallas_call(
        functools.partial(mlp_kernel, head_count),
        out_shape=(
            jax.ShapeDtypeStruct((span, width), jnp.bfloat16),
            jax.ShapeDtypeStruct((dec, width), jnp.bfloat16),
        ),
        in_specs=[any_space, any_space, in_vmem, in_vmem, in_vmem] + [any_space] * 3,
        out_specs=(any_space, in_vmem),
        scratch_shapes=[
            pltpu.VMEM((2, wide, width), jnp.bfloat16),
            pltpu.VMEM((2, wide, width), jnp.bfloat16),
            pltpu.VMEM(w_out.shape, jnp.bfloat16),
            pltpu.VMEM(w_gu.shape, jnp.bfloat16),
            pltpu.VMEM(w_down.shape, jnp.bfloat16),
            pltpu.VMEM((wide, width), jnp.float32),
            pltpu.VMEM((wide, width), jnp.bfloat16),
            pltpu.VMEM((wide, units), jnp.bfloat16),
            pltpu.VMEM((count, 2 * CHUNK, width), jnp.float32),
            pltpu.VMEM((dec, width), jnp.float32),
            pltpu.VMEM((2, count, CHUNK, width), jnp.bfloat16),
            pltpu.VMEM((head_count, dec, width), jnp.bfloat16),
            pltpu.SemaphoreType.DMA((2, 2, 2)),
            pltpu.SemaphoreType.DMA((3,)),
            both,
            both,
            both,
            both,
            both,
            pltpu.SemaphoreType.DMA((head_count,)),
            pltpu.SemaphoreType.DMA((head_count,)),
        ],
        compiler_params=pltpu.CompilerParams(
            collective_id=3, has_side_effects=True, vmem_limit_bytes=58 * 1024 * 1024
        ),
        cost_estimate=pl.CostEstimate(
            flops=2 * span * width * (width + 3 * units),
            bytes_accessed=2 * (4 * span * width + w_out.size + w_gu.size + w_down.size),
            transcendentals=span * units,
        ),
        name="mlp_layer",
    )(att, rows, dec_att, dec_rows, gain[None], w_out, w_gu, w_down)


def permuted(blocks, order):
    picked = [
        lax.dynamic_slice_in_dim(blocks, order[index], 1, axis=0)
        for index in range(blocks.shape[0])
    ]
    return jnp.concatenate(picked, axis=0)


def inverse_of(order):
    spots = jnp.arange(order.shape[0], dtype=jnp.int32)
    return jnp.sum(jnp.where(order[None, :] == spots[:, None], spots[None, :], 0), axis=1)


def picked_rows(rows, order):
    count = rows.shape[0]
    picker = order[:, None] == jnp.arange(count, dtype=jnp.int32)[None, :]
    return jnp.dot(
        picker.astype(jnp.bfloat16), rows, preferred_element_type=jnp.float32
    ).astype(jnp.bfloat16)


def on_device(
    pre_tokens,
    dec_tokens,
    attn_gain,
    mlp_gain,
    w_qkv,
    w_out,
    w_gate_up,
    w_down,
    pre_cache,
    dec_cache,
    pre_order,
    dec_order,
    pre_offsets,
    dec_lengths,
):
    tok_count = lax.axis_size("tok")
    tok_index = lax.axis_index("tok")
    head_count = lax.axis_size("head")
    span_rows, width = pre_tokens.shape
    piece_len = span_rows // tok_count
    dec_local = dec_tokens.shape[0]
    dec_total = dec_order.shape[0]
    group_width = w_qkv.shape[1]

    rows = permuted(pre_tokens.reshape(tok_count, piece_len, width), pre_order)
    rows = rows.reshape(span_rows, width)
    dec_rows = lax.all_gather(dec_tokens, "tok", axis=0, tiled=True)
    w_qkv_full = whole(w_qkv, 2)
    normed = rms_norm(jnp.concatenate([rows, dec_rows], axis=0), attn_gain)
    projected = fold_rows(normed, w_qkv_full).astype(jnp.bfloat16)
    pre_send = projected[:, :span_rows].reshape(3, tok_count, piece_len, group_width)
    pre_recv = lax.all_to_all(pre_send, "tok", split_axis=1, concat_axis=1, tiled=True)
    pre_recv = pre_recv.reshape(3, span_rows, group_width)
    own_slots = lax.dynamic_slice_in_dim(dec_order, tok_index * dec_local, dec_local)
    dec_part = projected[:, span_rows:].reshape(3, dec_total, group_width)
    dec_mine = jnp.stack([picked_rows(dec_part[which], own_slots) for which in range(3)])
    dec_att = decode_attend(dec_mine, dec_lengths, dec_cache)
    dec_all = lax.all_gather(dec_att, ("tok", "head"), axis=0)
    dec_all = dec_all.reshape(tok_count, head_count, dec_local, group_width)
    dec_all = jnp.transpose(dec_all, (0, 2, 1, 3)).reshape(dec_total, width)
    dec_all = picked_rows(dec_all, inverse_of(dec_order))

    pre_att = prefill_attend(pre_recv, pre_offsets[0], pre_cache)
    pre_back = lax.all_to_all(
        pre_att.reshape(tok_count, piece_len, group_width),
        "tok",
        split_axis=0,
        concat_axis=0,
        tiled=True,
    ).reshape(span_rows, group_width)
    mixed = lax.all_gather(pre_back, "head", axis=1, tiled=True)
    out_full = lax.all_gather(w_out, "head", axis=1, tiled=True)
    out_full = lax.all_gather(out_full, "tok", axis=0, tiled=True)
    gate_up_full = lax.all_gather(w_gate_up, "tok", axis=0)
    down_full = lax.all_gather(w_down, "tok", axis=0, tiled=True)
    pre_out, dec_out = mlp_layer(
        mixed, rows, dec_all, dec_rows, mlp_gain, out_full, gate_up_full, down_full
    )
    pre_out = permuted(pre_out.reshape(tok_count, piece_len, width), inverse_of(pre_order))
    dec_out = lax.dynamic_slice_in_dim(dec_out, tok_index * dec_local, dec_local)
    return (pre_out.reshape(span_rows, width), dec_out)


def solution(mesh):
    placed = (
        P("tok", None),
        P("tok", None),
        P(),
        P(),
        P(None, "head", "tok"),
        P("tok", "head"),
        P(None, "head", "tok"),
        P("tok", "head"),
        P("tok", None, None, "head"),
        P("tok", None, None, "head"),
        P(),
        P(),
        P("tok"),
        P("tok"),
    )
    return jax.shard_map(
        on_device,
        mesh=mesh,
        in_specs=placed,
        out_specs=(P("tok", None), P("tok", None)),
        check_vma=False,
    )
```

```python
import functools

import jax
import jax.numpy as jnp
from jax import lax
from jax.experimental import pallas as pl
from jax.experimental.pallas import tpu as pltpu
from jax.sharding import PartitionSpec as P

HD = 64
Q_ROWS = 512
K_ROWS = 512
DEC_ROWS = 1024
DEC_PAD = 16


rope_base = 130000.0
norm_eps = 1e-05
masked_score = -1e30


def rotate(values, positions):
    width = values.shape[-1]
    half = width // 2
    freqs = rope_base ** (-(jnp.arange(half, dtype=jnp.float32) * 2.0 / width))
    angles = positions.astype(jnp.float32)[:, None] * freqs[None, :]
    cosine = jnp.cos(angles)[:, None, :]
    sine = jnp.sin(angles)[:, None, :]
    first = values[..., :half]
    second = values[..., half:]
    return jnp.concatenate(
        [first * cosine - second * sine, second * cosine + first * sine], axis=-1
    )


def rope_tables(positions, width):
    half = HD // 2
    freqs = rope_base ** (-(jnp.arange(half, dtype=jnp.float32) * 2.0 / HD))
    angles = positions.astype(jnp.float32)[:, None] * freqs[None, :]
    cosine = jnp.cos(angles)
    sine = jnp.sin(angles)
    copies = width // HD
    return (
        jnp.tile(jnp.concatenate([cosine, cosine], axis=1), (1, copies)),
        jnp.tile(jnp.concatenate([-sine, sine], axis=1), (1, copies)),
    )


def swap_halves(values):
    half = HD // 2
    width = values.shape[-1]
    lane = lax.broadcasted_iota(jnp.int32, values.shape, values.ndim - 1)
    axis = values.ndim - 1
    return jnp.where(
        lane % HD < half,
        pltpu.roll(values, width - half, axis),
        pltpu.roll(values, half, axis),
    )


def decode_kernel(limits_ref, q_ref, k_ref, v_ref, cache_ref, out_ref, top_ref, total_ref, mixed_ref):
    request = pl.program_id(0)
    index = pl.program_id(1)
    limit = limits_ref[request]
    heads, width = q_ref.shape[1:]
    block = cache_ref.shape[2]

    @pl.when(index == 0)
    def _():
        own = q_ref[0].astype(jnp.float32) * k_ref[0].astype(jnp.float32)
        top_ref[...] = jnp.sum(own, axis=-1, keepdims=True)
        total_ref[...] = jnp.ones_like(total_ref)
        mixed_ref[...] = jnp.broadcast_to(v_ref[0].astype(jnp.float32), (heads, width))

    @pl.when(index * block < limit)
    def _():
        scores = lax.dot_general(
            q_ref[0],
            cache_ref[0, 0],
            (((1,), (1,)), ((), ())),
            preferred_element_type=jnp.float32,
        )
        spot = index * block + lax.broadcasted_iota(jnp.int32, (1, block), 1)
        scores = jnp.where(spot < limit, scores, masked_score)
        top = top_ref[...]
        new_top = jnp.maximum(top, jnp.max(scores, axis=-1, keepdims=True))
        weights = jnp.exp(scores - new_top)
        factor = jnp.exp(top - new_top)
        top_ref[...] = new_top
        total_ref[...] = total_ref[...] * factor + jnp.sum(weights, axis=-1, keepdims=True)
        mixed_ref[...] = mixed_ref[...] * factor + jnp.dot(
            weights.astype(jnp.bfloat16), cache_ref[0, 1], preferred_element_type=jnp.float32
        )

    @pl.when(index == pl.num_programs(1) - 1)
    def _():
        shape = (heads, width)
        mine = lax.broadcasted_iota(jnp.int32, shape, 1) // HD == lax.broadcasted_iota(
            jnp.int32, shape, 0
        )
        value = jnp.where(mine, mixed_ref[...] / total_ref[...], 0.0)
        out_ref[0] = jnp.sum(value, axis=0, keepdims=True).astype(jnp.bfloat16)


def decode_attend(qkv, lengths, cache):
    _, count, width = qkv.shape
    heads = width // HD
    block = min(DEC_ROWS, cache.shape[2])
    split = qkv.reshape(3, count, heads, HD)
    q_rot = rotate(split[0].astype(jnp.float32), lengths).astype(jnp.bfloat16)
    k_rot = rotate(split[1].astype(jnp.float32), lengths).astype(jnp.bfloat16)
    q_rot = q_rot * jnp.bfloat16(HD**-0.5)
    spread = jnp.where(
        jnp.eye(heads, dtype=jnp.bool_)[None, :, :, None], q_rot[:, None], jnp.bfloat16(0)
    ).reshape(count, heads, width)

    def cache_at(request, index, limits):
        last = (limits[request] - 1) // block
        return (request, 0, jnp.minimum(index, last), 0)

    row = pl.BlockSpec((1, 1, width), lambda request, index, limits: (request, 0, 0))
    return pl.pallas_call(
        decode_kernel,
        out_shape=jax.ShapeDtypeStruct((count, 1, width), jnp.bfloat16),
        grid_spec=pltpu.PrefetchScalarGridSpec(
            num_scalar_prefetch=1,
            grid=(count, cache.shape[2] // block),
            in_specs=[
                pl.BlockSpec((1, heads, width), lambda request, index, limits: (request, 0, 0)),
                row,
                row,
                pl.BlockSpec((1, 2, block, width), cache_at),
            ],
            out_specs=row,
            scratch_shapes=[
                pltpu.VMEM((heads, 1), jnp.float32),
                pltpu.VMEM((heads, 1), jnp.float32),
                pltpu.VMEM((heads, width), jnp.float32),
            ],
        ),
        compiler_params=pltpu.CompilerParams(vmem_limit_bytes=32 * 1024 * 1024),
        cost_estimate=pl.CostEstimate(
            flops=4 * count * heads * cache.shape[2] * width,
            bytes_accessed=4 * count * cache.shape[2] * width,
            transcendentals=count * cache.shape[2] * heads,
        ),
        name="decode_attend",
    )(lengths, spread, k_rot.reshape(count, 1, width), qkv[2].reshape(count, 1, width), cache)[:, 0]


MESH = pl.DeviceIdType.MESH
CHUNK = 64
TILE = 512


def nt_dot(rows, weights):
    return lax.dot_general(
        rows, weights, (((1,), (1,)), ((), ())), preferred_element_type=jnp.float32
    )


def tiles_of(extent):
    tile = min(TILE, extent)
    return tile, extent // tile


class PlaneGather:
    SLOTS = 9

    def __init__(self, source, target, axis, begin, extent, send, recv, local):
        self.source, self.target, self.axis = source, target, axis
        self.begin, self.extent = begin, extent
        self.send, self.recv, self.local = send, recv, local
        self.count = lax.axis_size("tok")
        self.me = lax.axis_index("tok")
        me = self.me
        self.cube = self.count == 8
        if self.cube:
            core = lax.rem(me, 2)
            column = lax.rem(me // 2, 2)
            line = me // 4
            turn = 1 - 2 * core
            self.twin = me + turn
            self.x = me + 2 - 4 * column
            self.y = me + 4 - 8 * line
            far = self.x + self.y - me
            whole_part = (0, 2)
            self.table = [
                (me, whole_part, self.twin, self.twin),
                (me, whole_part, self.x, self.x),
                (me, whole_part, self.y, self.y),
                (self.x, whole_part, self.twin, self.x + turn),
                (self.y, whole_part, self.twin, self.y + turn),
                (self.x, (0, 1), self.y, far),
                (self.y, (1, 1), self.x, far),
                (far, (0, 1), self.twin, far + turn),
                (far, (1, 1), self.twin, far + turn),
            ]
        else:
            self.table = [
                (
                    me,
                    (0, 2),
                    lax.rem(me + offset, self.count),
                    lax.rem(me + self.count - offset, self.count),
                )
                for offset in range(1, self.count)
            ]

    @staticmethod
    def slots():
        count = lax.axis_size("tok")
        return PlaneGather.SLOTS if count == 8 else count - 1

    def place(self, tok, part):
        half = self.extent // 2
        begin, extent = self.begin + part[0] * half, part[1] * half
        rows, columns = self.source.shape
        if self.axis == 0:
            return self.target.at[pl.ds(pl.multiple_of(tok * rows + begin, 16), extent), :]
        return self.target.at[
            pl.ds(begin, extent), pl.ds(pl.multiple_of(tok * columns, columns), columns)
        ]

    def own(self):
        return self.source.at[pl.ds(self.begin, self.extent), :]

    def copy(self, slot):
        what, part, dest, _ = self.table[slot]
        source = self.own() if slot < 3 or not self.cube else self.place(what, part)
        return pltpu.make_async_remote_copy(
            src_ref=source,
            dst_ref=self.place(what, part),
            send_sem=self.send.at[slot],
            recv_sem=self.recv.at[slot],
            device_id={"tok": dest},
            device_id_type=MESH,
        )

    def arrived(self, slot):
        _, part, dest, comes = self.table[slot]
        place = self.place(comes, part)
        pltpu.make_async_remote_copy(
            src_ref=place,
            dst_ref=place,
            send_sem=self.send.at[slot],
            recv_sem=self.recv.at[slot],
            device_id={"tok": dest},
            device_id_type=MESH,
        ).wait_recv()

    def keep(self):
        return pltpu.make_async_copy(self.own(), self.place(self.me, (0, 2)), self.local)

    def start(self):
        first = (1, 2, 0) if self.cube else range(len(self.table))
        for slot in first:
            self.copy(slot).start()
        self.keep().start()

    def relay(self):
        if self.cube:
            self.arrived(1)
            self.copy(5).start()
            self.copy(3).start()
            self.arrived(2)
            self.copy(6).start()
            self.copy(4).start()

    def relay_far(self):
        if self.cube:
            self.arrived(5)
            self.copy(7).start()
            self.arrived(6)
            self.copy(8).start()

    def collect(self):
        for slot in (0, 3, 4, 7, 8) if self.cube else range(len(self.table)):
            self.arrived(slot)
        self.keep().wait()

    def drain(self):
        for slot in range(len(self.table)):
            self.copy(slot).wait_send()


def greet(axes):
    barrier = pltpu.get_barrier_semaphore()
    total = 0
    for axis in axes:
        count = lax.axis_size(axis)
        me = lax.axis_index(axis)
        for offset in range(1, count):
            pl.semaphore_signal(
                barrier,
                inc=1,
                device_id={axis: lax.rem(me + offset, count)},
                device_id_type=MESH,
            )
        total += count - 1
    pl.semaphore_wait(barrier, total)


def project_kernel(
    order_ref,
    x_ref,
    dec_ref,
    gain_ref,
    w_ref,
    out_ref,
    dec_out_ref,
    dec_rows_ref,
    w_v,
    dec_v,
    normed,
    dec_normed,
    staged,
    w_send,
    w_recv,
    w_local,
    send,
    recv,
    local,
    dec_send,
    dec_recv,
    dec_local,
):
    tok_count, piece, width = x_ref.shape
    me = lax.axis_index("tok")
    group = w_ref.shape[0] // 3
    columns = w_ref.shape[1]
    packed = dec_ref.shape[0]
    dec_each = packed * columns // width
    dec_total = tok_count * dec_each
    gathers = [
        PlaneGather(
            w_ref, w_v, 1, kind * group, group, w_send.at[kind], w_recv.at[kind], w_local.at[kind]
        )
        for kind in range(3)
    ]

    def dec_copy(offset):
        return pltpu.make_async_remote_copy(
            src_ref=dec_ref,
            dst_ref=dec_v.at[me],
            send_sem=dec_send.at[offset],
            recv_sem=dec_recv.at[offset],
            device_id={"tok": lax.rem(me + offset, tok_count)},
            device_id_type=MESH,
        )

    dec_keep = pltpu.make_async_copy(dec_ref, dec_v.at[me], dec_local)
    dec_keep.start()
    greet(("tok",))
    for gather in gathers:
        gather.start()
    for offset in range(1, tok_count):
        dec_copy(offset).start()

    def norm(rows):
        squares = jnp.mean(rows * rows, axis=-1, keepdims=True)
        return (rows * lax.rsqrt(squares + norm_eps) * gain_ref[...]).astype(jnp.bfloat16)

    def norm_piece(index, carry):
        rows = x_ref[order_ref[index]].astype(jnp.float32)
        normed[pl.ds(pl.multiple_of(index * piece, piece), piece), :] = norm(rows)
        return carry

    lax.fori_loop(0, tok_count, norm_piece, 0)
    gathers[0].relay()
    dec_keep.wait()
    for offset in range(1, tok_count):
        dec_copy(offset).wait()
    gathers[1].relay()
    gathers[0].relay_far()
    flat = dec_v[...].reshape(tok_count * packed, columns)
    shape = (dec_total, tok_count * packed)
    line = lax.broadcasted_iota(jnp.int32, shape, 0)
    spot = lax.broadcasted_iota(jnp.int32, shape, 1)
    for block in range(width // columns):
        wanted = (line // dec_each) * packed + block * dec_each + line % dec_each
        picker = jnp.where(spot == wanted, 1.0, 0.0).astype(jnp.bfloat16)
        dec_rows_ref[:, block * columns : (block + 1) * columns] = jnp.dot(
            picker, flat, preferred_element_type=jnp.float32
        ).astype(jnp.bfloat16)
    dec_normed[...] = norm(dec_rows_ref[...].astype(jnp.float32))

    rows_each = min(256, tok_count * piece)

    def give(kind, offset):
        dest = lax.rem(me + offset, tok_count)
        return pltpu.make_async_remote_copy(
            src_ref=staged.at[kind, pl.ds(pl.multiple_of(dest * piece, piece), piece), :],
            dst_ref=out_ref.at[kind, pl.ds(pl.multiple_of(me * piece, piece), piece), :],
            send_sem=send.at[kind, offset],
            recv_sem=recv.at[kind, offset],
            device_id={"tok": dest},
            device_id_type=MESH,
        )

    def keep(kind):
        mine = pl.ds(pl.multiple_of(me * piece, piece), piece)
        return pltpu.make_async_copy(
            staged.at[kind, mine, :], out_ref.at[kind, mine, :], local.at[kind]
        )

    for kind in range(3):
        if kind + 2 < 3:
            gathers[kind + 2].relay()
        if kind + 1 < 3:
            gathers[kind + 1].relay_far()
        gathers[kind].collect()
        weights = w_v.at[pl.ds(kind * group, group), :]

        def multiply(index, carry):
            begin = pl.multiple_of(index * rows_each, rows_each)
            staged[kind, pl.ds(begin, rows_each), :] = nt_dot(
                normed[pl.ds(begin, rows_each), :], weights[...]
            ).astype(jnp.bfloat16)
            return carry

        lax.fori_loop(0, tok_count * piece // rows_each, multiply, 0)
        for offset in range(1, tok_count):
            give(kind, offset).start()
        keep(kind).start()
        dec_out_ref[kind] = nt_dot(dec_normed[...], weights[...]).astype(jnp.bfloat16)

    for gather in gathers:
        gather.drain()
    for kind in range(3):
        for offset in range(1, tok_count):
            give(kind, offset).wait()
        keep(kind).wait()


def project_layer(pre_order, rows, dec_packed, gain, w_qkv):
    tok_count, piece, width = rows.shape
    group = w_qkv.shape[0] // 3
    columns = w_qkv.shape[1]
    packed = dec_packed.shape[0]
    dec_total = tok_count * packed * columns // width
    span = tok_count * piece
    any_space = pl.BlockSpec(memory_space=pl.ANY)
    in_vmem = pl.BlockSpec(memory_space=pltpu.VMEM)
    slots = PlaneGather.slots()
    return pl.pallas_call(
        project_kernel,
        out_shape=(
            jax.ShapeDtypeStruct((3, span, group), jnp.bfloat16),
            jax.ShapeDtypeStruct((3, dec_total, group), jnp.bfloat16),
            jax.ShapeDtypeStruct((dec_total, width), jnp.bfloat16),
        ),
        in_specs=[
            pl.BlockSpec(memory_space=pltpu.SMEM),
            in_vmem,
            any_space,
            in_vmem,
            any_space,
        ],
        out_specs=(any_space, in_vmem, in_vmem),
        scratch_shapes=[
            pltpu.VMEM((3 * group, width), jnp.bfloat16),
            pltpu.VMEM((tok_count, packed, columns), jnp.bfloat16),
            pltpu.VMEM((span, width), jnp.bfloat16),
            pltpu.VMEM((dec_total, width), jnp.bfloat16),
            pltpu.VMEM((3, span, group), jnp.bfloat16),
            pltpu.SemaphoreType.DMA((3, slots)),
            pltpu.SemaphoreType.DMA((3, slots)),
            pltpu.SemaphoreType.DMA((3,)),
            pltpu.SemaphoreType.DMA((3, tok_count)),
            pltpu.SemaphoreType.DMA((3, tok_count)),
            pltpu.SemaphoreType.DMA((3,)),
            pltpu.SemaphoreType.DMA((tok_count,)),
            pltpu.SemaphoreType.DMA((tok_count,)),
            pltpu.SemaphoreType.DMA,
        ],
        compiler_params=pltpu.CompilerParams(
            collective_id=1, has_side_effects=True, vmem_limit_bytes=48 * 1024 * 1024
        ),
        cost_estimate=pl.CostEstimate(
            flops=6 * span * width * group,
            bytes_accessed=2 * (span * width + 6 * span * group + 3 * group * width),
            transcendentals=span,
        ),
        name="project_layer",
    )(pre_order, rows, dec_packed, gain[None], w_qkv)


def attend_pair(limit, q_ref, k_ref, v_ref, cos_ref, sin_ref, cache_ref, pair_at, q_rot, k_rot, v_ext, c_ext, out_ref):
    span = q_rot.shape[1]
    length = c_ext.shape[1]
    pair = q_rot.shape[2]
    cosine = cos_ref[...]
    sine = sin_ref[...]
    lane = lax.broadcasted_iota(jnp.int32, (1, pair), 1)
    halves = (lane < HD, lane >= HD)

    key = k_ref[:, pair_at].astype(jnp.float32)
    k_rot[...] = (key * cosine + swap_halves(key) * sine).astype(jnp.bfloat16)
    query = q_ref[:, pair_at].astype(jnp.float32)
    query = (query * cosine + swap_halves(query) * sine).astype(jnp.bfloat16)
    query = query * jnp.bfloat16(HD**-0.5)
    one = jnp.ones((), jnp.bfloat16)
    zero = jnp.zeros((), jnp.bfloat16)
    for side in range(2):
        q_rot[side] = jnp.where(halves[side], query, zero)
        v_ext[side] = jnp.where(halves[side], v_ref[:, pair_at], one)
        c_ext[side] = jnp.where(halves[side], cache_ref[1, :, pair_at], one)

    def fold(state, scores, values):
        top, mixed = state
        new_top = jnp.maximum(top, jnp.max(scores, axis=-1, keepdims=True))
        weights = jnp.exp(scores - new_top).astype(jnp.bfloat16)
        factor = jnp.exp(top - new_top)
        return new_top, mixed * factor + jnp.dot(
            weights, values, preferred_element_type=jnp.float32
        )

    for block in range(span // Q_ROWS):
        start = block * Q_ROWS
        rows = [q_rot[side, start : start + Q_ROWS, :] for side in range(2)]
        keys = k_rot[start : start + Q_ROWS, :]
        shape = (Q_ROWS, Q_ROWS)
        seen = lax.broadcasted_iota(jnp.int32, shape, 1) <= lax.broadcasted_iota(
            jnp.int32, shape, 0
        )
        states = []
        for side in range(2):
            scores = jnp.where(seen, nt_dot(rows[side], keys), masked_score)
            top = jnp.max(scores, axis=-1, keepdims=True)
            weights = jnp.exp(scores - top).astype(jnp.bfloat16)
            mixed = jnp.dot(
                weights,
                v_ext[side, start : start + Q_ROWS, :],
                preferred_element_type=jnp.float32,
            )
            states.append((top, mixed))
        for earlier in range(block):
            begin = earlier * Q_ROWS
            keys = k_rot[begin : begin + Q_ROWS, :]
            for side in range(2):
                states[side] = fold(
                    states[side],
                    nt_dot(rows[side], keys),
                    v_ext[side, begin : begin + Q_ROWS, :],
                )

        def cached(index, state):
            begin = pl.multiple_of(index * K_ROWS, K_ROWS)
            keys_now = cache_ref[0, pl.ds(begin, K_ROWS), pair_at]
            spot = begin + lax.broadcasted_iota(jnp.int32, (1, K_ROWS), 1)
            live = spot < limit
            result = []
            for side in range(2):
                scores = jnp.where(live, nt_dot(rows[side], keys_now), masked_score)
                result.append(
                    fold(state[side], scores, c_ext[side, pl.ds(begin, K_ROWS), :])
                )
            return tuple(result)

        states = lax.fori_loop(0, length // K_ROWS, cached, tuple(states))
        parts = []
        for side in range(2):
            mixed = states[side][1]
            total = pltpu.roll(mixed, HD, 1)
            parts.append(mixed / total)
        out_ref[start : start + Q_ROWS, :] = jnp.where(halves[0], parts[0], parts[1]).astype(
            jnp.bfloat16
        )


GU_CHUNKS = 4
ROW_CHUNKS = 2
AHEAD = 3


def attend_kernel(
    limit_ref,
    qkv_ref,
    cos_ref,
    sin_ref,
    cache_ref,
    dec_ref,
    w_gu_ref,
    w_down_ref,
    w_out_ref,
    dec_all_ref,
    att_ref,
    gu_ref,
    down_ref,
    outw_ref,
    q_rot,
    k_rot,
    v_ext,
    c_ext,
    mixed,
    g_send,
    g_recv,
    g_local,
    b_send,
    b_recv,
    b_local,
    z_send,
    z_recv,
    d_send,
    d_recv,
    d_local,
    e_send,
    e_recv,
):
    tok_count = lax.axis_size("tok")
    head_count = lax.axis_size("head")
    me = lax.axis_index("tok")
    head = lax.axis_index("head")
    last = head_count - 1
    span, group = qkv_ref.shape[1:]
    piece = span // tok_count
    pair = 2 * HD
    pairs = group // pair

    gathers = []
    for source, target, axis, chunks in (
        (w_gu_ref, gu_ref, 1, GU_CHUNKS),
        (w_out_ref, outw_ref, 0, ROW_CHUNKS),
        (w_down_ref, down_ref, 0, ROW_CHUNKS),
    ):
        extent = source.shape[0] // chunks
        for chunk in range(chunks):
            at = len(gathers)
            gathers.append(
                PlaneGather(
                    source, target, axis, chunk * extent, extent, g_send.at[at], g_recv.at[at], g_local.at[at]
                )
            )
    total = len(gathers)

    def pump(index):
        gathers[index].relay()
        if index + AHEAD < total:
            gathers[index + AHEAD].start()
        if index > 0:
            gathers[index - 1].relay_far()

    def spot_of(rows, origin, index):
        begin = pl.multiple_of(origin * group + index * pair, pair)
        return att_ref.at[rows, pl.ds(begin, pair)]

    def back(index, offset):
        dest = lax.rem(me + offset, tok_count)
        return pltpu.make_async_remote_copy(
            src_ref=mixed.at[index, pl.ds(pl.multiple_of(dest * piece, piece), piece), :],
            dst_ref=spot_of(pl.ds(pl.multiple_of(me * piece, piece), piece), head, index),
            send_sem=b_send.at[index, offset],
            recv_sem=b_recv.at[index, offset],
            device_id={"tok": dest},
            device_id_type=MESH,
        )

    def back_keep(index):
        mine = pl.ds(pl.multiple_of(me * piece, piece), piece)
        return pltpu.make_async_copy(
            mixed.at[index, mine, :], spot_of(mine, head, index), b_local.at[index]
        )

    def pass_on(way, origin, index):
        block = spot_of(pl.ds(0, span), origin, index)
        target = jnp.minimum(head + 1, last) if way == 0 else jnp.maximum(head - 1, 0)
        return pltpu.make_async_remote_copy(
            src_ref=block,
            dst_ref=block,
            send_sem=z_send.at[way, origin, index],
            recv_sem=z_recv.at[way, origin, index],
            device_id={"head": target},
            device_id_type=MESH,
        )

    goes = (head < last, head > 0)

    def originate(index):
        for offset in range(1, tok_count):
            back(index, offset).wait_recv()
        back_keep(index).wait()
        for way in range(2):

            @pl.when(goes[way])
            def _():
                pass_on(way, head, index).start()

    def relay(index, hop):
        for way in range(2):
            origin = head - hop if way == 0 else head + hop
            there = origin >= 0 if way == 0 else origin <= last

            @pl.when(there)
            def _():
                pass_on(way, origin, index).wait_recv()

                @pl.when(goes[way])
                def _():
                    pass_on(way, origin, index).start()

    dec_pad = dec_ref.shape[0]
    dec_columns = pl.ds(pl.multiple_of(head * group, group), group)
    dec_mine = dec_all_ref.at[pl.ds(pl.multiple_of(me * dec_pad, dec_pad), dec_pad), dec_columns]
    dec_keep = pltpu.make_async_copy(dec_ref, dec_mine, d_local)

    def dec_copy(offset):
        return pltpu.make_async_remote_copy(
            src_ref=dec_ref,
            dst_ref=dec_mine,
            send_sem=d_send.at[offset],
            recv_sem=d_recv.at[offset],
            device_id={"tok": lax.rem(me + offset, tok_count)},
            device_id_type=MESH,
        )

    def dec_spread(offset):
        return pltpu.make_async_remote_copy(
            src_ref=dec_all_ref.at[:, dec_columns],
            dst_ref=dec_all_ref.at[:, dec_columns],
            send_sem=e_send.at[offset],
            recv_sem=e_recv.at[offset],
            device_id={"head": lax.rem(head + offset, head_count)},
            device_id_type=MESH,
        )

    greet(("tok", "head"))
    dec_keep.start()
    for offset in range(1, tok_count):
        dec_copy(offset).start()
    for gather in gathers[:AHEAD]:
        gather.start()

    limit = limit_ref[0]
    every = max(1, pairs // 2)

    def one_pair(index, carry):
        pair_at = pl.ds(pl.multiple_of(index * pair, pair), pair)
        attend_pair(
            limit,
            qkv_ref.at[0],
            qkv_ref.at[1],
            qkv_ref.at[2],
            cos_ref,
            sin_ref,
            cache_ref.at[0],
            pair_at,
            q_rot,
            k_rot,
            v_ext,
            c_ext,
            mixed.at[index],
        )
        for offset in range(1, tok_count):
            back(index, offset).start()
        back_keep(index).start()

        @pl.when(index > 0)
        def _():
            originate(index - 1)

        for turn in range(2):

            @pl.when(index == (turn + 1) * every - 1)
            def _():
                pump(turn)

        return carry

    lax.fori_loop(0, pairs, one_pair, 0)
    originate(pairs - 1)
    dec_keep.wait()
    for offset in range(1, tok_count):
        dec_copy(offset).wait()
    for offset in range(1, head_count):
        dec_spread(offset).start()

    def relay_all(hop):
        def body(index, carry):
            relay(index, hop)
            return carry

        lax.fori_loop(0, pairs, body, 0)

    hop = 1
    for index in range(2, total):
        pump(index)
        if hop <= last:
            relay_all(hop)
            hop += 1
    while hop <= last:
        relay_all(hop)
        hop += 1
    gathers[total - 1].relay_far()
    for offset in range(1, head_count):
        dec_spread(offset).wait()
    for gather in gathers:
        gather.collect()
    for gather in gathers:
        gather.drain()

    def drain(index, carry):
        for offset in range(1, tok_count):
            back(index, offset).wait_send()
        for origin in range(head_count):
            for way in range(2):
                passed = origin <= head if way == 0 else origin >= head

                @pl.when(jnp.logical_and(passed, goes[way]))
                def _():
                    pass_on(way, origin, index).wait_send()

        return carry

    lax.fori_loop(0, pairs, drain, 0)


def attend_layer(qkv, offset, cache, dec_att, w_gu, w_down, w_out):
    tok_count = lax.axis_size("tok")
    head_count = lax.axis_size("head")
    _, span, group = qkv.shape
    length = cache.shape[2]
    pair = 2 * HD
    pairs = group // pair
    cosine, sine = rope_tables(offset + jnp.arange(span, dtype=jnp.int32), pair)
    any_space = pl.BlockSpec(memory_space=pl.ANY)
    in_vmem = pl.BlockSpec(memory_space=pltpu.VMEM)
    slots = PlaneGather.slots()
    total = GU_CHUNKS + 2 * ROW_CHUNKS
    gather_sems = pltpu.SemaphoreType.DMA((total, slots))
    back_sems = pltpu.SemaphoreType.DMA((pairs, tok_count))
    pass_sems = pltpu.SemaphoreType.DMA((2, head_count, pairs))
    return pl.pallas_call(
        attend_kernel,
        out_shape=(
            jax.ShapeDtypeStruct((tok_count * dec_att.shape[0], head_count * group), jnp.bfloat16),
            jax.ShapeDtypeStruct((span, head_count * group), jnp.bfloat16),
            jax.ShapeDtypeStruct((w_gu.shape[0], tok_count * w_gu.shape[1]), jnp.bfloat16),
            jax.ShapeDtypeStruct((tok_count * w_down.shape[0], w_down.shape[1]), jnp.bfloat16),
            jax.ShapeDtypeStruct((tok_count * w_out.shape[0], w_out.shape[1]), jnp.bfloat16),
        ),
        in_specs=[pl.BlockSpec(memory_space=pltpu.SMEM)] + [in_vmem] * 5 + [any_space] * 3,
        out_specs=(in_vmem,) + (any_space,) * 4,
        scratch_shapes=[
            pltpu.VMEM((2, span, pair), jnp.bfloat16),
            pltpu.VMEM((span, pair), jnp.bfloat16),
            pltpu.VMEM((2, span, pair), jnp.bfloat16),
            pltpu.VMEM((2, length, pair), jnp.bfloat16),
            pltpu.VMEM((pairs, span, pair), jnp.bfloat16),
            gather_sems,
            gather_sems,
            pltpu.SemaphoreType.DMA((total,)),
            back_sems,
            back_sems,
            pltpu.SemaphoreType.DMA((pairs,)),
            pass_sems,
            pass_sems,
            pltpu.SemaphoreType.DMA((tok_count,)),
            pltpu.SemaphoreType.DMA((tok_count,)),
            pltpu.SemaphoreType.DMA,
            pltpu.SemaphoreType.DMA((head_count,)),
            pltpu.SemaphoreType.DMA((head_count,)),
        ],
        compiler_params=pltpu.CompilerParams(
            collective_id=2, has_side_effects=True, vmem_limit_bytes=56 * 1024 * 1024
        ),
        cost_estimate=pl.CostEstimate(
            flops=16 * span * 3 * span * group,
            bytes_accessed=4 * length * group + 8 * span * group,
            transcendentals=span * 3 * span * group // HD,
        ),
        name="attend_layer",
    )(offset[None], qkv, cosine, sine, cache, dec_att, w_gu, w_down, w_out)


def copy_block(order_ref, source_ref, target_ref):
    target_ref[...] = source_ref[...]


def unpermuted(blocks, order):
    count, piece, width = blocks.shape
    return pl.pallas_call(
        copy_block,
        out_shape=jax.ShapeDtypeStruct(blocks.shape, blocks.dtype),
        grid_spec=pltpu.PrefetchScalarGridSpec(
            num_scalar_prefetch=1,
            grid=(count,),
            in_specs=[pl.BlockSpec((1, piece, width), lambda index, order: (index, 0, 0))],
            out_specs=pl.BlockSpec((1, piece, width), lambda index, order: (order[index], 0, 0)),
        ),
        name="unpermute",
    )(order, blocks)


def mlp_kernel(
    head_count,
    order_ref,
    att_ref,
    rows_ref,
    dec_att_ref,
    dec_rows_ref,
    gain_ref,
    w_out_ref,
    w_gu_ref,
    w_down_ref,
    out_ref,
    dec_out_ref,
    x_v,
    r_v,
    w_out_v,
    w_gu_v,
    w_down_v,
    resid,
    mlp_in,
    hidden,
    partial,
    dec_resid,
    slots,
    dec_slots,
    in_sem,
    load_sem,
    rs_send,
    rs_recv,
    ag_send,
    ag_recv,
    keep_sem,
    dec_send,
    dec_recv,
):
    last = head_count - 1
    me = lax.axis_index("head")
    span, width = att_ref.shape
    half = span // 2
    count = half // CHUNK
    wide = 2 * CHUNK
    units = w_gu_ref.shape[0] // 2
    piece = rows_ref.shape[1]
    dec = dec_att_ref.shape[0]

    loads = [
        pltpu.make_async_copy(w_out_ref, w_out_v, load_sem.at[0]),
        pltpu.make_async_copy(w_gu_ref, w_gu_v, load_sem.at[1]),
        pltpu.make_async_copy(w_down_ref, w_down_v, load_sem.at[2]),
    ]

    def inputs(step, slot):
        copies = []
        for side in range(2):
            begin = pl.multiple_of(side * half + step * CHUNK, CHUNK)
            copies.append(
                pltpu.make_async_copy(
                    att_ref.at[pl.ds(begin, CHUNK)],
                    x_v.at[slot, pl.ds(side * CHUNK, CHUNK)],
                    in_sem.at[slot, side],
                )
            )
        return copies

    for copy in inputs(0, 0):
        copy.start()
    for copy in loads:
        copy.start()
    for slot in range(2):
        x_v[slot, wide:, :] = dec_att_ref[...]
    r_v[wide:, :] = dec_rows_ref[...]

    greet(("head",))

    spot = lax.broadcasted_iota(jnp.int32, (wide, 1), 0)
    owner = jnp.where(spot < CHUNK, 0, last)
    owned = jnp.where(owner == me, 1.0, 0.0).astype(jnp.float32)

    def compute(step):
        slot = lax.rem(step, 2)

        @pl.when(step + 1 < count)
        def _():
            for copy in inputs(step + 1, lax.rem(step + 1, 2)):
                copy.start()

        for side in range(2):
            begin = side * half + step * CHUNK
            inner = pl.multiple_of(lax.rem(begin, piece), CHUNK)
            r_v[side * CHUNK : (side + 1) * CHUNK, :] = rows_ref[
                order_ref[begin // piece], pl.ds(inner, CHUNK), :
            ]
        for copy in inputs(step, slot):
            copy.wait()

        @pl.when(step == 0)
        def _():
            loads[0].wait()

        out_tile, out_tiles = tiles_of(width)

        def project(index, squares):
            begin = pl.multiple_of(index * out_tile, out_tile)
            value = nt_dot(x_v[slot], w_out_v[pl.ds(begin, out_tile), :])
            value = value + r_v[:, pl.ds(begin, out_tile)].astype(jnp.float32)
            resid[:, pl.ds(begin, out_tile)] = value
            return squares + jnp.sum(value * value, axis=-1, keepdims=True)

        squares = lax.fori_loop(
            0, out_tiles, project, jnp.zeros((wide + dec, 1), jnp.float32)
        )
        factor = lax.rsqrt(squares / width + norm_eps)
        mlp_in[...] = (resid[...] * factor * gain_ref[...]).astype(jnp.bfloat16)

        @pl.when(step == 0)
        def _():
            loads[1].wait()

        unit_tile, unit_tiles = tiles_of(units)

        def gate_up(index, carry):
            begin = pl.multiple_of(index * unit_tile, unit_tile)
            gate = nt_dot(mlp_in[...], w_gu_v[pl.ds(begin, unit_tile), :])
            up = nt_dot(mlp_in[...], w_gu_v[pl.ds(units + begin, unit_tile), :])
            hidden[:, pl.ds(begin, unit_tile)] = (
                gate / (1.0 + jnp.exp(-gate)) * up
            ).astype(jnp.bfloat16)
            return carry

        lax.fori_loop(0, unit_tiles, gate_up, 0)

        @pl.when(step == 0)
        def _():
            loads[2].wait()

        def down(index, carry):
            begin = pl.multiple_of(index * out_tile, out_tile)
            value = nt_dot(hidden[...], w_down_v[pl.ds(begin, out_tile), :])
            columns = pl.ds(begin, out_tile)
            partial[step, :, columns] = value[:wide] + resid[:wide, columns] * owned

            @pl.when(step == 0)
            def _():
                dec_slots[me, :, columns] = value[wide:].astype(jnp.bfloat16)

            return carry

        lax.fori_loop(0, out_tiles, down, 0)

        @pl.when(step == 0)
        def _():
            dec_resid[...] = resid[wide:, :]
            for offset in range(1, head_count):
                dec_copy(offset).start()

    def dec_copy(offset):
        return pltpu.make_async_remote_copy(
            src_ref=dec_slots.at[me],
            dst_ref=dec_slots.at[me],
            send_sem=dec_send.at[offset],
            recv_sem=dec_recv.at[offset],
            device_id={"head": lax.rem(me + offset, head_count)},
            device_id_type=MESH,
        )

    def out_rows(side, index):
        return out_ref.at[pl.ds(pl.multiple_of(side * half + index * CHUNK, CHUNK), CHUNK)]

    def next_of(side):
        return jnp.maximum(me - 1, 0) if side == 0 else jnp.minimum(me + 1, last)

    def before_of(side):
        return next_of(1 - side)

    def sum_copy(side, index):
        return pltpu.make_async_remote_copy(
            src_ref=slots.at[side, index],
            dst_ref=slots.at[side, index],
            send_sem=rs_send.at[side, index],
            recv_sem=rs_recv.at[side, index],
            device_id={"head": next_of(side)},
            device_id_type=MESH,
        )

    def final_copy(side, index, source):
        return pltpu.make_async_remote_copy(
            src_ref=source,
            dst_ref=out_rows(side, index),
            send_sem=ag_send.at[side, index],
            recv_sem=ag_recv.at[side, index],
            device_id={"head": before_of(side)},
            device_id_type=MESH,
        )

    def keep_copy(side, index):
        return pltpu.make_async_copy(
            slots.at[side, index], out_rows(side, index), keep_sem.at[side, index]
        )

    hops = [last - me, me]
    to_end = [me, last - me]

    def combine(side, index):
        mine = partial.at[index, pl.ds(side * CHUNK, CHUNK)]

        @pl.when(hops[side] == 0)
        def _():
            slots[side, index] = mine[...].astype(jnp.bfloat16)

        @pl.when(hops[side] > 0)
        def _():
            sum_copy(side, index).wait_recv()
            slots[side, index] = (
                mine[...] + slots[side, index].astype(jnp.float32)
            ).astype(jnp.bfloat16)

        @pl.when(to_end[side] > 0)
        def _():
            sum_copy(side, index).start()

        @pl.when(to_end[side] == 0)
        def _():
            final_copy(side, index, slots.at[side, index]).start()
            keep_copy(side, index).start()

    def forward(side, index):
        final_copy(side, index, out_rows(side, index)).wait_recv()

        @pl.when(hops[side] > 0)
        def _():
            final_copy(side, index, out_rows(side, index)).start()

    def tick(step, carry):
        @pl.when(step < count)
        def _():
            compute(step)

        for side in range(2):
            index = step - hops[side]

            @pl.when(jnp.logical_and(index >= 0, index < count))
            def _():
                combine(side, index)

        for side in range(2):
            spread = step - last - to_end[side]

            @pl.when(
                jnp.logical_and(
                    to_end[side] > 0, jnp.logical_and(spread >= 0, spread < count)
                )
            )
            def _():
                forward(side, spread)

        return carry

    lax.fori_loop(0, count + 2 * last, tick, 0)

    for offset in range(1, head_count):
        dec_copy(offset).wait()
    total = dec_resid[...]
    for index in range(head_count):
        total = total + dec_slots[index].astype(jnp.float32)
    dec_out_ref[...] = total.astype(jnp.bfloat16)

    def drain(index, carry):
        for side in range(2):

            @pl.when(to_end[side] > 0)
            def _():
                sum_copy(side, index).wait_send()

            @pl.when(to_end[side] == 0)
            def _():
                keep_copy(side, index).wait()

            @pl.when(hops[side] > 0)
            def _():
                final_copy(side, index, out_rows(side, index)).wait_send()

        return carry

    lax.fori_loop(0, count, drain, 0)


def mlp_layer(pre_order, att, rows, dec_att, dec_rows, gain, w_out, w_gu, w_down):
    head_count = lax.axis_size("head")
    span, width = att.shape
    units = w_gu.shape[0] // 2
    count = span // 2 // CHUNK
    dec = dec_att.shape[0]
    wide = 2 * CHUNK + dec
    any_space = pl.BlockSpec(memory_space=pl.ANY)
    in_vmem = pl.BlockSpec(memory_space=pltpu.VMEM)
    both = pltpu.SemaphoreType.DMA((2, count))
    return pl.pallas_call(
        functools.partial(mlp_kernel, head_count),
        out_shape=(
            jax.ShapeDtypeStruct((span, width), jnp.bfloat16),
            jax.ShapeDtypeStruct((dec, width), jnp.bfloat16),
        ),
        in_specs=[pl.BlockSpec(memory_space=pltpu.SMEM), any_space]
        + [in_vmem] * 4
        + [any_space] * 3,
        out_specs=(any_space, in_vmem),
        scratch_shapes=[
            pltpu.VMEM((2, wide, width), jnp.bfloat16),
            pltpu.VMEM((wide, width), jnp.bfloat16),
            pltpu.VMEM(w_out.shape, jnp.bfloat16),
            pltpu.VMEM(w_gu.shape, jnp.bfloat16),
            pltpu.VMEM(w_down.shape, jnp.bfloat16),
            pltpu.VMEM((wide, width), jnp.float32),
            pltpu.VMEM((wide, width), jnp.bfloat16),
            pltpu.VMEM((wide, units), jnp.bfloat16),
            pltpu.VMEM((count, 2 * CHUNK, width), jnp.float32),
            pltpu.VMEM((dec, width), jnp.float32),
            pltpu.VMEM((2, count, CHUNK, width), jnp.bfloat16),
            pltpu.VMEM((head_count, dec, width), jnp.bfloat16),
            pltpu.SemaphoreType.DMA((2, 2)),
            pltpu.SemaphoreType.DMA((3,)),
            both,
            both,
            both,
            both,
            both,
            pltpu.SemaphoreType.DMA((head_count,)),
            pltpu.SemaphoreType.DMA((head_count,)),
        ],
        compiler_params=pltpu.CompilerParams(
            collective_id=3, has_side_effects=True, vmem_limit_bytes=58 * 1024 * 1024
        ),
        cost_estimate=pl.CostEstimate(
            flops=2 * span * width * (width + 3 * units),
            bytes_accessed=2 * (4 * span * width + w_out.size + w_gu.size + w_down.size),
            transcendentals=span * units,
        ),
        name="mlp_layer",
    )(pre_order, att, rows, dec_att, dec_rows, gain[None], w_out, w_gu, w_down)


def picked_rows(rows, order):
    count = rows.shape[0]
    picker = order[:, None] == jnp.arange(count, dtype=jnp.int32)[None, :]
    return jnp.dot(
        picker.astype(jnp.bfloat16), rows, preferred_element_type=jnp.float32
    ).astype(jnp.bfloat16)


def inverse_of(order):
    spots = jnp.arange(order.shape[0], dtype=jnp.int32)
    return jnp.sum(jnp.where(order[None, :] == spots[:, None], spots[None, :], 0), axis=1)


def on_device(
    pre_tokens,
    dec_tokens,
    attn_gain,
    mlp_gain,
    w_qkv,
    w_out,
    w_gate_up,
    w_down,
    pre_cache,
    dec_cache,
    pre_order,
    dec_order,
    pre_offsets,
    dec_lengths,
):
    tok_count = lax.axis_size("tok")
    tok_index = lax.axis_index("tok")
    head_count = lax.axis_size("head")
    span_rows, width = pre_tokens.shape
    piece_len = span_rows // tok_count
    dec_local = dec_tokens.shape[0]
    group_width, depth = w_qkv.shape[1:]
    units = w_gate_up.shape[1]

    blocks = pre_tokens.reshape(tok_count, piece_len, width)
    packed = dec_tokens.reshape(dec_local, width // depth, depth)
    packed = jnp.transpose(packed, (1, 0, 2)).reshape(dec_local * width // depth, depth)
    qkv, dec_qkv, dec_rows = project_layer(
        pre_order, blocks, packed, attn_gain, w_qkv.reshape(3 * group_width, depth)
    )
    w_out_rows = lax.all_gather(w_out, "head", axis=1, tiled=True)

    own_slots = lax.dynamic_slice_in_dim(dec_order, tok_index * dec_local, dec_local)
    dec_mine = jnp.stack([picked_rows(dec_qkv[which], own_slots) for which in range(3)])
    dec_att = decode_attend(dec_mine, dec_lengths, dec_cache)
    dec_att = jnp.pad(dec_att, ((0, DEC_PAD - dec_local), (0, 0)))

    dec_all, attended, gate_up_full, down_full, out_full = attend_layer(
        qkv,
        pre_offsets[0],
        pre_cache,
        dec_att,
        w_gate_up.reshape(2 * units, depth),
        w_down,
        w_out_rows,
    )
    dec_spots = inverse_of(dec_order)
    dec_spots = dec_spots // dec_local * DEC_PAD + dec_spots % dec_local
    dec_all = picked_rows(dec_all, dec_spots)
    pre_out, dec_out = mlp_layer(
        pre_order,
        attended,
        blocks,
        dec_all,
        dec_rows,
        mlp_gain,
        out_full,
        gate_up_full,
        down_full,
    )
    pre_out = unpermuted(pre_out.reshape(tok_count, piece_len, width), pre_order)
    dec_out = lax.dynamic_slice_in_dim(dec_out, tok_index * dec_local, dec_local)
    return (pre_out.reshape(span_rows, width), dec_out)


def solution(mesh):
    placed = (
        P("tok", None),
        P("tok", None),
        P(),
        P(),
        P(None, "head", "tok"),
        P("tok", "head"),
        P(None, "head", "tok"),
        P("tok", "head"),
        P("tok", None, None, "head"),
        P("tok", None, None, "head"),
        P(),
        P(),
        P("tok"),
        P("tok"),
    )
    return jax.shard_map(
        on_device,
        mesh=mesh,
        in_specs=placed,
        out_specs=(P("tok", None), P("tok", None)),
        check_vma=False,
    )
```

```python
import functools

import jax
import jax.numpy as jnp
from jax import lax
from jax.experimental import pallas as pl
from jax.experimental.pallas import tpu as pltpu
from jax.sharding import PartitionSpec as P

HD = 64
Q_ROWS = 512
K_ROWS = 512
DEC_ROWS = 1024
DEC_PAD = 16


rope_base = 130000.0
norm_eps = 1e-05
masked_score = -1e30


def rotate(values, positions):
    width = values.shape[-1]
    half = width // 2
    freqs = rope_base ** (-(jnp.arange(half, dtype=jnp.float32) * 2.0 / width))
    angles = positions.astype(jnp.float32)[:, None] * freqs[None, :]
    cosine = jnp.cos(angles)[:, None, :]
    sine = jnp.sin(angles)[:, None, :]
    first = values[..., :half]
    second = values[..., half:]
    return jnp.concatenate(
        [first * cosine - second * sine, second * cosine + first * sine], axis=-1
    )


def rope_tables(positions, width):
    half = HD // 2
    freqs = rope_base ** (-(jnp.arange(half, dtype=jnp.float32) * 2.0 / HD))
    angles = positions.astype(jnp.float32)[:, None] * freqs[None, :]
    cosine = jnp.cos(angles)
    sine = jnp.sin(angles)
    copies = width // HD
    return (
        jnp.tile(jnp.concatenate([cosine, cosine], axis=1), (1, copies)),
        jnp.tile(jnp.concatenate([-sine, sine], axis=1), (1, copies)),
    )


def swap_halves(values):
    half = HD // 2
    width = values.shape[-1]
    lane = lax.broadcasted_iota(jnp.int32, values.shape, values.ndim - 1)
    axis = values.ndim - 1
    return jnp.where(
        lane % HD < half,
        pltpu.roll(values, width - half, axis),
        pltpu.roll(values, half, axis),
    )


def decode_kernel(limits_ref, q_ref, k_ref, v_ref, cache_ref, out_ref, top_ref, total_ref, mixed_ref):
    request = pl.program_id(0)
    index = pl.program_id(1)
    limit = limits_ref[request]
    heads, width = q_ref.shape[1:]
    block = cache_ref.shape[2]

    @pl.when(index == 0)
    def _():
        own = q_ref[0].astype(jnp.float32) * k_ref[0].astype(jnp.float32)
        top_ref[...] = jnp.sum(own, axis=-1, keepdims=True)
        total_ref[...] = jnp.ones_like(total_ref)
        mixed_ref[...] = jnp.broadcast_to(v_ref[0].astype(jnp.float32), (heads, width))

    @pl.when(index * block < limit)
    def _():
        scores = lax.dot_general(
            q_ref[0],
            cache_ref[0, 0],
            (((1,), (1,)), ((), ())),
            preferred_element_type=jnp.float32,
        )
        spot = index * block + lax.broadcasted_iota(jnp.int32, (1, block), 1)
        scores = jnp.where(spot < limit, scores, masked_score)
        top = top_ref[...]
        new_top = jnp.maximum(top, jnp.max(scores, axis=-1, keepdims=True))
        weights = jnp.exp(scores - new_top)
        factor = jnp.exp(top - new_top)
        top_ref[...] = new_top
        total_ref[...] = total_ref[...] * factor + jnp.sum(weights, axis=-1, keepdims=True)
        mixed_ref[...] = mixed_ref[...] * factor + jnp.dot(
            weights.astype(jnp.bfloat16), cache_ref[0, 1], preferred_element_type=jnp.float32
        )

    @pl.when(index == pl.num_programs(1) - 1)
    def _():
        shape = (heads, width)
        mine = lax.broadcasted_iota(jnp.int32, shape, 1) // HD == lax.broadcasted_iota(
            jnp.int32, shape, 0
        )
        value = jnp.where(mine, mixed_ref[...] / total_ref[...], 0.0)
        out_ref[0] = jnp.sum(value, axis=0, keepdims=True).astype(jnp.bfloat16)


def decode_attend(qkv, lengths, cache):
    _, count, width = qkv.shape
    heads = width // HD
    block = min(DEC_ROWS, cache.shape[2])
    split = qkv.reshape(3, count, heads, HD)
    q_rot = rotate(split[0].astype(jnp.float32), lengths).astype(jnp.bfloat16)
    k_rot = rotate(split[1].astype(jnp.float32), lengths).astype(jnp.bfloat16)
    q_rot = q_rot * jnp.bfloat16(HD**-0.5)
    spread = jnp.where(
        jnp.eye(heads, dtype=jnp.bool_)[None, :, :, None], q_rot[:, None], jnp.bfloat16(0)
    ).reshape(count, heads, width)

    def cache_at(request, index, limits):
        last = (limits[request] - 1) // block
        return (request, 0, jnp.minimum(index, last), 0)

    row = pl.BlockSpec((1, 1, width), lambda request, index, limits: (request, 0, 0))
    return pl.pallas_call(
        decode_kernel,
        out_shape=jax.ShapeDtypeStruct((count, 1, width), jnp.bfloat16),
        grid_spec=pltpu.PrefetchScalarGridSpec(
            num_scalar_prefetch=1,
            grid=(count, cache.shape[2] // block),
            in_specs=[
                pl.BlockSpec((1, heads, width), lambda request, index, limits: (request, 0, 0)),
                row,
                row,
                pl.BlockSpec((1, 2, block, width), cache_at),
            ],
            out_specs=row,
            scratch_shapes=[
                pltpu.VMEM((heads, 1), jnp.float32),
                pltpu.VMEM((heads, 1), jnp.float32),
                pltpu.VMEM((heads, width), jnp.float32),
            ],
        ),
        compiler_params=pltpu.CompilerParams(vmem_limit_bytes=56 * 1024 * 1024),
        cost_estimate=pl.CostEstimate(
            flops=4 * count * heads * cache.shape[2] * width,
            bytes_accessed=4 * count * cache.shape[2] * width,
            transcendentals=count * cache.shape[2] * heads,
        ),
        name="decode_attend",
    )(lengths, spread, k_rot.reshape(count, 1, width), qkv[2].reshape(count, 1, width), cache)[:, 0]


MESH = pl.DeviceIdType.MESH
CHUNK = 32
GROUP_ROWS = 128
TILE = 512


def nt_dot(rows, weights):
    return lax.dot_general(
        rows, weights, (((1,), (1,)), ((), ())), preferred_element_type=jnp.float32
    )


def tiles_of(extent):
    tile = min(TILE, extent)
    return tile, extent // tile


class PlaneGather:
    SLOTS = 9

    def __init__(self, source, target, axis, begin, extent, send, recv, local):
        self.source, self.target, self.axis = source, target, axis
        self.begin, self.extent = begin, extent
        self.send, self.recv, self.local = send, recv, local
        self.count = lax.axis_size("tok")
        self.me = lax.axis_index("tok")
        me = self.me
        self.cube = self.count == 8
        if self.cube:
            core = lax.rem(me, 2)
            column = lax.rem(me // 2, 2)
            line = me // 4
            turn = 1 - 2 * core
            self.twin = me + turn
            self.x = me + 2 - 4 * column
            self.y = me + 4 - 8 * line
            far = self.x + self.y - me
            whole_part = (0, 2)
            self.table = [
                (me, whole_part, self.twin, self.twin),
                (me, whole_part, self.x, self.x),
                (me, whole_part, self.y, self.y),
                (self.x, whole_part, self.twin, self.x + turn),
                (self.y, whole_part, self.twin, self.y + turn),
                (self.x, (0, 1), self.y, far),
                (self.y, (1, 1), self.x, far),
                (far, (0, 1), self.twin, far + turn),
                (far, (1, 1), self.twin, far + turn),
            ]
        else:
            self.table = [
                (
                    me,
                    (0, 2),
                    lax.rem(me + offset, self.count),
                    lax.rem(me + self.count - offset, self.count),
                )
                for offset in range(1, self.count)
            ]

    @staticmethod
    def slots():
        count = lax.axis_size("tok")
        return PlaneGather.SLOTS if count == 8 else count - 1

    def place(self, tok, part):
        half = self.extent // 2
        begin, extent = self.begin + part[0] * half, part[1] * half
        rows, columns = self.source.shape
        if self.axis == 0:
            return self.target.at[pl.ds(pl.multiple_of(tok * rows + begin, 16), extent), :]
        return self.target.at[
            pl.ds(begin, extent), pl.ds(pl.multiple_of(tok * columns, columns), columns)
        ]

    def own(self):
        return self.source.at[pl.ds(self.begin, self.extent), :]

    def copy(self, slot):
        what, part, dest, _ = self.table[slot]
        source = self.own() if slot < 3 or not self.cube else self.place(what, part)
        return pltpu.make_async_remote_copy(
            src_ref=source,
            dst_ref=self.place(what, part),
            send_sem=self.send.at[slot],
            recv_sem=self.recv.at[slot],
            device_id={"tok": dest},
            device_id_type=MESH,
        )

    def arrived(self, slot):
        _, part, dest, comes = self.table[slot]
        place = self.place(comes, part)
        pltpu.make_async_remote_copy(
            src_ref=place,
            dst_ref=place,
            send_sem=self.send.at[slot],
            recv_sem=self.recv.at[slot],
            device_id={"tok": dest},
            device_id_type=MESH,
        ).wait_recv()

    def keep(self):
        return pltpu.make_async_copy(self.own(), self.place(self.me, (0, 2)), self.local)

    def start(self):
        first = (1, 2, 0) if self.cube else range(len(self.table))
        for slot in first:
            self.copy(slot).start()
        self.keep().start()

    def relay(self):
        if self.cube:
            self.arrived(1)
            self.copy(5).start()
            self.copy(3).start()
            self.arrived(2)
            self.copy(6).start()
            self.copy(4).start()

    def relay_far(self):
        if self.cube:
            self.arrived(5)
            self.copy(7).start()
            self.arrived(6)
            self.copy(8).start()

    def collect(self):
        for slot in (0, 3, 4, 7, 8) if self.cube else range(len(self.table)):
            self.arrived(slot)
        self.keep().wait()

    def drain(self):
        for slot in range(len(self.table)):
            self.copy(slot).wait_send()


def greet(axes):
    barrier = pltpu.get_barrier_semaphore()
    total = 0
    for axis in axes:
        count = lax.axis_size(axis)
        me = lax.axis_index(axis)
        for offset in range(1, count):
            pl.semaphore_signal(
                barrier,
                inc=1,
                device_id={axis: lax.rem(me + offset, count)},
                device_id_type=MESH,
            )
        total += count - 1
    pl.semaphore_wait(barrier, total)


def project_kernel(
    order_ref,
    x_ref,
    dec_ref,
    gain_ref,
    w_ref,
    out_ref,
    dec_out_ref,
    dec_rows_ref,
    w_v,
    dec_v,
    normed,
    dec_normed,
    staged,
    w_send,
    w_recv,
    w_local,
    send,
    recv,
    local,
    dec_send,
    dec_recv,
    dec_local,
):
    tok_count, piece, width = x_ref.shape
    me = lax.axis_index("tok")
    group = w_ref.shape[0] // 3
    columns = w_ref.shape[1]
    packed = dec_ref.shape[0]
    dec_each = packed * columns // width
    dec_total = tok_count * dec_each
    gathers = [
        PlaneGather(
            w_ref, w_v, 1, kind * group, group, w_send.at[kind], w_recv.at[kind], w_local.at[kind]
        )
        for kind in range(3)
    ]

    def dec_copy(offset):
        return pltpu.make_async_remote_copy(
            src_ref=dec_ref,
            dst_ref=dec_v.at[me],
            send_sem=dec_send.at[offset],
            recv_sem=dec_recv.at[offset],
            device_id={"tok": lax.rem(me + offset, tok_count)},
            device_id_type=MESH,
        )

    dec_keep = pltpu.make_async_copy(dec_ref, dec_v.at[me], dec_local)
    dec_keep.start()
    greet(("tok",))
    for gather in gathers:
        gather.start()
    for offset in range(1, tok_count):
        dec_copy(offset).start()

    def norm(rows):
        squares = jnp.mean(rows * rows, axis=-1, keepdims=True)
        return (rows * lax.rsqrt(squares + norm_eps) * gain_ref[...]).astype(jnp.bfloat16)

    def norm_piece(index, carry):
        rows = x_ref[order_ref[index]].astype(jnp.float32)
        normed[pl.ds(pl.multiple_of(index * piece, piece), piece), :] = norm(rows)
        return carry

    lax.fori_loop(0, tok_count, norm_piece, 0)
    gathers[0].relay()
    dec_keep.wait()
    for offset in range(1, tok_count):
        dec_copy(offset).wait()
    gathers[1].relay()
    gathers[0].relay_far()
    flat = dec_v[...].reshape(tok_count * packed, columns)
    shape = (dec_total, tok_count * packed)
    line = lax.broadcasted_iota(jnp.int32, shape, 0)
    spot = lax.broadcasted_iota(jnp.int32, shape, 1)
    for block in range(width // columns):
        wanted = (line // dec_each) * packed + block * dec_each + line % dec_each
        picker = jnp.where(spot == wanted, 1.0, 0.0).astype(jnp.bfloat16)
        dec_rows_ref[:, block * columns : (block + 1) * columns] = jnp.dot(
            picker, flat, preferred_element_type=jnp.float32
        ).astype(jnp.bfloat16)
    dec_normed[...] = norm(dec_rows_ref[...].astype(jnp.float32))

    rows_each = min(256, tok_count * piece)

    def give(kind, offset):
        dest = lax.rem(me + offset, tok_count)
        return pltpu.make_async_remote_copy(
            src_ref=staged.at[kind, pl.ds(pl.multiple_of(dest * piece, piece), piece), :],
            dst_ref=out_ref.at[kind, pl.ds(pl.multiple_of(me * piece, piece), piece), :],
            send_sem=send.at[kind, offset],
            recv_sem=recv.at[kind, offset],
            device_id={"tok": dest},
            device_id_type=MESH,
        )

    def keep(kind):
        mine = pl.ds(pl.multiple_of(me * piece, piece), piece)
        return pltpu.make_async_copy(
            staged.at[kind, mine, :], out_ref.at[kind, mine, :], local.at[kind]
        )

    for kind in range(3):
        if kind + 2 < 3:
            gathers[kind + 2].relay()
        if kind + 1 < 3:
            gathers[kind + 1].relay_far()
        gathers[kind].collect()
        weights = w_v.at[pl.ds(kind * group, group), :]

        def multiply(index, carry):
            begin = pl.multiple_of(index * rows_each, rows_each)
            staged[kind, pl.ds(begin, rows_each), :] = nt_dot(
                normed[pl.ds(begin, rows_each), :], weights[...]
            ).astype(jnp.bfloat16)
            return carry

        lax.fori_loop(0, tok_count * piece // rows_each, multiply, 0)
        for offset in range(1, tok_count):
            give(kind, offset).start()
        keep(kind).start()
        dec_out_ref[kind] = nt_dot(dec_normed[...], weights[...]).astype(jnp.bfloat16)

    for gather in gathers:
        gather.drain()
    for kind in range(3):
        for offset in range(1, tok_count):
            give(kind, offset).wait()
        keep(kind).wait()


def project_layer(pre_order, rows, dec_packed, gain, w_qkv):
    tok_count, piece, width = rows.shape
    group = w_qkv.shape[0] // 3
    columns = w_qkv.shape[1]
    packed = dec_packed.shape[0]
    dec_total = tok_count * packed * columns // width
    span = tok_count * piece
    any_space = pl.BlockSpec(memory_space=pl.ANY)
    in_vmem = pl.BlockSpec(memory_space=pltpu.VMEM)
    slots = PlaneGather.slots()
    return pl.pallas_call(
        project_kernel,
        out_shape=(
            jax.ShapeDtypeStruct((3, span, group), jnp.bfloat16),
            jax.ShapeDtypeStruct((3, dec_total, group), jnp.bfloat16),
            jax.ShapeDtypeStruct((dec_total, width), jnp.bfloat16),
        ),
        in_specs=[
            pl.BlockSpec(memory_space=pltpu.SMEM),
            in_vmem,
            any_space,
            in_vmem,
            any_space,
        ],
        out_specs=(any_space, in_vmem, in_vmem),
        scratch_shapes=[
            pltpu.VMEM((3 * group, width), jnp.bfloat16),
            pltpu.VMEM((tok_count, packed, columns), jnp.bfloat16),
            pltpu.VMEM((span, width), jnp.bfloat16),
            pltpu.VMEM((dec_total, width), jnp.bfloat16),
            pltpu.VMEM((3, span, group), jnp.bfloat16),
            pltpu.SemaphoreType.DMA((3, slots)),
            pltpu.SemaphoreType.DMA((3, slots)),
            pltpu.SemaphoreType.DMA((3,)),
            pltpu.SemaphoreType.DMA((3, tok_count)),
            pltpu.SemaphoreType.DMA((3, tok_count)),
            pltpu.SemaphoreType.DMA((3,)),
            pltpu.SemaphoreType.DMA((tok_count,)),
            pltpu.SemaphoreType.DMA((tok_count,)),
            pltpu.SemaphoreType.DMA,
        ],
        compiler_params=pltpu.CompilerParams(
            collective_id=1, has_side_effects=True, vmem_limit_bytes=48 * 1024 * 1024
        ),
        cost_estimate=pl.CostEstimate(
            flops=6 * span * width * group,
            bytes_accessed=2 * (span * width + 6 * span * group + 3 * group * width),
            transcendentals=span,
        ),
        name="project_layer",
    )(pre_order, rows, dec_packed, gain[None], w_qkv)


def attend_pair(limit, q_ref, k_ref, v_ref, cos_ref, sin_ref, cache_ref, pair_at, q_rot, k_rot, v_ext, c_ext, out_ref):
    span = q_rot.shape[1]
    length = c_ext.shape[1]
    pair = q_rot.shape[2]
    cosine = cos_ref[...]
    sine = sin_ref[...]
    lane = lax.broadcasted_iota(jnp.int32, (1, pair), 1)
    halves = (lane < HD, lane >= HD)

    key = k_ref[:, pair_at].astype(jnp.float32)
    k_rot[...] = (key * cosine + swap_halves(key) * sine).astype(jnp.bfloat16)
    query = q_ref[:, pair_at].astype(jnp.float32)
    query = (query * cosine + swap_halves(query) * sine).astype(jnp.bfloat16)
    query = query * jnp.bfloat16(HD**-0.5)
    one = jnp.ones((), jnp.bfloat16)
    zero = jnp.zeros((), jnp.bfloat16)
    for side in range(2):
        q_rot[side] = jnp.where(halves[side], query, zero)
        v_ext[side] = jnp.where(halves[side], v_ref[:, pair_at], one)
        c_ext[side] = jnp.where(halves[side], cache_ref[1, :, pair_at], one)

    def fold(state, scores, values):
        top, mixed = state
        new_top = jnp.maximum(top, jnp.max(scores, axis=-1, keepdims=True))
        weights = jnp.exp(scores - new_top).astype(jnp.bfloat16)
        factor = jnp.exp(top - new_top)
        return new_top, mixed * factor + jnp.dot(
            weights, values, preferred_element_type=jnp.float32
        )

    for block in range(span // Q_ROWS):
        start = block * Q_ROWS
        rows = [q_rot[side, start : start + Q_ROWS, :] for side in range(2)]
        keys = k_rot[start : start + Q_ROWS, :]
        shape = (Q_ROWS, Q_ROWS)
        seen = lax.broadcasted_iota(jnp.int32, shape, 1) <= lax.broadcasted_iota(
            jnp.int32, shape, 0
        )
        states = []
        for side in range(2):
            scores = jnp.where(seen, nt_dot(rows[side], keys), masked_score)
            top = jnp.max(scores, axis=-1, keepdims=True)
            weights = jnp.exp(scores - top).astype(jnp.bfloat16)
            mixed = jnp.dot(
                weights,
                v_ext[side, start : start + Q_ROWS, :],
                preferred_element_type=jnp.float32,
            )
            states.append((top, mixed))
        for earlier in range(block):
            begin = earlier * Q_ROWS
            keys = k_rot[begin : begin + Q_ROWS, :]
            for side in range(2):
                states[side] = fold(
                    states[side],
                    nt_dot(rows[side], keys),
                    v_ext[side, begin : begin + Q_ROWS, :],
                )

        def cached(index, state):
            begin = pl.multiple_of(index * K_ROWS, K_ROWS)
            keys_now = cache_ref[0, pl.ds(begin, K_ROWS), pair_at]
            spot = begin + lax.broadcasted_iota(jnp.int32, (1, K_ROWS), 1)
            live = spot < limit
            result = []
            for side in range(2):
                scores = jnp.where(live, nt_dot(rows[side], keys_now), masked_score)
                result.append(
                    fold(state[side], scores, c_ext[side, pl.ds(begin, K_ROWS), :])
                )
            return tuple(result)

        states = lax.fori_loop(0, length // K_ROWS, cached, tuple(states))
        parts = []
        for side in range(2):
            mixed = states[side][1]
            total = pltpu.roll(mixed, HD, 1)
            parts.append(mixed / total)
        out_ref[start : start + Q_ROWS, :] = jnp.where(halves[0], parts[0], parts[1]).astype(
            jnp.bfloat16
        )


GU_CHUNKS = 4
ROW_CHUNKS = 2
AHEAD = 2


def attend_kernel(
    limit_ref,
    qkv_ref,
    cos_ref,
    sin_ref,
    cache_ref,
    dec_ref,
    w_gu_ref,
    w_out_ref,
    dec_all_ref,
    att_ref,
    gu_ref,
    outw_ref,
    q_rot,
    k_rot,
    v_ext,
    c_ext,
    mixed,
    g_send,
    g_recv,
    g_local,
    b_send,
    b_recv,
    b_local,
    z_send,
    z_recv,
    d_send,
    d_recv,
    d_local,
    e_send,
    e_recv,
):
    tok_count = lax.axis_size("tok")
    head_count = lax.axis_size("head")
    me = lax.axis_index("tok")
    head = lax.axis_index("head")
    last = head_count - 1
    span, group = qkv_ref.shape[1:]
    piece = span // tok_count
    pair = 2 * HD
    pairs = group // pair

    gathers = []
    for source, target, axis, chunks in (
        (w_gu_ref, gu_ref, 1, GU_CHUNKS),
        (w_out_ref, outw_ref, 0, ROW_CHUNKS),
    ):
        extent = source.shape[0] // chunks
        for chunk in range(chunks):
            at = len(gathers)
            gathers.append(
                PlaneGather(
                    source, target, axis, chunk * extent, extent, g_send.at[at], g_recv.at[at], g_local.at[at]
                )
            )
    total = len(gathers)

    def pump(index):
        gathers[index].relay()
        if index + AHEAD < total:
            gathers[index + AHEAD].start()
        if index > 0:
            gathers[index - 1].relay_far()

    def spot_of(rows, origin, index):
        begin = pl.multiple_of(origin * group + index * pair, pair)
        return att_ref.at[rows, pl.ds(begin, pair)]

    def back(index, offset):
        dest = lax.rem(me + offset, tok_count)
        return pltpu.make_async_remote_copy(
            src_ref=mixed.at[index, pl.ds(pl.multiple_of(dest * piece, piece), piece), :],
            dst_ref=spot_of(pl.ds(pl.multiple_of(me * piece, piece), piece), head, index),
            send_sem=b_send.at[index, offset],
            recv_sem=b_recv.at[index, offset],
            device_id={"tok": dest},
            device_id_type=MESH,
        )

    def back_keep(index):
        mine = pl.ds(pl.multiple_of(me * piece, piece), piece)
        return pltpu.make_async_copy(
            mixed.at[index, mine, :], spot_of(mine, head, index), b_local.at[index]
        )

    def pass_on(way, origin, index):
        block = spot_of(pl.ds(0, span), origin, index)
        target = jnp.minimum(head + 1, last) if way == 0 else jnp.maximum(head - 1, 0)
        return pltpu.make_async_remote_copy(
            src_ref=block,
            dst_ref=block,
            send_sem=z_send.at[way, origin, index],
            recv_sem=z_recv.at[way, origin, index],
            device_id={"head": target},
            device_id_type=MESH,
        )

    goes = (head < last, head > 0)

    def originate(index):
        for offset in range(1, tok_count):
            back(index, offset).wait_recv()
        back_keep(index).wait()
        for way in range(2):

            @pl.when(goes[way])
            def _():
                pass_on(way, head, index).start()

    def relay(index, hop):
        for way in range(2):
            origin = head - hop if way == 0 else head + hop
            there = origin >= 0 if way == 0 else origin <= last

            @pl.when(there)
            def _():
                pass_on(way, origin, index).wait_recv()

                @pl.when(goes[way])
                def _():
                    pass_on(way, origin, index).start()

    dec_pad = dec_ref.shape[0]
    dec_columns = pl.ds(pl.multiple_of(head * group, group), group)
    dec_mine = dec_all_ref.at[pl.ds(pl.multiple_of(me * dec_pad, dec_pad), dec_pad), dec_columns]
    dec_keep = pltpu.make_async_copy(dec_ref, dec_mine, d_local)

    def dec_copy(offset):
        return pltpu.make_async_remote_copy(
            src_ref=dec_ref,
            dst_ref=dec_mine,
            send_sem=d_send.at[offset],
            recv_sem=d_recv.at[offset],
            device_id={"tok": lax.rem(me + offset, tok_count)},
            device_id_type=MESH,
        )

    def dec_spread(offset):
        return pltpu.make_async_remote_copy(
            src_ref=dec_all_ref.at[:, dec_columns],
            dst_ref=dec_all_ref.at[:, dec_columns],
            send_sem=e_send.at[offset],
            recv_sem=e_recv.at[offset],
            device_id={"head": lax.rem(head + offset, head_count)},
            device_id_type=MESH,
        )

    greet(("tok", "head"))
    dec_keep.start()
    for offset in range(1, tok_count):
        dec_copy(offset).start()
    for gather in gathers[:AHEAD]:
        gather.start()

    limit = limit_ref[0]
    every = max(1, pairs // 2)

    def one_pair(index, carry):
        pair_at = pl.ds(pl.multiple_of(index * pair, pair), pair)
        attend_pair(
            limit,
            qkv_ref.at[0],
            qkv_ref.at[1],
            qkv_ref.at[2],
            cos_ref,
            sin_ref,
            cache_ref.at[0],
            pair_at,
            q_rot,
            k_rot,
            v_ext,
            c_ext,
            mixed.at[index],
        )
        for offset in range(1, tok_count):
            back(index, offset).start()
        back_keep(index).start()

        @pl.when(index > 0)
        def _():
            originate(index - 1)

        for turn in range(2):

            @pl.when(index == (turn + 1) * every - 1)
            def _():
                pump(turn)

        return carry

    lax.fori_loop(0, pairs, one_pair, 0)
    originate(pairs - 1)
    dec_keep.wait()
    for offset in range(1, tok_count):
        dec_copy(offset).wait()
    for offset in range(1, head_count):
        dec_spread(offset).start()

    def relay_all(hop):
        def body(index, carry):
            relay(index, hop)
            return carry

        lax.fori_loop(0, pairs, body, 0)

    hop = 1
    for index in range(2, total):
        pump(index)
        if hop <= last:
            relay_all(hop)
            hop += 1
    while hop <= last:
        relay_all(hop)
        hop += 1
    gathers[total - 1].relay_far()
    for offset in range(1, head_count):
        dec_spread(offset).wait()
    for gather in gathers:
        gather.collect()
    for gather in gathers:
        gather.drain()

    def drain(index, carry):
        for offset in range(1, tok_count):
            back(index, offset).wait_send()
        for origin in range(head_count):
            for way in range(2):
                passed = origin <= head if way == 0 else origin >= head

                @pl.when(jnp.logical_and(passed, goes[way]))
                def _():
                    pass_on(way, origin, index).wait_send()

        return carry

    lax.fori_loop(0, pairs, drain, 0)


def attend_layer(qkv, offset, cache, dec_att, w_gu, w_out):
    tok_count = lax.axis_size("tok")
    head_count = lax.axis_size("head")
    _, span, group = qkv.shape
    length = cache.shape[2]
    pair = 2 * HD
    pairs = group // pair
    cosine, sine = rope_tables(offset + jnp.arange(span, dtype=jnp.int32), pair)
    any_space = pl.BlockSpec(memory_space=pl.ANY)
    in_vmem = pl.BlockSpec(memory_space=pltpu.VMEM)
    slots = PlaneGather.slots()
    total = GU_CHUNKS + ROW_CHUNKS
    gather_sems = pltpu.SemaphoreType.DMA((total, slots))
    back_sems = pltpu.SemaphoreType.DMA((pairs, tok_count))
    pass_sems = pltpu.SemaphoreType.DMA((2, head_count, pairs))
    return pl.pallas_call(
        attend_kernel,
        out_shape=(
            jax.ShapeDtypeStruct((tok_count * dec_att.shape[0], head_count * group), jnp.bfloat16),
            jax.ShapeDtypeStruct((span, head_count * group), jnp.bfloat16),
            jax.ShapeDtypeStruct((w_gu.shape[0], tok_count * w_gu.shape[1]), jnp.bfloat16),
            jax.ShapeDtypeStruct((tok_count * w_out.shape[0], w_out.shape[1]), jnp.bfloat16),
        ),
        in_specs=[pl.BlockSpec(memory_space=pltpu.SMEM)] + [in_vmem] * 7,
        out_specs=(in_vmem,) + (any_space,) * 3,
        scratch_shapes=[
            pltpu.VMEM((2, span, pair), jnp.bfloat16),
            pltpu.VMEM((span, pair), jnp.bfloat16),
            pltpu.VMEM((2, span, pair), jnp.bfloat16),
            pltpu.VMEM((2, length, pair), jnp.bfloat16),
            pltpu.VMEM((pairs, span, pair), jnp.bfloat16),
            gather_sems,
            gather_sems,
            pltpu.SemaphoreType.DMA((total,)),
            back_sems,
            back_sems,
            pltpu.SemaphoreType.DMA((pairs,)),
            pass_sems,
            pass_sems,
            pltpu.SemaphoreType.DMA((tok_count,)),
            pltpu.SemaphoreType.DMA((tok_count,)),
            pltpu.SemaphoreType.DMA,
            pltpu.SemaphoreType.DMA((head_count,)),
            pltpu.SemaphoreType.DMA((head_count,)),
        ],
        compiler_params=pltpu.CompilerParams(
            collective_id=2, has_side_effects=True, vmem_limit_bytes=56 * 1024 * 1024
        ),
        cost_estimate=pl.CostEstimate(
            flops=16 * span * 3 * span * group,
            bytes_accessed=4 * length * group + 8 * span * group,
            transcendentals=span * 3 * span * group // HD,
        ),
        name="attend_layer",
    )(offset[None], qkv, cosine, sine, cache, dec_att, w_gu, w_out)


def copy_block(order_ref, source_ref, target_ref):
    target_ref[...] = source_ref[...]


def unpermuted(blocks, order):
    count, piece, width = blocks.shape
    return pl.pallas_call(
        copy_block,
        out_shape=jax.ShapeDtypeStruct(blocks.shape, blocks.dtype),
        grid_spec=pltpu.PrefetchScalarGridSpec(
            num_scalar_prefetch=1,
            grid=(count,),
            in_specs=[pl.BlockSpec((1, piece, width), lambda index, order: (index, 0, 0))],
            out_specs=pl.BlockSpec((1, piece, width), lambda index, order: (order[index], 0, 0)),
        ),
        name="unpermute",
    )(order, blocks)


def mlp_kernel(
    head_count,
    order_ref,
    att_ref,
    rows_ref,
    dec_att_ref,
    dec_rows_ref,
    gain_ref,
    w_out_ref,
    w_gu_ref,
    w_down_ref,
    out_ref,
    dec_out_ref,
    hidden,
    w_out_v,
    w_gu_v,
    w_down_v,
    resid,
    mlp_in,
    wide_v,
    slots,
    dec_slots,
    load_sem,
    rs_send,
    rs_recv,
    ag_send,
    ag_recv,
    keep_sem,
    dec_send,
    dec_recv,
    g_send,
    g_recv,
    g_local,
):
    last = head_count - 1
    me = lax.axis_index("head")
    span, width = att_ref.shape
    half = span // 2
    count = half // CHUNK
    units = w_gu_ref.shape[0] // 2
    pieces, piece = rows_ref.shape[:2]
    dec = dec_att_ref.shape[0]
    group = (wide_v.shape[0] - dec) // 2

    loads = [
        pltpu.make_async_copy(att_ref, hidden.at[pl.ds(0, span), pl.ds(0, width)], load_sem.at[0]),
        pltpu.make_async_copy(w_out_ref, w_out_v, load_sem.at[1]),
        pltpu.make_async_copy(w_gu_ref, w_gu_v, load_sem.at[2]),
    ]
    for copy in loads:
        copy.start()
    extent = w_down_ref.shape[0] // ROW_CHUNKS
    gathers = [
        PlaneGather(
            w_down_ref, w_down_v, 0, chunk * extent, extent, g_send.at[chunk], g_recv.at[chunk], g_local.at[chunk]
        )
        for chunk in range(ROW_CHUNKS)
    ]
    greet(("tok", "head"))
    for gather in gathers:
        gather.start()
    hidden[span:, :width] = dec_att_ref[...]

    def begin_rows(index, carry):
        at = pl.ds(pl.multiple_of(index * piece, piece), piece)
        resid[at, :] = rows_ref[order_ref[index]].astype(jnp.float32)
        return carry

    lax.fori_loop(0, pieces, begin_rows, 0)
    resid[span:, :] = dec_rows_ref[...].astype(jnp.float32)
    loads[0].wait()
    loads[1].wait()
    out_tile, out_tiles = tiles_of(width)
    unit_tile, unit_tiles = tiles_of(units)

    def rows_in(begin, block):
        at = slice(begin, begin + block)

        def project(tile, squares):
            columns = pl.ds(pl.multiple_of(tile * out_tile, out_tile), out_tile)
            value = resid[at, columns] + nt_dot(hidden[at, :width], w_out_v[columns, :])
            resid[at, columns] = value
            return squares + jnp.sum(value * value, axis=-1, keepdims=True)

        squares = lax.fori_loop(0, out_tiles, project, jnp.zeros((block, 1), jnp.float32))
        factor = lax.rsqrt(squares / width + norm_eps)
        mlp_in[:block, :] = (resid[at, :] * factor * gain_ref[...]).astype(jnp.bfloat16)
        if begin == 0:
            loads[2].wait()

        def gate_up(tile, carry):
            begin = pl.multiple_of(tile * unit_tile, unit_tile)
            gate = 0.5 * nt_dot(mlp_in[:block, :], w_gu_v[pl.ds(begin, unit_tile), :])
            up = nt_dot(mlp_in[:block, :], w_gu_v[pl.ds(units + begin, unit_tile), :])
            hidden[at, pl.ds(begin, unit_tile)] = (
                (gate + gate * jnp.tanh(gate)) * up
            ).astype(jnp.bfloat16)
            return carry

        lax.fori_loop(0, unit_tiles, gate_up, 0)

    rows_in(0, half)
    for gather in gathers:
        gather.relay()
    rows_in(half, half + dec)
    for gather in gathers:
        gather.relay_far()
    for gather in gathers:
        gather.collect()

    spot = lax.broadcasted_iota(jnp.int32, (2 * group, 1), 0)
    owner = jnp.where(spot < group, 0, last)
    owned = jnp.where(owner == me, 1.0, 0.0).astype(jnp.float32)
    wide_v[2 * group :, :] = hidden[span:, :units]

    def dec_copy(offset):
        return pltpu.make_async_remote_copy(
            src_ref=dec_slots.at[me],
            dst_ref=dec_slots.at[me],
            send_sem=dec_send.at[offset],
            recv_sem=dec_recv.at[offset],
            device_id={"head": lax.rem(me + offset, head_count)},
            device_id_type=MESH,
        )

    def compute(index):
        spots = [
            pl.ds(pl.multiple_of(side * half + index * group, group), group) for side in range(2)
        ]
        for side in range(2):
            wide_v[side * group : (side + 1) * group, :] = hidden[spots[side], :units]

        def down(tile, carry):
            columns = pl.ds(pl.multiple_of(tile * out_tile, out_tile), out_tile)
            value = nt_dot(wide_v[...], w_down_v[columns, :])
            for side in range(2):
                mine = slice(side * group, (side + 1) * group)
                resid[spots[side], columns] = (
                    value[mine] + resid[spots[side], columns] * owned[mine]
                )

            @pl.when(index == 0)
            def _():
                dec_slots[me, :, columns] = value[2 * group :].astype(jnp.bfloat16)

            return carry

        lax.fori_loop(0, out_tiles, down, 0)

        @pl.when(index == 0)
        def _():
            for offset in range(1, head_count):
                dec_copy(offset).start()

    def out_rows(side, index):
        return out_ref.at[pl.ds(pl.multiple_of(side * half + index * CHUNK, CHUNK), CHUNK)]

    def next_of(side):
        return jnp.maximum(me - 1, 0) if side == 0 else jnp.minimum(me + 1, last)

    def before_of(side):
        return next_of(1 - side)

    def sum_copy(side, index):
        return pltpu.make_async_remote_copy(
            src_ref=slots.at[side, index],
            dst_ref=slots.at[side, index],
            send_sem=rs_send.at[side, index],
            recv_sem=rs_recv.at[side, index],
            device_id={"head": next_of(side)},
            device_id_type=MESH,
        )

    def final_copy(side, index, source):
        return pltpu.make_async_remote_copy(
            src_ref=source,
            dst_ref=out_rows(side, index),
            send_sem=ag_send.at[side, index],
            recv_sem=ag_recv.at[side, index],
            device_id={"head": before_of(side)},
            device_id_type=MESH,
        )

    def keep_copy(side, index):
        return pltpu.make_async_copy(
            slots.at[side, index], out_rows(side, index), keep_sem.at[side, index]
        )

    hops = [last - me, me]
    to_end = [me, last - me]

    def combine(side, index):
        mine = pl.ds(pl.multiple_of(side * half + index * CHUNK, CHUNK), CHUNK)

        @pl.when(hops[side] == 0)
        def _():
            slots[side, index] = resid[mine, :].astype(jnp.bfloat16)

        @pl.when(hops[side] > 0)
        def _():
            sum_copy(side, index).wait_recv()
            slots[side, index] = (
                resid[mine, :] + slots[side, index].astype(jnp.float32)
            ).astype(jnp.bfloat16)

        @pl.when(to_end[side] > 0)
        def _():
            sum_copy(side, index).start()

        @pl.when(to_end[side] == 0)
        def _():
            final_copy(side, index, slots.at[side, index]).start()
            keep_copy(side, index).start()

    def forward(side, index):
        final_copy(side, index, out_rows(side, index)).wait_recv()

        @pl.when(hops[side] > 0)
        def _():
            final_copy(side, index, out_rows(side, index)).start()

    every = group // CHUNK

    def tick(step, carry):
        @pl.when(jnp.logical_and(step < count, lax.rem(step, every) == 0))
        def _():
            compute(step // every)

        for side in range(2):
            index = step - hops[side]

            @pl.when(jnp.logical_and(index >= 0, index < count))
            def _():
                combine(side, index)

        for side in range(2):
            spread = step - last - to_end[side]

            @pl.when(
                jnp.logical_and(
                    to_end[side] > 0, jnp.logical_and(spread >= 0, spread < count)
                )
            )
            def _():
                forward(side, spread)

        return carry

    lax.fori_loop(0, count + 2 * last, tick, 0)

    for offset in range(1, head_count):
        dec_copy(offset).wait()
    total = resid[span:, :]
    for index in range(head_count):
        total = total + dec_slots[index].astype(jnp.float32)
    dec_out_ref[...] = total.astype(jnp.bfloat16)

    for gather in gathers:
        gather.drain()

    def drain(index, carry):
        for side in range(2):

            @pl.when(to_end[side] > 0)
            def _():
                sum_copy(side, index).wait_send()

            @pl.when(to_end[side] == 0)
            def _():
                keep_copy(side, index).wait()

            @pl.when(hops[side] > 0)
            def _():
                final_copy(side, index, out_rows(side, index)).wait_send()

        return carry

    lax.fori_loop(0, count, drain, 0)


def mlp_layer(pre_order, att, rows, dec_att, dec_rows, gain, w_out, w_gu, w_down):
    head_count = lax.axis_size("head")
    tok_count = lax.axis_size("tok")
    span, width = att.shape
    units = w_gu.shape[0] // 2
    count = span // 2 // CHUNK
    dec = dec_att.shape[0]
    group = min(GROUP_ROWS, span // 2)
    any_space = pl.BlockSpec(memory_space=pl.ANY)
    in_vmem = pl.BlockSpec(memory_space=pltpu.VMEM)
    both = pltpu.SemaphoreType.DMA((2, count))
    gather_sems = pltpu.SemaphoreType.DMA((ROW_CHUNKS, PlaneGather.slots()))
    return pl.pallas_call(
        functools.partial(mlp_kernel, head_count),
        out_shape=(
            jax.ShapeDtypeStruct((span, width), jnp.bfloat16),
            jax.ShapeDtypeStruct((dec, width), jnp.bfloat16),
        ),
        in_specs=[pl.BlockSpec(memory_space=pltpu.SMEM), any_space]
        + [in_vmem] * 4
        + [any_space] * 3,
        out_specs=(any_space, in_vmem),
        scratch_shapes=[
            pltpu.VMEM((span + dec, max(width, units)), jnp.bfloat16),
            pltpu.VMEM(w_out.shape, jnp.bfloat16),
            pltpu.VMEM(w_gu.shape, jnp.bfloat16),
            pltpu.VMEM((tok_count * w_down.shape[0], units), jnp.bfloat16),
            pltpu.VMEM((span + dec, width), jnp.float32),
            pltpu.VMEM((span // 2 + dec, width), jnp.bfloat16),
            pltpu.VMEM((2 * group + dec, units), jnp.bfloat16),
            pltpu.VMEM((2, count, CHUNK, width), jnp.bfloat16),
            pltpu.VMEM((head_count, dec, width), jnp.bfloat16),
            pltpu.SemaphoreType.DMA((3,)),
            both,
            both,
            both,
            both,
            both,
            pltpu.SemaphoreType.DMA((head_count,)),
            pltpu.SemaphoreType.DMA((head_count,)),
            gather_sems,
            gather_sems,
            pltpu.SemaphoreType.DMA((ROW_CHUNKS,)),
        ],
        compiler_params=pltpu.CompilerParams(
            collective_id=3, has_side_effects=True, vmem_limit_bytes=60 * 1024 * 1024
        ),
        cost_estimate=pl.CostEstimate(
            flops=2 * span * width * (width + 3 * units),
            bytes_accessed=2 * (4 * span * width + w_out.size + w_gu.size + w_down.size),
            transcendentals=span * units,
        ),
        name="mlp_layer",
    )(pre_order, att, rows, dec_att, dec_rows, gain[None], w_out, w_gu, w_down)


def picked_rows(rows, order):
    count = rows.shape[0]
    picker = order[:, None] == jnp.arange(count, dtype=jnp.int32)[None, :]
    return jnp.dot(
        picker.astype(jnp.bfloat16), rows, preferred_element_type=jnp.float32
    ).astype(jnp.bfloat16)


def inverse_of(order):
    spots = jnp.arange(order.shape[0], dtype=jnp.int32)
    return jnp.sum(jnp.where(order[None, :] == spots[:, None], spots[None, :], 0), axis=1)


def on_device(
    pre_tokens,
    dec_tokens,
    attn_gain,
    mlp_gain,
    w_qkv,
    w_out,
    w_gate_up,
    w_down,
    pre_cache,
    dec_cache,
    pre_order,
    dec_order,
    pre_offsets,
    dec_lengths,
):
    tok_count = lax.axis_size("tok")
    tok_index = lax.axis_index("tok")
    head_count = lax.axis_size("head")
    span_rows, width = pre_tokens.shape
    piece_len = span_rows // tok_count
    dec_local = dec_tokens.shape[0]
    group_width, depth = w_qkv.shape[1:]
    units = w_gate_up.shape[1]

    blocks = pre_tokens.reshape(tok_count, piece_len, width)
    packed = dec_tokens.reshape(dec_local, width // depth, depth)
    packed = jnp.transpose(packed, (1, 0, 2)).reshape(dec_local * width // depth, depth)
    qkv, dec_qkv, dec_rows = project_layer(
        pre_order, blocks, packed, attn_gain, w_qkv.reshape(3 * group_width, depth)
    )
    w_out_rows = lax.all_gather(w_out, "head", axis=1, tiled=True)

    own_slots = lax.dynamic_slice_in_dim(dec_order, tok_index * dec_local, dec_local)
    dec_mine = jnp.stack([picked_rows(dec_qkv[which], own_slots) for which in range(3)])
    dec_att = decode_attend(dec_mine, dec_lengths, dec_cache)
    dec_att = jnp.pad(dec_att, ((0, DEC_PAD - dec_local), (0, 0)))

    dec_all, attended, gate_up_full, out_full = attend_layer(
        qkv,
        pre_offsets[0],
        pre_cache,
        dec_att,
        w_gate_up.reshape(2 * units, depth),
        w_out_rows,
    )
    dec_spots = inverse_of(dec_order)
    dec_spots = dec_spots // dec_local * DEC_PAD + dec_spots % dec_local
    dec_all = picked_rows(dec_all, dec_spots)
    pre_out, dec_out = mlp_layer(
        pre_order,
        attended,
        blocks,
        dec_all,
        dec_rows,
        mlp_gain,
        out_full,
        gate_up_full,
        w_down,
    )
    pre_out = unpermuted(pre_out.reshape(tok_count, piece_len, width), pre_order)
    dec_out = lax.dynamic_slice_in_dim(dec_out, tok_index * dec_local, dec_local)
    return (pre_out.reshape(span_rows, width), dec_out)


def solution(mesh):
    placed = (
        P("tok", None),
        P("tok", None),
        P(),
        P(),
        P(None, "head", "tok"),
        P("tok", "head"),
        P(None, "head", "tok"),
        P("tok", "head"),
        P("tok", None, None, "head"),
        P("tok", None, None, "head"),
        P(),
        P(),
        P("tok"),
        P("tok"),
    )
    return jax.shard_map(
        on_device,
        mesh=mesh,
        in_specs=placed,
        out_specs=(P("tok", None), P("tok", None)),
        check_vma=False,
    )
```

```python
import functools

import jax
import jax.numpy as jnp
from jax import lax
from jax.experimental import pallas as pl
from jax.experimental.pallas import tpu as pltpu
from jax.sharding import PartitionSpec as P

HD = 64
Q_ROWS = 512
K_ROWS = 512
DEC_ROWS = 1024
DEC_PAD = 16


rope_base = 130000.0
norm_eps = 1e-05
masked_score = -1e30


def rotate(values, positions):
    width = values.shape[-1]
    half = width // 2
    freqs = rope_base ** (-(jnp.arange(half, dtype=jnp.float32) * 2.0 / width))
    angles = positions.astype(jnp.float32)[:, None] * freqs[None, :]
    cosine = jnp.cos(angles)[:, None, :]
    sine = jnp.sin(angles)[:, None, :]
    first = values[..., :half]
    second = values[..., half:]
    return jnp.concatenate(
        [first * cosine - second * sine, second * cosine + first * sine], axis=-1
    )


def rope_tables(positions, width):
    half = HD // 2
    freqs = rope_base ** (-(jnp.arange(half, dtype=jnp.float32) * 2.0 / HD))
    angles = positions.astype(jnp.float32)[:, None] * freqs[None, :]
    cosine = jnp.cos(angles)
    sine = jnp.sin(angles)
    copies = width // HD
    return (
        jnp.tile(jnp.concatenate([cosine, cosine], axis=1), (1, copies)),
        jnp.tile(jnp.concatenate([-sine, sine], axis=1), (1, copies)),
    )


def swap_halves(values):
    half = HD // 2
    width = values.shape[-1]
    lane = lax.broadcasted_iota(jnp.int32, values.shape, values.ndim - 1)
    axis = values.ndim - 1
    return jnp.where(
        lane % HD < half,
        pltpu.roll(values, width - half, axis),
        pltpu.roll(values, half, axis),
    )


def decode_inputs(qkv, lengths):
    _, count, width = qkv.shape
    heads = width // HD
    split = qkv.reshape(3, count, heads, HD)
    q_rot = rotate(split[0].astype(jnp.float32), lengths).astype(jnp.bfloat16)
    k_rot = rotate(split[1].astype(jnp.float32), lengths).astype(jnp.bfloat16)
    q_rot = q_rot * jnp.bfloat16(HD**-0.5)
    spread = jnp.where(
        jnp.eye(heads, dtype=jnp.bool_)[None, :, :, None], q_rot[:, None], jnp.bfloat16(0)
    ).reshape(count, heads, width)
    return spread, k_rot.reshape(count, 1, width), qkv[2].reshape(count, 1, width)


def decode_one(request, limit, q_ref, k_ref, v_ref, cache_ref):
    heads, width = q_ref.shape[1:]
    length = cache_ref.shape[2]
    rows = min(DEC_ROWS, length)
    query = q_ref[request]
    own = query.astype(jnp.float32) * k_ref[request].astype(jnp.float32)

    def fold(index, state):
        top, total, mixed = state
        begin = pl.multiple_of(index * rows, rows)
        scores = nt_dot(query, cache_ref[request, 0, pl.ds(begin, rows), :])
        spot = begin + lax.broadcasted_iota(jnp.int32, (1, rows), 1)
        scores = jnp.where(spot < limit, scores, masked_score)
        new_top = jnp.maximum(top, jnp.max(scores, axis=-1, keepdims=True))
        weights = jnp.exp(scores - new_top)
        factor = jnp.exp(top - new_top)
        values = cache_ref[request, 1, pl.ds(begin, rows), :]
        return (
            new_top,
            total * factor + jnp.sum(weights, axis=-1, keepdims=True),
            mixed * factor
            + jnp.dot(weights.astype(jnp.bfloat16), values, preferred_element_type=jnp.float32),
        )

    state = (
        jnp.sum(own, axis=-1, keepdims=True),
        jnp.ones((heads, 1), jnp.float32),
        jnp.broadcast_to(v_ref[request].astype(jnp.float32), (heads, width)),
    )
    _, total, mixed = lax.fori_loop(0, length // rows, fold, state)
    shape = (heads, width)
    mine = lax.broadcasted_iota(jnp.int32, shape, 1) // HD == lax.broadcasted_iota(
        jnp.int32, shape, 0
    )
    return jnp.sum(jnp.where(mine, mixed / total, 0.0), axis=0, keepdims=True)


MESH = pl.DeviceIdType.MESH
CHUNK = 32
GROUP_ROWS = 128
TILE = 512


def nt_dot(rows, weights):
    return lax.dot_general(
        rows, weights, (((1,), (1,)), ((), ())), preferred_element_type=jnp.float32
    )


def tiles_of(extent):
    tile = min(TILE, extent)
    return tile, extent // tile


class PlaneGather:
    SLOTS = 9

    def __init__(self, source, target, axis, begin, extent, send, recv, local):
        self.source, self.target, self.axis = source, target, axis
        self.begin, self.extent = begin, extent
        self.send, self.recv, self.local = send, recv, local
        self.count = lax.axis_size("tok")
        self.me = lax.axis_index("tok")
        me = self.me
        self.cube = self.count == 8
        if self.cube:
            core = lax.rem(me, 2)
            column = lax.rem(me // 2, 2)
            line = me // 4
            turn = 1 - 2 * core
            self.twin = me + turn
            self.x = me + 2 - 4 * column
            self.y = me + 4 - 8 * line
            far = self.x + self.y - me
            whole_part = (0, 2)
            self.table = [
                (me, whole_part, self.twin, self.twin),
                (me, whole_part, self.x, self.x),
                (me, whole_part, self.y, self.y),
                (self.x, whole_part, self.twin, self.x + turn),
                (self.y, whole_part, self.twin, self.y + turn),
                (self.x, (0, 1), self.y, far),
                (self.y, (1, 1), self.x, far),
                (far, (0, 1), self.twin, far + turn),
                (far, (1, 1), self.twin, far + turn),
            ]
        else:
            self.table = [
                (
                    me,
                    (0, 2),
                    lax.rem(me + offset, self.count),
                    lax.rem(me + self.count - offset, self.count),
                )
                for offset in range(1, self.count)
            ]

    @staticmethod
    def slots():
        count = lax.axis_size("tok")
        return PlaneGather.SLOTS if count == 8 else count - 1

    def place(self, tok, part):
        half = self.extent // 2
        begin, extent = self.begin + part[0] * half, part[1] * half
        rows, columns = self.source.shape
        if self.axis == 0:
            return self.target.at[pl.ds(pl.multiple_of(tok * rows + begin, 16), extent), :]
        return self.target.at[
            pl.ds(begin, extent), pl.ds(pl.multiple_of(tok * columns, columns), columns)
        ]

    def own(self):
        return self.source.at[pl.ds(self.begin, self.extent), :]

    def copy(self, slot):
        what, part, dest, _ = self.table[slot]
        source = self.own() if slot < 3 or not self.cube else self.place(what, part)
        return pltpu.make_async_remote_copy(
            src_ref=source,
            dst_ref=self.place(what, part),
            send_sem=self.send.at[slot],
            recv_sem=self.recv.at[slot],
            device_id={"tok": dest},
            device_id_type=MESH,
        )

    def arrived(self, slot):
        _, part, dest, comes = self.table[slot]
        place = self.place(comes, part)
        pltpu.make_async_remote_copy(
            src_ref=place,
            dst_ref=place,
            send_sem=self.send.at[slot],
            recv_sem=self.recv.at[slot],
            device_id={"tok": dest},
            device_id_type=MESH,
        ).wait_recv()

    def keep(self):
        return pltpu.make_async_copy(self.own(), self.place(self.me, (0, 2)), self.local)

    def start(self):
        first = (1, 2, 0) if self.cube else range(len(self.table))
        for slot in first:
            self.copy(slot).start()
        self.keep().start()

    def relay(self):
        if self.cube:
            self.arrived(1)
            self.copy(5).start()
            self.copy(3).start()
            self.arrived(2)
            self.copy(6).start()
            self.copy(4).start()

    def relay_far(self):
        if self.cube:
            self.arrived(5)
            self.copy(7).start()
            self.arrived(6)
            self.copy(8).start()

    def collect(self):
        for slot in (0, 3, 4, 7, 8) if self.cube else range(len(self.table)):
            self.arrived(slot)
        self.keep().wait()

    def drain(self):
        for slot in range(len(self.table)):
            self.copy(slot).wait_send()


def greet(axes):
    barrier = pltpu.get_barrier_semaphore()
    total = 0
    for axis in axes:
        count = lax.axis_size(axis)
        me = lax.axis_index(axis)
        for offset in range(1, count):
            pl.semaphore_signal(
                barrier,
                inc=1,
                device_id={axis: lax.rem(me + offset, count)},
                device_id_type=MESH,
            )
        total += count - 1
    pl.semaphore_wait(barrier, total)


def project_kernel(
    order_ref,
    x_ref,
    dec_ref,
    gain_ref,
    w_ref,
    out_ref,
    dec_out_ref,
    dec_rows_ref,
    w_v,
    dec_v,
    normed,
    dec_normed,
    staged,
    w_send,
    w_recv,
    w_local,
    send,
    recv,
    local,
    dec_send,
    dec_recv,
    dec_local,
):
    tok_count, piece, width = x_ref.shape
    me = lax.axis_index("tok")
    group = w_ref.shape[0] // 3
    columns = w_ref.shape[1]
    packed = dec_ref.shape[0]
    dec_each = packed * columns // width
    dec_total = tok_count * dec_each
    gathers = [
        PlaneGather(
            w_ref, w_v, 1, kind * group, group, w_send.at[kind], w_recv.at[kind], w_local.at[kind]
        )
        for kind in range(3)
    ]

    def dec_copy(offset):
        return pltpu.make_async_remote_copy(
            src_ref=dec_ref,
            dst_ref=dec_v.at[me],
            send_sem=dec_send.at[offset],
            recv_sem=dec_recv.at[offset],
            device_id={"tok": lax.rem(me + offset, tok_count)},
            device_id_type=MESH,
        )

    dec_keep = pltpu.make_async_copy(dec_ref, dec_v.at[me], dec_local)
    dec_keep.start()
    greet(("tok",))
    for gather in gathers:
        gather.start()
    for offset in range(1, tok_count):
        dec_copy(offset).start()

    def norm(rows):
        squares = jnp.mean(rows * rows, axis=-1, keepdims=True)
        return (rows * lax.rsqrt(squares + norm_eps) * gain_ref[...]).astype(jnp.bfloat16)

    def norm_piece(index, carry):
        rows = x_ref[order_ref[index]].astype(jnp.float32)
        normed[pl.ds(pl.multiple_of(index * piece, piece), piece), :] = norm(rows)
        return carry

    lax.fori_loop(0, tok_count, norm_piece, 0)
    gathers[0].relay()
    dec_keep.wait()
    for offset in range(1, tok_count):
        dec_copy(offset).wait()
    gathers[1].relay()
    gathers[0].relay_far()
    flat = dec_v[...].reshape(tok_count * packed, columns)
    shape = (dec_total, tok_count * packed)
    line = lax.broadcasted_iota(jnp.int32, shape, 0)
    spot = lax.broadcasted_iota(jnp.int32, shape, 1)
    for block in range(width // columns):
        wanted = (line // dec_each) * packed + block * dec_each + line % dec_each
        picker = jnp.where(spot == wanted, 1.0, 0.0).astype(jnp.bfloat16)
        dec_rows_ref[:, block * columns : (block + 1) * columns] = jnp.dot(
            picker, flat, preferred_element_type=jnp.float32
        ).astype(jnp.bfloat16)
    dec_normed[...] = norm(dec_rows_ref[...].astype(jnp.float32))

    rows_each = min(256, tok_count * piece)

    def give(kind, offset):
        dest = lax.rem(me + offset, tok_count)
        return pltpu.make_async_remote_copy(
            src_ref=staged.at[kind, pl.ds(pl.multiple_of(dest * piece, piece), piece), :],
            dst_ref=out_ref.at[kind, pl.ds(pl.multiple_of(me * piece, piece), piece), :],
            send_sem=send.at[kind, offset],
            recv_sem=recv.at[kind, offset],
            device_id={"tok": dest},
            device_id_type=MESH,
        )

    def keep(kind):
        mine = pl.ds(pl.multiple_of(me * piece, piece), piece)
        return pltpu.make_async_copy(
            staged.at[kind, mine, :], out_ref.at[kind, mine, :], local.at[kind]
        )

    for kind in range(3):
        if kind + 2 < 3:
            gathers[kind + 2].relay()
        if kind + 1 < 3:
            gathers[kind + 1].relay_far()
        gathers[kind].collect()
        weights = w_v.at[pl.ds(kind * group, group), :]

        def multiply(index, carry):
            begin = pl.multiple_of(index * rows_each, rows_each)
            staged[kind, pl.ds(begin, rows_each), :] = nt_dot(
                normed[pl.ds(begin, rows_each), :], weights[...]
            ).astype(jnp.bfloat16)
            return carry

        lax.fori_loop(0, tok_count * piece // rows_each, multiply, 0)
        for offset in range(1, tok_count):
            give(kind, offset).start()
        keep(kind).start()
        dec_out_ref[kind] = nt_dot(dec_normed[...], weights[...]).astype(jnp.bfloat16)

    for gather in gathers:
        gather.drain()
    for kind in range(3):
        for offset in range(1, tok_count):
            give(kind, offset).wait()
        keep(kind).wait()


def project_layer(pre_order, rows, dec_packed, gain, w_qkv):
    tok_count, piece, width = rows.shape
    group = w_qkv.shape[0] // 3
    columns = w_qkv.shape[1]
    packed = dec_packed.shape[0]
    dec_total = tok_count * packed * columns // width
    span = tok_count * piece
    any_space = pl.BlockSpec(memory_space=pl.ANY)
    in_vmem = pl.BlockSpec(memory_space=pltpu.VMEM)
    slots = PlaneGather.slots()
    return pl.pallas_call(
        project_kernel,
        out_shape=(
            jax.ShapeDtypeStruct((3, span, group), jnp.bfloat16),
            jax.ShapeDtypeStruct((3, dec_total, group), jnp.bfloat16),
            jax.ShapeDtypeStruct((dec_total, width), jnp.bfloat16),
        ),
        in_specs=[
            pl.BlockSpec(memory_space=pltpu.SMEM),
            in_vmem,
            any_space,
            in_vmem,
            any_space,
        ],
        out_specs=(any_space, in_vmem, in_vmem),
        scratch_shapes=[
            pltpu.VMEM((3 * group, width), jnp.bfloat16),
            pltpu.VMEM((tok_count, packed, columns), jnp.bfloat16),
            pltpu.VMEM((span, width), jnp.bfloat16),
            pltpu.VMEM((dec_total, width), jnp.bfloat16),
            pltpu.VMEM((3, span, group), jnp.bfloat16),
            pltpu.SemaphoreType.DMA((3, slots)),
            pltpu.SemaphoreType.DMA((3, slots)),
            pltpu.SemaphoreType.DMA((3,)),
            pltpu.SemaphoreType.DMA((3, tok_count)),
            pltpu.SemaphoreType.DMA((3, tok_count)),
            pltpu.SemaphoreType.DMA((3,)),
            pltpu.SemaphoreType.DMA((tok_count,)),
            pltpu.SemaphoreType.DMA((tok_count,)),
            pltpu.SemaphoreType.DMA,
        ],
        compiler_params=pltpu.CompilerParams(
            collective_id=1, has_side_effects=True, vmem_limit_bytes=48 * 1024 * 1024
        ),
        cost_estimate=pl.CostEstimate(
            flops=6 * span * width * group,
            bytes_accessed=2 * (span * width + 6 * span * group + 3 * group * width),
            transcendentals=span,
        ),
        name="project_layer",
    )(pre_order, rows, dec_packed, gain[None], w_qkv)


def attend_pair(limit, q_ref, k_ref, v_ref, cos_ref, sin_ref, cache_ref, pair_at, q_rot, k_rot, v_ext, c_ext, out_ref):
    span = q_rot.shape[1]
    length = c_ext.shape[1]
    pair = q_rot.shape[2]
    cosine = cos_ref[...]
    sine = sin_ref[...]
    lane = lax.broadcasted_iota(jnp.int32, (1, pair), 1)
    halves = (lane < HD, lane >= HD)

    key = k_ref[:, pair_at].astype(jnp.float32)
    k_rot[...] = (key * cosine + swap_halves(key) * sine).astype(jnp.bfloat16)
    query = q_ref[:, pair_at].astype(jnp.float32)
    query = (query * cosine + swap_halves(query) * sine).astype(jnp.bfloat16)
    query = query * jnp.bfloat16(HD**-0.5)
    one = jnp.ones((), jnp.bfloat16)
    zero = jnp.zeros((), jnp.bfloat16)
    for side in range(2):
        q_rot[side] = jnp.where(halves[side], query, zero)
        v_ext[side] = jnp.where(halves[side], v_ref[:, pair_at], one)
        c_ext[side] = jnp.where(halves[side], cache_ref[1, :, pair_at], one)

    def fold(state, scores, values):
        top, mixed = state
        new_top = jnp.maximum(top, jnp.max(scores, axis=-1, keepdims=True))
        weights = jnp.exp(scores - new_top).astype(jnp.bfloat16)
        factor = jnp.exp(top - new_top)
        return new_top, mixed * factor + jnp.dot(
            weights, values, preferred_element_type=jnp.float32
        )

    for block in range(span // Q_ROWS):
        start = block * Q_ROWS
        rows = [q_rot[side, start : start + Q_ROWS, :] for side in range(2)]
        keys = k_rot[start : start + Q_ROWS, :]
        shape = (Q_ROWS, Q_ROWS)
        seen = lax.broadcasted_iota(jnp.int32, shape, 1) <= lax.broadcasted_iota(
            jnp.int32, shape, 0
        )
        states = []
        for side in range(2):
            scores = jnp.where(seen, nt_dot(rows[side], keys), masked_score)
            top = jnp.max(scores, axis=-1, keepdims=True)
            weights = jnp.exp(scores - top).astype(jnp.bfloat16)
            mixed = jnp.dot(
                weights,
                v_ext[side, start : start + Q_ROWS, :],
                preferred_element_type=jnp.float32,
            )
            states.append((top, mixed))
        for earlier in range(block):
            begin = earlier * Q_ROWS
            keys = k_rot[begin : begin + Q_ROWS, :]
            for side in range(2):
                states[side] = fold(
                    states[side],
                    nt_dot(rows[side], keys),
                    v_ext[side, begin : begin + Q_ROWS, :],
                )

        def cached(index, state):
            begin = pl.multiple_of(index * K_ROWS, K_ROWS)
            keys_now = cache_ref[0, pl.ds(begin, K_ROWS), pair_at]
            spot = begin + lax.broadcasted_iota(jnp.int32, (1, K_ROWS), 1)
            live = spot < limit
            result = []
            for side in range(2):
                scores = jnp.where(live, nt_dot(rows[side], keys_now), masked_score)
                result.append(
                    fold(state[side], scores, c_ext[side, pl.ds(begin, K_ROWS), :])
                )
            return tuple(result)

        states = lax.fori_loop(0, length // K_ROWS, cached, tuple(states))
        parts = []
        for side in range(2):
            mixed = states[side][1]
            total = pltpu.roll(mixed, HD, 1)
            parts.append(mixed / total)
        out_ref[start : start + Q_ROWS, :] = jnp.where(halves[0], parts[0], parts[1]).astype(
            jnp.bfloat16
        )


GU_CHUNKS = 4
ROW_CHUNKS = 2
AHEAD = 2


def attend_kernel(
    limit_ref,
    qkv_ref,
    cos_ref,
    sin_ref,
    cache_ref,
    lengths_ref,
    dec_q_ref,
    dec_k_ref,
    dec_v_ref,
    dec_cache_ref,
    w_gu_ref,
    w_out_ref,
    dec_all_ref,
    att_ref,
    gu_ref,
    outw_ref,
    q_rot,
    k_rot,
    v_ext,
    c_ext,
    mixed,
    g_send,
    g_recv,
    g_local,
    b_send,
    b_recv,
    b_local,
    z_send,
    z_recv,
    d_send,
    d_recv,
    d_local,
    e_send,
    e_recv,
    dec_ref,
    dec_cache_v,
    dec_load,
):
    tok_count = lax.axis_size("tok")
    head_count = lax.axis_size("head")
    me = lax.axis_index("tok")
    head = lax.axis_index("head")
    last = head_count - 1
    span, group = qkv_ref.shape[1:]
    piece = span // tok_count
    pair = 2 * HD
    pairs = group // pair

    gathers = []
    for source, target, axis, chunks in (
        (w_gu_ref, gu_ref, 1, GU_CHUNKS),
        (w_out_ref, outw_ref, 0, ROW_CHUNKS),
    ):
        extent = source.shape[0] // chunks
        for chunk in range(chunks):
            at = len(gathers)
            gathers.append(
                PlaneGather(
                    source, target, axis, chunk * extent, extent, g_send.at[at], g_recv.at[at], g_local.at[at]
                )
            )
    total = len(gathers)

    def pump(index):
        gathers[index].relay()
        if index + AHEAD < total:
            gathers[index + AHEAD].start()
        if index > 0:
            gathers[index - 1].relay_far()

    def spot_of(rows, origin, index):
        begin = pl.multiple_of(origin * group + index * pair, pair)
        return att_ref.at[rows, pl.ds(begin, pair)]

    def back(index, offset):
        dest = lax.rem(me + offset, tok_count)
        return pltpu.make_async_remote_copy(
            src_ref=mixed.at[index, pl.ds(pl.multiple_of(dest * piece, piece), piece), :],
            dst_ref=spot_of(pl.ds(pl.multiple_of(me * piece, piece), piece), head, index),
            send_sem=b_send.at[index, offset],
            recv_sem=b_recv.at[index, offset],
            device_id={"tok": dest},
            device_id_type=MESH,
        )

    def back_keep(index):
        mine = pl.ds(pl.multiple_of(me * piece, piece), piece)
        return pltpu.make_async_copy(
            mixed.at[index, mine, :], spot_of(mine, head, index), b_local.at[index]
        )

    def pass_on(way, origin, index):
        block = spot_of(pl.ds(0, span), origin, index)
        target = jnp.minimum(head + 1, last) if way == 0 else jnp.maximum(head - 1, 0)
        return pltpu.make_async_remote_copy(
            src_ref=block,
            dst_ref=block,
            send_sem=z_send.at[way, origin, index],
            recv_sem=z_recv.at[way, origin, index],
            device_id={"head": target},
            device_id_type=MESH,
        )

    goes = (head < last, head > 0)

    def originate(index):
        for offset in range(1, tok_count):
            back(index, offset).wait_recv()
        back_keep(index).wait()
        for way in range(2):

            @pl.when(goes[way])
            def _():
                pass_on(way, head, index).start()

    def relay(index, hop):
        for way in range(2):
            origin = head - hop if way == 0 else head + hop
            there = origin >= 0 if way == 0 else origin <= last

            @pl.when(there)
            def _():
                pass_on(way, origin, index).wait_recv()

                @pl.when(goes[way])
                def _():
                    pass_on(way, origin, index).start()

    dec_pad = dec_ref.shape[0]
    dec_columns = pl.ds(pl.multiple_of(head * group, group), group)
    dec_mine = dec_all_ref.at[pl.ds(pl.multiple_of(me * dec_pad, dec_pad), dec_pad), dec_columns]
    dec_keep = pltpu.make_async_copy(dec_ref, dec_mine, d_local)

    def dec_copy(offset):
        return pltpu.make_async_remote_copy(
            src_ref=dec_ref,
            dst_ref=dec_mine,
            send_sem=d_send.at[offset],
            recv_sem=d_recv.at[offset],
            device_id={"tok": lax.rem(me + offset, tok_count)},
            device_id_type=MESH,
        )

    def dec_spread(offset):
        return pltpu.make_async_remote_copy(
            src_ref=dec_all_ref.at[:, dec_columns],
            dst_ref=dec_all_ref.at[:, dec_columns],
            send_sem=e_send.at[offset],
            recv_sem=e_recv.at[offset],
            device_id={"head": lax.rem(head + offset, head_count)},
            device_id_type=MESH,
        )

    dec_count = dec_q_ref.shape[0]
    dec_loads = [
        pltpu.make_async_copy(
            dec_cache_ref.at[request], dec_cache_v.at[request], dec_load.at[request]
        )
        for request in range(dec_count)
    ]

    def decode():
        line = lax.broadcasted_iota(jnp.int32, (dec_pad, 1), 0)
        result = jnp.zeros((dec_pad, group), jnp.float32)
        for request in range(dec_count):
            dec_loads[request].wait()
            row = decode_one(
                request, lengths_ref[request], dec_q_ref, dec_k_ref, dec_v_ref, dec_cache_v
            )
            result = jnp.where(line == request, row, result)
        dec_ref[...] = result.astype(jnp.bfloat16)
        dec_keep.start()
        for offset in range(1, tok_count):
            dec_copy(offset).start()

    def decode_on():
        dec_keep.wait()
        for offset in range(1, tok_count):
            dec_copy(offset).wait()
        for offset in range(1, head_count):
            dec_spread(offset).start()

    for load in dec_loads:
        load.start()
    greet(("tok", "head"))
    for gather in gathers[:AHEAD]:
        gather.start()

    limit = limit_ref[0]
    every = max(1, pairs // 2)

    def one_pair(index, carry):
        pair_at = pl.ds(pl.multiple_of(index * pair, pair), pair)
        attend_pair(
            limit,
            qkv_ref.at[0],
            qkv_ref.at[1],
            qkv_ref.at[2],
            cos_ref,
            sin_ref,
            cache_ref.at[0],
            pair_at,
            q_rot,
            k_rot,
            v_ext,
            c_ext,
            mixed.at[index],
        )
        for offset in range(1, tok_count):
            back(index, offset).start()
        back_keep(index).start()

        @pl.when(index > 0)
        def _():
            originate(index - 1)

        for turn in range(2):

            @pl.when(index == (turn + 1) * every - 1)
            def _():
                pump(turn)

        return carry

    lax.fori_loop(0, pairs, one_pair, 0)
    originate(pairs - 1)

    def relay_all(hop):
        def body(index, carry):
            relay(index, hop)
            return carry

        lax.fori_loop(0, pairs, body, 0)

    hop = 1
    for index in range(2, total):
        pump(index)
        if hop <= last:
            relay_all(hop)
            hop += 1
        if index == 2:
            decode()
        if index == 3:
            decode_on()
    while hop <= last:
        relay_all(hop)
        hop += 1
    gathers[total - 1].relay_far()
    for offset in range(1, head_count):
        dec_spread(offset).wait()
    for gather in gathers:
        gather.collect()
    for gather in gathers:
        gather.drain()

    def drain(index, carry):
        for offset in range(1, tok_count):
            back(index, offset).wait_send()
        for origin in range(head_count):
            for way in range(2):
                passed = origin <= head if way == 0 else origin >= head

                @pl.when(jnp.logical_and(passed, goes[way]))
                def _():
                    pass_on(way, origin, index).wait_send()

        return carry

    lax.fori_loop(0, pairs, drain, 0)


def attend_layer(qkv, offset, cache, lengths, dec_parts, dec_cache, w_gu, w_out):
    tok_count = lax.axis_size("tok")
    head_count = lax.axis_size("head")
    _, span, group = qkv.shape
    length = cache.shape[2]
    pair = 2 * HD
    pairs = group // pair
    cosine, sine = rope_tables(offset + jnp.arange(span, dtype=jnp.int32), pair)
    any_space = pl.BlockSpec(memory_space=pl.ANY)
    in_vmem = pl.BlockSpec(memory_space=pltpu.VMEM)
    smem = pl.BlockSpec(memory_space=pltpu.SMEM)
    slots = PlaneGather.slots()
    total = GU_CHUNKS + ROW_CHUNKS
    gather_sems = pltpu.SemaphoreType.DMA((total, slots))
    back_sems = pltpu.SemaphoreType.DMA((pairs, tok_count))
    pass_sems = pltpu.SemaphoreType.DMA((2, head_count, pairs))
    return pl.pallas_call(
        attend_kernel,
        out_shape=(
            jax.ShapeDtypeStruct((tok_count * DEC_PAD, head_count * group), jnp.bfloat16),
            jax.ShapeDtypeStruct((span, head_count * group), jnp.bfloat16),
            jax.ShapeDtypeStruct((w_gu.shape[0], tok_count * w_gu.shape[1]), jnp.bfloat16),
            jax.ShapeDtypeStruct((tok_count * w_out.shape[0], w_out.shape[1]), jnp.bfloat16),
        ),
        in_specs=[smem] + [in_vmem] * 4 + [smem] + [in_vmem] * 3 + [any_space] + [in_vmem] * 2,
        out_specs=(in_vmem,) + (any_space,) * 3,
        scratch_shapes=[
            pltpu.VMEM((2, span, pair), jnp.bfloat16),
            pltpu.VMEM((span, pair), jnp.bfloat16),
            pltpu.VMEM((2, span, pair), jnp.bfloat16),
            pltpu.VMEM((2, length, pair), jnp.bfloat16),
            pltpu.VMEM((pairs, span, pair), jnp.bfloat16),
            gather_sems,
            gather_sems,
            pltpu.SemaphoreType.DMA((total,)),
            back_sems,
            back_sems,
            pltpu.SemaphoreType.DMA((pairs,)),
            pass_sems,
            pass_sems,
            pltpu.SemaphoreType.DMA((tok_count,)),
            pltpu.SemaphoreType.DMA((tok_count,)),
            pltpu.SemaphoreType.DMA,
            pltpu.SemaphoreType.DMA((head_count,)),
            pltpu.SemaphoreType.DMA((head_count,)),
            pltpu.VMEM((DEC_PAD, group), jnp.bfloat16),
            pltpu.VMEM(dec_cache.shape, jnp.bfloat16),
            pltpu.SemaphoreType.DMA((dec_cache.shape[0],)),
        ],
        compiler_params=pltpu.CompilerParams(
            collective_id=2, has_side_effects=True, vmem_limit_bytes=56 * 1024 * 1024
        ),
        cost_estimate=pl.CostEstimate(
            flops=16 * span * 3 * span * group,
            bytes_accessed=4 * length * group + 8 * span * group,
            transcendentals=span * 3 * span * group // HD,
        ),
        name="attend_layer",
    )(offset[None], qkv, cosine, sine, cache, lengths, *dec_parts, dec_cache, w_gu, w_out)


def unpermute_kernel(order_ref, source_ref, target_ref, held, in_sem, out_sem):
    count = source_ref.shape[0]
    ins = [
        pltpu.make_async_copy(source_ref.at[index], held.at[index], in_sem.at[index])
        for index in range(count)
    ]
    outs = [
        pltpu.make_async_copy(
            held.at[index], target_ref.at[order_ref[index]], out_sem.at[index]
        )
        for index in range(count)
    ]
    for copy in ins:
        copy.start()
    for index in range(count):
        ins[index].wait()
        outs[index].start()
    for copy in outs:
        copy.wait()


def unpermuted(blocks, order):
    any_space = pl.BlockSpec(memory_space=pl.ANY)
    return pl.pallas_call(
        unpermute_kernel,
        out_shape=jax.ShapeDtypeStruct(blocks.shape, blocks.dtype),
        in_specs=[pl.BlockSpec(memory_space=pltpu.SMEM), any_space],
        out_specs=any_space,
        scratch_shapes=[
            pltpu.VMEM(blocks.shape, blocks.dtype),
            pltpu.SemaphoreType.DMA((blocks.shape[0],)),
            pltpu.SemaphoreType.DMA((blocks.shape[0],)),
        ],
        compiler_params=pltpu.CompilerParams(vmem_limit_bytes=58 * 1024 * 1024),
        name="unpermute",
    )(order, blocks)


def mlp_kernel(
    head_count,
    order_ref,
    att_ref,
    rows_ref,
    dec_att_ref,
    dec_rows_ref,
    gain_ref,
    w_out_ref,
    w_gu_ref,
    w_down_ref,
    out_ref,
    dec_out_ref,
    hidden,
    w_out_v,
    w_gu_v,
    w_down_v,
    resid,
    mlp_in,
    wide_v,
    slots,
    dec_slots,
    load_sem,
    rs_send,
    rs_recv,
    ag_send,
    ag_recv,
    keep_sem,
    dec_send,
    dec_recv,
    g_send,
    g_recv,
    g_local,
):
    last = head_count - 1
    me = lax.axis_index("head")
    span, width = att_ref.shape
    half = span // 2
    count = half // CHUNK
    units = w_gu_ref.shape[0] // 2
    pieces, piece = rows_ref.shape[:2]
    dec = dec_att_ref.shape[0]
    group = (wide_v.shape[0] - dec) // 2

    loads = [
        pltpu.make_async_copy(att_ref, hidden.at[pl.ds(0, span), pl.ds(0, width)], load_sem.at[0]),
        pltpu.make_async_copy(w_out_ref, w_out_v, load_sem.at[1]),
        pltpu.make_async_copy(w_gu_ref, w_gu_v, load_sem.at[2]),
    ]
    for copy in loads:
        copy.start()
    extent = w_down_ref.shape[0] // ROW_CHUNKS
    gathers = [
        PlaneGather(
            w_down_ref, w_down_v, 0, chunk * extent, extent, g_send.at[chunk], g_recv.at[chunk], g_local.at[chunk]
        )
        for chunk in range(ROW_CHUNKS)
    ]
    greet(("tok", "head"))
    for gather in gathers:
        gather.start()
    hidden[span:, :width] = dec_att_ref[...]

    def begin_rows(index, carry):
        at = pl.ds(pl.multiple_of(index * piece, piece), piece)
        resid[at, :] = rows_ref[order_ref[index]].astype(jnp.float32)
        return carry

    lax.fori_loop(0, pieces, begin_rows, 0)
    resid[span:, :] = dec_rows_ref[...].astype(jnp.float32)
    loads[0].wait()
    loads[1].wait()
    out_tile, out_tiles = tiles_of(width)
    unit_tile, unit_tiles = tiles_of(units)

    def rows_in(begin, block):
        at = slice(begin, begin + block)

        def project(tile, squares):
            columns = pl.ds(pl.multiple_of(tile * out_tile, out_tile), out_tile)
            value = resid[at, columns] + nt_dot(hidden[at, :width], w_out_v[columns, :])
            resid[at, columns] = value
            return squares + jnp.sum(value * value, axis=-1, keepdims=True)

        squares = lax.fori_loop(0, out_tiles, project, jnp.zeros((block, 1), jnp.float32))
        factor = lax.rsqrt(squares / width + norm_eps)
        mlp_in[:block, :] = (resid[at, :] * factor * gain_ref[...]).astype(jnp.bfloat16)
        if begin == 0:
            loads[2].wait()

        def gate_up(tile, carry):
            begin = pl.multiple_of(tile * unit_tile, unit_tile)
            gate = 0.5 * nt_dot(mlp_in[:block, :], w_gu_v[pl.ds(begin, unit_tile), :])
            up = nt_dot(mlp_in[:block, :], w_gu_v[pl.ds(units + begin, unit_tile), :])
            hidden[at, pl.ds(begin, unit_tile)] = (
                (gate + gate * jnp.tanh(gate)) * up
            ).astype(jnp.bfloat16)
            return carry

        lax.fori_loop(0, unit_tiles, gate_up, 0)

    rows_in(0, half)
    for gather in gathers:
        gather.relay()
    rows_in(half, half + dec)
    for gather in gathers:
        gather.relay_far()
    for gather in gathers:
        gather.collect()

    spot = lax.broadcasted_iota(jnp.int32, (2 * group, 1), 0)
    owner = jnp.where(spot < group, 0, last)
    owned = jnp.where(owner == me, 1.0, 0.0).astype(jnp.float32)
    wide_v[2 * group :, :] = hidden[span:, :units]

    def dec_copy(offset):
        return pltpu.make_async_remote_copy(
            src_ref=dec_slots.at[me],
            dst_ref=dec_slots.at[me],
            send_sem=dec_send.at[offset],
            recv_sem=dec_recv.at[offset],
            device_id={"head": lax.rem(me + offset, head_count)},
            device_id_type=MESH,
        )

    def compute(index):
        spots = [
            pl.ds(pl.multiple_of(side * half + index * group, group), group) for side in range(2)
        ]
        for side in range(2):
            wide_v[side * group : (side + 1) * group, :] = hidden[spots[side], :units]

        def down(tile, carry):
            columns = pl.ds(pl.multiple_of(tile * out_tile, out_tile), out_tile)
            value = nt_dot(wide_v[...], w_down_v[columns, :])
            for side in range(2):
                mine = slice(side * group, (side + 1) * group)
                resid[spots[side], columns] = (
                    value[mine] + resid[spots[side], columns] * owned[mine]
                )

            @pl.when(index == 0)
            def _():
                dec_slots[me, :, columns] = value[2 * group :].astype(jnp.bfloat16)

            return carry

        lax.fori_loop(0, out_tiles, down, 0)

        @pl.when(index == 0)
        def _():
            for offset in range(1, head_count):
                dec_copy(offset).start()

    def out_rows(side, index):
        return out_ref.at[pl.ds(pl.multiple_of(side * half + index * CHUNK, CHUNK), CHUNK)]

    def next_of(side):
        return jnp.maximum(me - 1, 0) if side == 0 else jnp.minimum(me + 1, last)

    def before_of(side):
        return next_of(1 - side)

    def sum_copy(side, index):
        return pltpu.make_async_remote_copy(
            src_ref=slots.at[side, index],
            dst_ref=slots.at[side, index],
            send_sem=rs_send.at[side, index],
            recv_sem=rs_recv.at[side, index],
            device_id={"head": next_of(side)},
            device_id_type=MESH,
        )

    def final_copy(side, index, source):
        return pltpu.make_async_remote_copy(
            src_ref=source,
            dst_ref=out_rows(side, index),
            send_sem=ag_send.at[side, index],
            recv_sem=ag_recv.at[side, index],
            device_id={"head": before_of(side)},
            device_id_type=MESH,
        )

    def keep_copy(side, index):
        return pltpu.make_async_copy(
            slots.at[side, index], out_rows(side, index), keep_sem.at[side, index]
        )

    hops = [last - me, me]
    to_end = [me, last - me]

    def combine(side, index):
        mine = pl.ds(pl.multiple_of(side * half + index * CHUNK, CHUNK), CHUNK)

        @pl.when(hops[side] == 0)
        def _():
            slots[side, index] = resid[mine, :].astype(jnp.bfloat16)

        @pl.when(hops[side] > 0)
        def _():
            sum_copy(side, index).wait_recv()
            slots[side, index] = (
                resid[mine, :] + slots[side, index].astype(jnp.float32)
            ).astype(jnp.bfloat16)

        @pl.when(to_end[side] > 0)
        def _():
            sum_copy(side, index).start()

        @pl.when(to_end[side] == 0)
        def _():
            final_copy(side, index, slots.at[side, index]).start()
            keep_copy(side, index).start()

    def forward(side, index):
        final_copy(side, index, out_rows(side, index)).wait_recv()

        @pl.when(hops[side] > 0)
        def _():
            final_copy(side, index, out_rows(side, index)).start()

    every = group // CHUNK

    def tick(step, carry):
        @pl.when(jnp.logical_and(step < count, lax.rem(step, every) == 0))
        def _():
            compute(step // every)

        for side in range(2):
            index = step - hops[side]

            @pl.when(jnp.logical_and(index >= 0, index < count))
            def _():
                combine(side, index)

        for side in range(2):
            spread = step - last - to_end[side]

            @pl.when(
                jnp.logical_and(
                    to_end[side] > 0, jnp.logical_and(spread >= 0, spread < count)
                )
            )
            def _():
                forward(side, spread)

        return carry

    lax.fori_loop(0, count + 2 * last, tick, 0)

    for offset in range(1, head_count):
        dec_copy(offset).wait()
    total = resid[span:, :]
    for index in range(head_count):
        total = total + dec_slots[index].astype(jnp.float32)
    dec_out_ref[...] = total.astype(jnp.bfloat16)

    for gather in gathers:
        gather.drain()

    def drain(index, carry):
        for side in range(2):

            @pl.when(to_end[side] > 0)
            def _():
                sum_copy(side, index).wait_send()

            @pl.when(to_end[side] == 0)
            def _():
                keep_copy(side, index).wait()

            @pl.when(hops[side] > 0)
            def _():
                final_copy(side, index, out_rows(side, index)).wait_send()

        return carry

    lax.fori_loop(0, count, drain, 0)


def mlp_layer(pre_order, att, rows, dec_att, dec_rows, gain, w_out, w_gu, w_down):
    head_count = lax.axis_size("head")
    tok_count = lax.axis_size("tok")
    span, width = att.shape
    units = w_gu.shape[0] // 2
    count = span // 2 // CHUNK
    dec = dec_att.shape[0]
    group = min(GROUP_ROWS, span // 2)
    any_space = pl.BlockSpec(memory_space=pl.ANY)
    in_vmem = pl.BlockSpec(memory_space=pltpu.VMEM)
    both = pltpu.SemaphoreType.DMA((2, count))
    gather_sems = pltpu.SemaphoreType.DMA((ROW_CHUNKS, PlaneGather.slots()))
    return pl.pallas_call(
        functools.partial(mlp_kernel, head_count),
        out_shape=(
            jax.ShapeDtypeStruct((span, width), jnp.bfloat16),
            jax.ShapeDtypeStruct((dec, width), jnp.bfloat16),
        ),
        in_specs=[pl.BlockSpec(memory_space=pltpu.SMEM), any_space]
        + [in_vmem] * 4
        + [any_space] * 3,
        out_specs=(any_space, in_vmem),
        scratch_shapes=[
            pltpu.VMEM((span + dec, max(width, units)), jnp.bfloat16),
            pltpu.VMEM(w_out.shape, jnp.bfloat16),
            pltpu.VMEM(w_gu.shape, jnp.bfloat16),
            pltpu.VMEM((tok_count * w_down.shape[0], units), jnp.bfloat16),
            pltpu.VMEM((span + dec, width), jnp.float32),
            pltpu.VMEM((span // 2 + dec, width), jnp.bfloat16),
            pltpu.VMEM((2 * group + dec, units), jnp.bfloat16),
            pltpu.VMEM((2, count, CHUNK, width), jnp.bfloat16),
            pltpu.VMEM((head_count, dec, width), jnp.bfloat16),
            pltpu.SemaphoreType.DMA((3,)),
            both,
            both,
            both,
            both,
            both,
            pltpu.SemaphoreType.DMA((head_count,)),
            pltpu.SemaphoreType.DMA((head_count,)),
            gather_sems,
            gather_sems,
            pltpu.SemaphoreType.DMA((ROW_CHUNKS,)),
        ],
        compiler_params=pltpu.CompilerParams(
            collective_id=3, has_side_effects=True, vmem_limit_bytes=60 * 1024 * 1024
        ),
        cost_estimate=pl.CostEstimate(
            flops=2 * span * width * (width + 3 * units),
            bytes_accessed=2 * (4 * span * width + w_out.size + w_gu.size + w_down.size),
            transcendentals=span * units,
        ),
        name="mlp_layer",
    )(pre_order, att, rows, dec_att, dec_rows, gain[None], w_out, w_gu, w_down)


def picked_rows(rows, order):
    count = rows.shape[0]
    picker = order[:, None] == jnp.arange(count, dtype=jnp.int32)[None, :]
    return jnp.dot(
        picker.astype(jnp.bfloat16), rows, preferred_element_type=jnp.float32
    ).astype(jnp.bfloat16)


def inverse_of(order):
    spots = jnp.arange(order.shape[0], dtype=jnp.int32)
    return jnp.sum(jnp.where(order[None, :] == spots[:, None], spots[None, :], 0), axis=1)


def on_device(
    pre_tokens,
    dec_tokens,
    attn_gain,
    mlp_gain,
    w_qkv,
    w_out,
    w_gate_up,
    w_down,
    pre_cache,
    dec_cache,
    pre_order,
    dec_order,
    pre_offsets,
    dec_lengths,
):
    tok_count = lax.axis_size("tok")
    tok_index = lax.axis_index("tok")
    head_count = lax.axis_size("head")
    span_rows, width = pre_tokens.shape
    piece_len = span_rows // tok_count
    dec_local = dec_tokens.shape[0]
    group_width, depth = w_qkv.shape[1:]
    units = w_gate_up.shape[1]

    blocks = pre_tokens.reshape(tok_count, piece_len, width)
    packed = dec_tokens.reshape(dec_local, width // depth, depth)
    packed = jnp.transpose(packed, (1, 0, 2)).reshape(dec_local * width // depth, depth)
    qkv, dec_qkv, dec_rows = project_layer(
        pre_order, blocks, packed, attn_gain, w_qkv.reshape(3 * group_width, depth)
    )
    w_out_rows = lax.all_gather(w_out, "head", axis=1, tiled=True)

    own_slots = lax.dynamic_slice_in_dim(dec_order, tok_index * dec_local, dec_local)
    dec_mine = jnp.stack([picked_rows(dec_qkv[which], own_slots) for which in range(3)])

    dec_all, attended, gate_up_full, out_full = attend_layer(
        qkv,
        pre_offsets[0],
        pre_cache,
        dec_lengths,
        decode_inputs(dec_mine, dec_lengths),
        dec_cache,
        w_gate_up.reshape(2 * units, depth),
        w_out_rows,
    )
    dec_spots = inverse_of(dec_order)
    dec_spots = dec_spots // dec_local * DEC_PAD + dec_spots % dec_local
    dec_all = picked_rows(dec_all, dec_spots)
    pre_out, dec_out = mlp_layer(
        pre_order,
        attended,
        blocks,
        dec_all,
        dec_rows,
        mlp_gain,
        out_full,
        gate_up_full,
        w_down,
    )
    pre_out = unpermuted(pre_out.reshape(tok_count, piece_len, width), pre_order)
    dec_out = lax.dynamic_slice_in_dim(dec_out, tok_index * dec_local, dec_local)
    return (pre_out.reshape(span_rows, width), dec_out)


def solution(mesh):
    placed = (
        P("tok", None),
        P("tok", None),
        P(),
        P(),
        P(None, "head", "tok"),
        P("tok", "head"),
        P(None, "head", "tok"),
        P("tok", "head"),
        P("tok", None, None, "head"),
        P("tok", None, None, "head"),
        P(),
        P(),
        P("tok"),
        P("tok"),
    )
    return jax.shard_map(
        on_device,
        mesh=mesh,
        in_specs=placed,
        out_specs=(P("tok", None), P("tok", None)),
        check_vma=False,
    )
```

```python
import functools

import jax
import jax.numpy as jnp
from jax import lax
from jax.experimental import pallas as pl
from jax.experimental.pallas import tpu as pltpu
from jax.sharding import PartitionSpec as P

HD = 64
Q_ROWS = 512
K_ROWS = 512
DEC_ROWS = 1024
DEC_PAD = 16


rope_base = 130000.0
norm_eps = 1e-05
masked_score = -1e30


def rotate(values, positions):
    width = values.shape[-1]
    half = width // 2
    freqs = rope_base ** (-(jnp.arange(half, dtype=jnp.float32) * 2.0 / width))
    angles = positions.astype(jnp.float32)[:, None] * freqs[None, :]
    cosine = jnp.cos(angles)[:, None, :]
    sine = jnp.sin(angles)[:, None, :]
    first = values[..., :half]
    second = values[..., half:]
    return jnp.concatenate(
        [first * cosine - second * sine, second * cosine + first * sine], axis=-1
    )


def rope_tables(positions, width):
    half = HD // 2
    freqs = rope_base ** (-(jnp.arange(half, dtype=jnp.float32) * 2.0 / HD))
    angles = positions.astype(jnp.float32)[:, None] * freqs[None, :]
    cosine = jnp.cos(angles)
    sine = jnp.sin(angles)
    copies = width // HD
    return (
        jnp.tile(jnp.concatenate([cosine, cosine], axis=1), (1, copies)),
        jnp.tile(jnp.concatenate([-sine, sine], axis=1), (1, copies)),
    )


def swap_halves(values):
    half = HD // 2
    width = values.shape[-1]
    lane = lax.broadcasted_iota(jnp.int32, values.shape, values.ndim - 1)
    axis = values.ndim - 1
    return jnp.where(
        lane % HD < half,
        pltpu.roll(values, width - half, axis),
        pltpu.roll(values, half, axis),
    )


def decode_inputs(qkv, lengths):
    _, count, width = qkv.shape
    heads = width // HD
    split = qkv.reshape(3, count, heads, HD)
    q_rot = rotate(split[0].astype(jnp.float32), lengths).astype(jnp.bfloat16)
    k_rot = rotate(split[1].astype(jnp.float32), lengths).astype(jnp.bfloat16)
    q_rot = q_rot * jnp.bfloat16(HD**-0.5)
    spread = jnp.where(
        jnp.eye(heads, dtype=jnp.bool_)[None, :, :, None], q_rot[:, None], jnp.bfloat16(0)
    ).reshape(count, heads, width)
    return spread, k_rot.reshape(count, 1, width), qkv[2].reshape(count, 1, width)


def decode_one(request, limit, q_ref, k_ref, v_ref, cache_ref):
    heads, width = q_ref.shape[1:]
    length = cache_ref.shape[2]
    rows = min(DEC_ROWS, length)
    query = q_ref[request]
    own = query.astype(jnp.float32) * k_ref[request].astype(jnp.float32)

    def fold(index, state):
        top, total, mixed = state
        begin = pl.multiple_of(index * rows, rows)
        scores = nt_dot(query, cache_ref[request, 0, pl.ds(begin, rows), :])
        spot = begin + lax.broadcasted_iota(jnp.int32, (1, rows), 1)
        scores = jnp.where(spot < limit, scores, masked_score)
        new_top = jnp.maximum(top, jnp.max(scores, axis=-1, keepdims=True))
        weights = jnp.exp(scores - new_top)
        factor = jnp.exp(top - new_top)
        values = cache_ref[request, 1, pl.ds(begin, rows), :]
        return (
            new_top,
            total * factor + jnp.sum(weights, axis=-1, keepdims=True),
            mixed * factor
            + jnp.dot(weights.astype(jnp.bfloat16), values, preferred_element_type=jnp.float32),
        )

    state = (
        jnp.sum(own, axis=-1, keepdims=True),
        jnp.ones((heads, 1), jnp.float32),
        jnp.broadcast_to(v_ref[request].astype(jnp.float32), (heads, width)),
    )
    _, total, mixed = lax.fori_loop(0, length // rows, fold, state)
    shape = (heads, width)
    mine = lax.broadcasted_iota(jnp.int32, shape, 1) // HD == lax.broadcasted_iota(
        jnp.int32, shape, 0
    )
    return jnp.sum(jnp.where(mine, mixed / total, 0.0), axis=0, keepdims=True)


MESH = pl.DeviceIdType.MESH
CHUNK = 32
LAG = 2
GROUP_ROWS = 128
TILE = 512


def nt_dot(rows, weights):
    return lax.dot_general(
        rows, weights, (((1,), (1,)), ((), ())), preferred_element_type=jnp.float32
    )


def tiles_of(extent):
    tile = min(TILE, extent)
    return tile, extent // tile


class PlaneGather:
    SLOTS = 9

    def __init__(self, source, target, axis, begin, extent, send, recv, local):
        self.source, self.target, self.axis = source, target, axis
        self.begin, self.extent = begin, extent
        self.send, self.recv, self.local = send, recv, local
        self.count = lax.axis_size("tok")
        self.me = lax.axis_index("tok")
        me = self.me
        self.cube = self.count == 8
        if self.cube:
            core = lax.rem(me, 2)
            column = lax.rem(me // 2, 2)
            line = me // 4
            turn = 1 - 2 * core
            self.twin = me + turn
            self.x = me + 2 - 4 * column
            self.y = me + 4 - 8 * line
            far = self.x + self.y - me
            whole_part = (0, 2)
            self.table = [
                (me, whole_part, self.twin, self.twin),
                (me, whole_part, self.x, self.x),
                (me, whole_part, self.y, self.y),
                (self.x, whole_part, self.twin, self.x + turn),
                (self.y, whole_part, self.twin, self.y + turn),
                (self.x, (0, 1), self.y, far),
                (self.y, (1, 1), self.x, far),
                (far, (0, 1), self.twin, far + turn),
                (far, (1, 1), self.twin, far + turn),
            ]
        else:
            self.table = [
                (
                    me,
                    (0, 2),
                    lax.rem(me + offset, self.count),
                    lax.rem(me + self.count - offset, self.count),
                )
                for offset in range(1, self.count)
            ]

    @staticmethod
    def slots():
        count = lax.axis_size("tok")
        return PlaneGather.SLOTS if count == 8 else count - 1

    def place(self, tok, part):
        half = self.extent // 2
        begin, extent = self.begin + part[0] * half, part[1] * half
        rows, columns = self.source.shape
        if self.axis == 0:
            return self.target.at[pl.ds(pl.multiple_of(tok * rows + begin, 16), extent), :]
        return self.target.at[
            pl.ds(begin, extent), pl.ds(pl.multiple_of(tok * columns, columns), columns)
        ]

    def own(self):
        return self.source.at[pl.ds(self.begin, self.extent), :]

    def copy(self, slot):
        what, part, dest, _ = self.table[slot]
        source = self.own() if slot < 3 or not self.cube else self.place(what, part)
        return pltpu.make_async_remote_copy(
            src_ref=source,
            dst_ref=self.place(what, part),
            send_sem=self.send.at[slot],
            recv_sem=self.recv.at[slot],
            device_id={"tok": dest},
            device_id_type=MESH,
        )

    def arrived(self, slot):
        _, part, dest, comes = self.table[slot]
        place = self.place(comes, part)
        pltpu.make_async_remote_copy(
            src_ref=place,
            dst_ref=place,
            send_sem=self.send.at[slot],
            recv_sem=self.recv.at[slot],
            device_id={"tok": dest},
            device_id_type=MESH,
        ).wait_recv()

    def keep(self):
        return pltpu.make_async_copy(self.own(), self.place(self.me, (0, 2)), self.local)

    def start(self):
        first = (1, 2, 0) if self.cube else range(len(self.table))
        for slot in first:
            self.copy(slot).start()
        self.keep().start()

    def relay(self):
        if self.cube:
            self.arrived(1)
            self.copy(5).start()
            self.copy(3).start()
            self.arrived(2)
            self.copy(6).start()
            self.copy(4).start()

    def relay_far(self):
        if self.cube:
            self.arrived(5)
            self.copy(7).start()
            self.arrived(6)
            self.copy(8).start()

    def collect(self):
        for slot in (0, 3, 4, 7, 8) if self.cube else range(len(self.table)):
            self.arrived(slot)
        self.keep().wait()

    def drain(self):
        for slot in range(len(self.table)):
            self.copy(slot).wait_send()


def greet(axes):
    barrier = pltpu.get_barrier_semaphore()
    total = 0
    for axis in axes:
        count = lax.axis_size(axis)
        me = lax.axis_index(axis)
        for offset in range(1, count):
            pl.semaphore_signal(
                barrier,
                inc=1,
                device_id={axis: lax.rem(me + offset, count)},
                device_id_type=MESH,
            )
        total += count - 1
    pl.semaphore_wait(barrier, total)


def project_kernel(
    order_ref,
    x_ref,
    dec_ref,
    gain_ref,
    w_ref,
    out_ref,
    dec_out_ref,
    dec_rows_ref,
    w_v,
    dec_v,
    normed,
    dec_normed,
    staged,
    w_send,
    w_recv,
    w_local,
    send,
    recv,
    local,
    dec_send,
    dec_recv,
    dec_local,
):
    tok_count, piece, width = x_ref.shape
    me = lax.axis_index("tok")
    group = w_ref.shape[0] // 3
    columns = w_ref.shape[1]
    packed = dec_ref.shape[0]
    dec_each = packed * columns // width
    dec_total = tok_count * dec_each
    gathers = [
        PlaneGather(
            w_ref, w_v, 1, kind * group, group, w_send.at[kind], w_recv.at[kind], w_local.at[kind]
        )
        for kind in range(3)
    ]

    def dec_copy(offset):
        return pltpu.make_async_remote_copy(
            src_ref=dec_ref,
            dst_ref=dec_v.at[me],
            send_sem=dec_send.at[offset],
            recv_sem=dec_recv.at[offset],
            device_id={"tok": lax.rem(me + offset, tok_count)},
            device_id_type=MESH,
        )

    dec_keep = pltpu.make_async_copy(dec_ref, dec_v.at[me], dec_local)
    dec_keep.start()
    greet(("tok",))
    for gather in gathers:
        gather.start()
    for offset in range(1, tok_count):
        dec_copy(offset).start()

    def norm(rows):
        squares = jnp.mean(rows * rows, axis=-1, keepdims=True)
        return (rows * lax.rsqrt(squares + norm_eps) * gain_ref[...]).astype(jnp.bfloat16)

    def norm_piece(index, carry):
        rows = x_ref[order_ref[index]].astype(jnp.float32)
        normed[pl.ds(pl.multiple_of(index * piece, piece), piece), :] = norm(rows)
        return carry

    lax.fori_loop(0, tok_count, norm_piece, 0)
    gathers[0].relay()
    dec_keep.wait()
    for offset in range(1, tok_count):
        dec_copy(offset).wait()
    gathers[1].relay()
    gathers[0].relay_far()
    flat = dec_v[...].reshape(tok_count * packed, columns)
    shape = (dec_total, tok_count * packed)
    line = lax.broadcasted_iota(jnp.int32, shape, 0)
    spot = lax.broadcasted_iota(jnp.int32, shape, 1)
    for block in range(width // columns):
        wanted = (line // dec_each) * packed + block * dec_each + line % dec_each
        picker = jnp.where(spot == wanted, 1.0, 0.0).astype(jnp.bfloat16)
        dec_rows_ref[:, block * columns : (block + 1) * columns] = jnp.dot(
            picker, flat, preferred_element_type=jnp.float32
        ).astype(jnp.bfloat16)
    dec_normed[...] = norm(dec_rows_ref[...].astype(jnp.float32))

    rows_each = min(256, tok_count * piece)

    def give(kind, offset):
        dest = lax.rem(me + offset, tok_count)
        return pltpu.make_async_remote_copy(
            src_ref=staged.at[kind, pl.ds(pl.multiple_of(dest * piece, piece), piece), :],
            dst_ref=out_ref.at[kind, pl.ds(pl.multiple_of(me * piece, piece), piece), :],
            send_sem=send.at[kind, offset],
            recv_sem=recv.at[kind, offset],
            device_id={"tok": dest},
            device_id_type=MESH,
        )

    def keep(kind):
        mine = pl.ds(pl.multiple_of(me * piece, piece), piece)
        return pltpu.make_async_copy(
            staged.at[kind, mine, :], out_ref.at[kind, mine, :], local.at[kind]
        )

    for kind in range(3):
        if kind + 2 < 3:
            gathers[kind + 2].relay()
        if kind + 1 < 3:
            gathers[kind + 1].relay_far()
        gathers[kind].collect()
        weights = w_v.at[pl.ds(kind * group, group), :]

        def multiply(index, carry):
            begin = pl.multiple_of(index * rows_each, rows_each)
            staged[kind, pl.ds(begin, rows_each), :] = nt_dot(
                normed[pl.ds(begin, rows_each), :], weights[...]
            ).astype(jnp.bfloat16)
            return carry

        lax.fori_loop(0, tok_count * piece // rows_each, multiply, 0)
        for offset in range(1, tok_count):
            give(kind, offset).start()
        keep(kind).start()
        dec_out_ref[kind] = nt_dot(dec_normed[...], weights[...]).astype(jnp.bfloat16)

    for gather in gathers:
        gather.drain()
    for kind in range(3):
        for offset in range(1, tok_count):
            give(kind, offset).wait()
        keep(kind).wait()


def project_layer(pre_order, rows, dec_packed, gain, w_qkv):
    tok_count, piece, width = rows.shape
    group = w_qkv.shape[0] // 3
    columns = w_qkv.shape[1]
    packed = dec_packed.shape[0]
    dec_total = tok_count * packed * columns // width
    span = tok_count * piece
    any_space = pl.BlockSpec(memory_space=pl.ANY)
    in_vmem = pl.BlockSpec(memory_space=pltpu.VMEM)
    slots = PlaneGather.slots()
    return pl.pallas_call(
        project_kernel,
        out_shape=(
            jax.ShapeDtypeStruct((3, span, group), jnp.bfloat16),
            jax.ShapeDtypeStruct((3, dec_total, group), jnp.bfloat16),
            jax.ShapeDtypeStruct((dec_total, width), jnp.bfloat16),
        ),
        in_specs=[
            pl.BlockSpec(memory_space=pltpu.SMEM),
            in_vmem,
            any_space,
            in_vmem,
            any_space,
        ],
        out_specs=(any_space, in_vmem, in_vmem),
        scratch_shapes=[
            pltpu.VMEM((3 * group, width), jnp.bfloat16),
            pltpu.VMEM((tok_count, packed, columns), jnp.bfloat16),
            pltpu.VMEM((span, width), jnp.bfloat16),
            pltpu.VMEM((dec_total, width), jnp.bfloat16),
            pltpu.VMEM((3, span, group), jnp.bfloat16),
            pltpu.SemaphoreType.DMA((3, slots)),
            pltpu.SemaphoreType.DMA((3, slots)),
            pltpu.SemaphoreType.DMA((3,)),
            pltpu.SemaphoreType.DMA((3, tok_count)),
            pltpu.SemaphoreType.DMA((3, tok_count)),
            pltpu.SemaphoreType.DMA((3,)),
            pltpu.SemaphoreType.DMA((tok_count,)),
            pltpu.SemaphoreType.DMA((tok_count,)),
            pltpu.SemaphoreType.DMA,
        ],
        compiler_params=pltpu.CompilerParams(
            collective_id=1, has_side_effects=True, vmem_limit_bytes=48 * 1024 * 1024
        ),
        cost_estimate=pl.CostEstimate(
            flops=6 * span * width * group,
            bytes_accessed=2 * (span * width + 6 * span * group + 3 * group * width),
            transcendentals=span,
        ),
        name="project_layer",
    )(pre_order, rows, dec_packed, gain[None], w_qkv)


def attend_pair(limit, q_ref, k_ref, v_ref, cos_ref, sin_ref, cache_ref, pair_at, q_rot, k_rot, v_ext, c_ext, out_ref):
    span = q_rot.shape[1]
    length = c_ext.shape[1]
    pair = q_rot.shape[2]
    cosine = cos_ref[...]
    sine = sin_ref[...]
    lane = lax.broadcasted_iota(jnp.int32, (1, pair), 1)
    halves = (lane < HD, lane >= HD)

    key = k_ref[:, pair_at].astype(jnp.float32)
    k_rot[...] = (key * cosine + swap_halves(key) * sine).astype(jnp.bfloat16)
    query = q_ref[:, pair_at].astype(jnp.float32)
    query = (query * cosine + swap_halves(query) * sine).astype(jnp.bfloat16)
    query = query * jnp.bfloat16(HD**-0.5)
    one = jnp.ones((), jnp.bfloat16)
    zero = jnp.zeros((), jnp.bfloat16)
    for side in range(2):
        q_rot[side] = jnp.where(halves[side], query, zero)
        v_ext[side] = jnp.where(halves[side], v_ref[:, pair_at], one)
        c_ext[side] = jnp.where(halves[side], cache_ref[1, :, pair_at], one)

    def fold(state, scores, values):
        top, mixed = state
        new_top = jnp.maximum(top, jnp.max(scores, axis=-1, keepdims=True))
        weights = jnp.exp(scores - new_top).astype(jnp.bfloat16)
        factor = jnp.exp(top - new_top)
        return new_top, mixed * factor + jnp.dot(
            weights, values, preferred_element_type=jnp.float32
        )

    for block in range(span // Q_ROWS):
        start = block * Q_ROWS
        rows = [q_rot[side, start : start + Q_ROWS, :] for side in range(2)]
        keys = k_rot[start : start + Q_ROWS, :]
        shape = (Q_ROWS, Q_ROWS)
        seen = lax.broadcasted_iota(jnp.int32, shape, 1) <= lax.broadcasted_iota(
            jnp.int32, shape, 0
        )
        states = []
        for side in range(2):
            scores = jnp.where(seen, nt_dot(rows[side], keys), masked_score)
            top = jnp.max(scores, axis=-1, keepdims=True)
            weights = jnp.exp(scores - top).astype(jnp.bfloat16)
            mixed = jnp.dot(
                weights,
                v_ext[side, start : start + Q_ROWS, :],
                preferred_element_type=jnp.float32,
            )
            states.append((top, mixed))
        for earlier in range(block):
            begin = earlier * Q_ROWS
            keys = k_rot[begin : begin + Q_ROWS, :]
            for side in range(2):
                states[side] = fold(
                    states[side],
                    nt_dot(rows[side], keys),
                    v_ext[side, begin : begin + Q_ROWS, :],
                )

        def cached(index, state):
            begin = pl.multiple_of(index * K_ROWS, K_ROWS)
            keys_now = cache_ref[0, pl.ds(begin, K_ROWS), pair_at]
            spot = begin + lax.broadcasted_iota(jnp.int32, (1, K_ROWS), 1)
            live = spot < limit
            result = []
            for side in range(2):
                scores = jnp.where(live, nt_dot(rows[side], keys_now), masked_score)
                result.append(
                    fold(state[side], scores, c_ext[side, pl.ds(begin, K_ROWS), :])
                )
            return tuple(result)

        states = lax.fori_loop(0, length // K_ROWS, cached, tuple(states))
        parts = []
        for side in range(2):
            mixed = states[side][1]
            total = pltpu.roll(mixed, HD, 1)
            parts.append(mixed / total)
        out_ref[start : start + Q_ROWS, :] = jnp.where(halves[0], parts[0], parts[1]).astype(
            jnp.bfloat16
        )


GU_CHUNKS = 4
ROW_CHUNKS = 2
AHEAD = 2


def attend_kernel(
    limit_ref,
    qkv_ref,
    cos_ref,
    sin_ref,
    cache_ref,
    lengths_ref,
    dec_q_ref,
    dec_k_ref,
    dec_v_ref,
    dec_cache_ref,
    w_gu_ref,
    w_out_ref,
    dec_all_ref,
    att_ref,
    gu_ref,
    outw_ref,
    q_rot,
    k_rot,
    v_ext,
    c_ext,
    mixed,
    g_send,
    g_recv,
    g_local,
    b_send,
    b_recv,
    b_local,
    z_send,
    z_recv,
    d_send,
    d_recv,
    d_local,
    e_send,
    e_recv,
    dec_ref,
    dec_cache_v,
    dec_load,
):
    tok_count = lax.axis_size("tok")
    head_count = lax.axis_size("head")
    me = lax.axis_index("tok")
    head = lax.axis_index("head")
    last = head_count - 1
    span, group = qkv_ref.shape[1:]
    piece = span // tok_count
    pair = 2 * HD
    pairs = group // pair

    gathers = []
    for source, target, axis, chunks in (
        (w_gu_ref, gu_ref, 1, GU_CHUNKS),
        (w_out_ref, outw_ref, 0, ROW_CHUNKS),
    ):
        extent = source.shape[0] // chunks
        for chunk in range(chunks):
            at = len(gathers)
            gathers.append(
                PlaneGather(
                    source, target, axis, chunk * extent, extent, g_send.at[at], g_recv.at[at], g_local.at[at]
                )
            )
    total = len(gathers)

    def pump(index):
        gathers[index].relay()
        if index + AHEAD < total:
            gathers[index + AHEAD].start()
        if index > 0:
            gathers[index - 1].relay_far()

    def spot_of(rows, origin, index):
        begin = pl.multiple_of(origin * group + index * pair, pair)
        return att_ref.at[rows, pl.ds(begin, pair)]

    def back(index, offset):
        dest = lax.rem(me + offset, tok_count)
        return pltpu.make_async_remote_copy(
            src_ref=mixed.at[index, pl.ds(pl.multiple_of(dest * piece, piece), piece), :],
            dst_ref=spot_of(pl.ds(pl.multiple_of(me * piece, piece), piece), head, index),
            send_sem=b_send.at[index, offset],
            recv_sem=b_recv.at[index, offset],
            device_id={"tok": dest},
            device_id_type=MESH,
        )

    def back_keep(index):
        mine = pl.ds(pl.multiple_of(me * piece, piece), piece)
        return pltpu.make_async_copy(
            mixed.at[index, mine, :], spot_of(mine, head, index), b_local.at[index]
        )

    def pass_on(way, origin, index):
        block = spot_of(pl.ds(0, span), origin, index)
        target = jnp.minimum(head + 1, last) if way == 0 else jnp.maximum(head - 1, 0)
        return pltpu.make_async_remote_copy(
            src_ref=block,
            dst_ref=block,
            send_sem=z_send.at[way, origin, index],
            recv_sem=z_recv.at[way, origin, index],
            device_id={"head": target},
            device_id_type=MESH,
        )

    goes = (head < last, head > 0)

    def originate(index):
        for offset in range(1, tok_count):
            back(index, offset).wait_recv()
        back_keep(index).wait()
        for way in range(2):

            @pl.when(goes[way])
            def _():
                pass_on(way, head, index).start()

    def relay(index, hop):
        for way in range(2):
            origin = head - hop if way == 0 else head + hop
            there = origin >= 0 if way == 0 else origin <= last

            @pl.when(there)
            def _():
                pass_on(way, origin, index).wait_recv()

                @pl.when(goes[way])
                def _():
                    pass_on(way, origin, index).start()

    dec_pad = dec_ref.shape[0]
    dec_columns = pl.ds(pl.multiple_of(head * group, group), group)
    dec_mine = dec_all_ref.at[pl.ds(pl.multiple_of(me * dec_pad, dec_pad), dec_pad), dec_columns]
    dec_keep = pltpu.make_async_copy(dec_ref, dec_mine, d_local)

    def dec_copy(offset):
        return pltpu.make_async_remote_copy(
            src_ref=dec_ref,
            dst_ref=dec_mine,
            send_sem=d_send.at[offset],
            recv_sem=d_recv.at[offset],
            device_id={"tok": lax.rem(me + offset, tok_count)},
            device_id_type=MESH,
        )

    def dec_spread(offset):
        return pltpu.make_async_remote_copy(
            src_ref=dec_all_ref.at[:, dec_columns],
            dst_ref=dec_all_ref.at[:, dec_columns],
            send_sem=e_send.at[offset],
            recv_sem=e_recv.at[offset],
            device_id={"head": lax.rem(head + offset, head_count)},
            device_id_type=MESH,
        )

    dec_count = dec_q_ref.shape[0]
    dec_loads = [
        pltpu.make_async_copy(
            dec_cache_ref.at[request], dec_cache_v.at[request], dec_load.at[request]
        )
        for request in range(dec_count)
    ]

    def decode():
        line = lax.broadcasted_iota(jnp.int32, (dec_pad, 1), 0)
        result = jnp.zeros((dec_pad, group), jnp.float32)
        for request in range(dec_count):
            dec_loads[request].wait()
            row = decode_one(
                request, lengths_ref[request], dec_q_ref, dec_k_ref, dec_v_ref, dec_cache_v
            )
            result = jnp.where(line == request, row, result)
        dec_ref[...] = result.astype(jnp.bfloat16)
        dec_keep.start()
        for offset in range(1, tok_count):
            dec_copy(offset).start()

    def decode_on():
        dec_keep.wait()
        for offset in range(1, tok_count):
            dec_copy(offset).wait()
        for offset in range(1, head_count):
            dec_spread(offset).start()

    for load in dec_loads:
        load.start()
    greet(("tok", "head"))
    for gather in gathers[:AHEAD]:
        gather.start()

    limit = limit_ref[0]
    every = max(1, pairs // 2)

    def one_pair(index, carry):
        pair_at = pl.ds(pl.multiple_of(index * pair, pair), pair)
        attend_pair(
            limit,
            qkv_ref.at[0],
            qkv_ref.at[1],
            qkv_ref.at[2],
            cos_ref,
            sin_ref,
            cache_ref.at[0],
            pair_at,
            q_rot,
            k_rot,
            v_ext,
            c_ext,
            mixed.at[index],
        )
        for offset in range(1, tok_count):
            back(index, offset).start()
        back_keep(index).start()

        @pl.when(index > 0)
        def _():
            originate(index - 1)

        for turn in range(2):

            @pl.when(index == (turn + 1) * every - 1)
            def _():
                pump(turn)

        return carry

    lax.fori_loop(0, pairs, one_pair, 0)
    originate(pairs - 1)

    def relay_all(hop):
        def body(index, carry):
            relay(index, hop)
            return carry

        lax.fori_loop(0, pairs, body, 0)

    hop = 1
    for index in range(2, total):
        pump(index)
        if hop <= last:
            relay_all(hop)
            hop += 1
        if index == 2:
            decode()
        if index == 3:
            decode_on()
    while hop <= last:
        relay_all(hop)
        hop += 1
    gathers[total - 1].relay_far()
    for offset in range(1, head_count):
        dec_spread(offset).wait()
    for gather in gathers:
        gather.collect()
    for gather in gathers:
        gather.drain()

    def drain(index, carry):
        for offset in range(1, tok_count):
            back(index, offset).wait_send()
        for origin in range(head_count):
            for way in range(2):
                passed = origin <= head if way == 0 else origin >= head

                @pl.when(jnp.logical_and(passed, goes[way]))
                def _():
                    pass_on(way, origin, index).wait_send()

        return carry

    lax.fori_loop(0, pairs, drain, 0)


def attend_layer(qkv, offset, cache, lengths, dec_parts, dec_cache, w_gu, w_out):
    tok_count = lax.axis_size("tok")
    head_count = lax.axis_size("head")
    _, span, group = qkv.shape
    length = cache.shape[2]
    pair = 2 * HD
    pairs = group // pair
    cosine, sine = rope_tables(offset + jnp.arange(span, dtype=jnp.int32), pair)
    any_space = pl.BlockSpec(memory_space=pl.ANY)
    in_vmem = pl.BlockSpec(memory_space=pltpu.VMEM)
    smem = pl.BlockSpec(memory_space=pltpu.SMEM)
    slots = PlaneGather.slots()
    total = GU_CHUNKS + ROW_CHUNKS
    gather_sems = pltpu.SemaphoreType.DMA((total, slots))
    back_sems = pltpu.SemaphoreType.DMA((pairs, tok_count))
    pass_sems = pltpu.SemaphoreType.DMA((2, head_count, pairs))
    return pl.pallas_call(
        attend_kernel,
        out_shape=(
            jax.ShapeDtypeStruct((tok_count * DEC_PAD, head_count * group), jnp.bfloat16),
            jax.ShapeDtypeStruct((span, head_count * group), jnp.bfloat16),
            jax.ShapeDtypeStruct((w_gu.shape[0], tok_count * w_gu.shape[1]), jnp.bfloat16),
            jax.ShapeDtypeStruct((tok_count * w_out.shape[0], w_out.shape[1]), jnp.bfloat16),
        ),
        in_specs=[smem] + [in_vmem] * 4 + [smem] + [in_vmem] * 3 + [any_space] + [in_vmem] * 2,
        out_specs=(in_vmem,) + (any_space,) * 3,
        scratch_shapes=[
            pltpu.VMEM((2, span, pair), jnp.bfloat16),
            pltpu.VMEM((span, pair), jnp.bfloat16),
            pltpu.VMEM((2, span, pair), jnp.bfloat16),
            pltpu.VMEM((2, length, pair), jnp.bfloat16),
            pltpu.VMEM((pairs, span, pair), jnp.bfloat16),
            gather_sems,
            gather_sems,
            pltpu.SemaphoreType.DMA((total,)),
            back_sems,
            back_sems,
            pltpu.SemaphoreType.DMA((pairs,)),
            pass_sems,
            pass_sems,
            pltpu.SemaphoreType.DMA((tok_count,)),
            pltpu.SemaphoreType.DMA((tok_count,)),
            pltpu.SemaphoreType.DMA,
            pltpu.SemaphoreType.DMA((head_count,)),
            pltpu.SemaphoreType.DMA((head_count,)),
            pltpu.VMEM((DEC_PAD, group), jnp.bfloat16),
            pltpu.VMEM(dec_cache.shape, jnp.bfloat16),
            pltpu.SemaphoreType.DMA((dec_cache.shape[0],)),
        ],
        compiler_params=pltpu.CompilerParams(
            collective_id=2, has_side_effects=True, vmem_limit_bytes=56 * 1024 * 1024
        ),
        cost_estimate=pl.CostEstimate(
            flops=16 * span * 3 * span * group,
            bytes_accessed=4 * length * group + 8 * span * group,
            transcendentals=span * 3 * span * group // HD,
        ),
        name="attend_layer",
    )(offset[None], qkv, cosine, sine, cache, lengths, *dec_parts, dec_cache, w_gu, w_out)


def unpermute_kernel(order_ref, source_ref, target_ref, held, in_sem, out_sem):
    count = source_ref.shape[0]
    ins = [
        pltpu.make_async_copy(source_ref.at[index], held.at[index], in_sem.at[index])
        for index in range(count)
    ]
    outs = [
        pltpu.make_async_copy(
            held.at[index], target_ref.at[order_ref[index]], out_sem.at[index]
        )
        for index in range(count)
    ]
    for copy in ins:
        copy.start()
    for index in range(count):
        ins[index].wait()
        outs[index].start()
    for copy in outs:
        copy.wait()


def unpermuted(blocks, order):
    any_space = pl.BlockSpec(memory_space=pl.ANY)
    return pl.pallas_call(
        unpermute_kernel,
        out_shape=jax.ShapeDtypeStruct(blocks.shape, blocks.dtype),
        in_specs=[pl.BlockSpec(memory_space=pltpu.SMEM), any_space],
        out_specs=any_space,
        scratch_shapes=[
            pltpu.VMEM(blocks.shape, blocks.dtype),
            pltpu.SemaphoreType.DMA((blocks.shape[0],)),
            pltpu.SemaphoreType.DMA((blocks.shape[0],)),
        ],
        compiler_params=pltpu.CompilerParams(vmem_limit_bytes=58 * 1024 * 1024),
        name="unpermute",
    )(order, blocks)


def mlp_kernel(
    head_count,
    order_ref,
    att_ref,
    rows_ref,
    dec_att_ref,
    dec_rows_ref,
    gain_ref,
    w_out_ref,
    w_gu_ref,
    w_down_ref,
    out_ref,
    dec_out_ref,
    hidden,
    w_out_v,
    w_gu_v,
    w_down_v,
    resid,
    mlp_in,
    wide_v,
    slots,
    dec_slots,
    load_sem,
    rs_send,
    rs_recv,
    ag_send,
    ag_recv,
    keep_sem,
    dec_send,
    dec_recv,
    g_send,
    g_recv,
    g_local,
):
    last = head_count - 1
    me = lax.axis_index("head")
    span, width = att_ref.shape
    half = span // 2
    count = half // CHUNK
    units = w_gu_ref.shape[0] // 2
    pieces, piece = rows_ref.shape[:2]
    dec = dec_att_ref.shape[0]
    group = (wide_v.shape[0] - dec) // 2

    loads = [
        pltpu.make_async_copy(att_ref, hidden.at[pl.ds(0, span), pl.ds(0, width)], load_sem.at[0]),
        pltpu.make_async_copy(w_out_ref, w_out_v, load_sem.at[1]),
        pltpu.make_async_copy(w_gu_ref, w_gu_v, load_sem.at[2]),
    ]
    for copy in loads:
        copy.start()
    extent = w_down_ref.shape[0] // ROW_CHUNKS
    gathers = [
        PlaneGather(
            w_down_ref, w_down_v, 0, chunk * extent, extent, g_send.at[chunk], g_recv.at[chunk], g_local.at[chunk]
        )
        for chunk in range(ROW_CHUNKS)
    ]
    greet(("tok", "head"))
    for gather in gathers:
        gather.start()
    hidden[span:, :width] = dec_att_ref[...]

    def begin_rows(index, carry):
        at = pl.ds(pl.multiple_of(index * piece, piece), piece)
        resid[at, :] = rows_ref[order_ref[index]].astype(jnp.float32)
        return carry

    lax.fori_loop(0, pieces, begin_rows, 0)
    resid[span:, :] = dec_rows_ref[...].astype(jnp.float32)
    loads[0].wait()
    loads[1].wait()
    out_tile, out_tiles = tiles_of(width)
    unit_tile, unit_tiles = tiles_of(units)

    def rows_in(begin, block):
        at = slice(begin, begin + block)

        def project(tile, squares):
            columns = pl.ds(pl.multiple_of(tile * out_tile, out_tile), out_tile)
            value = resid[at, columns] + nt_dot(hidden[at, :width], w_out_v[columns, :])
            resid[at, columns] = value
            return squares + jnp.sum(value * value, axis=-1, keepdims=True)

        squares = lax.fori_loop(0, out_tiles, project, jnp.zeros((block, 1), jnp.float32))
        factor = lax.rsqrt(squares / width + norm_eps)
        mlp_in[:block, :] = (resid[at, :] * factor * gain_ref[...]).astype(jnp.bfloat16)
        if begin == 0:
            loads[2].wait()

        def gate_up(tile, carry):
            begin = pl.multiple_of(tile * unit_tile, unit_tile)
            gate = 0.5 * nt_dot(mlp_in[:block, :], w_gu_v[pl.ds(begin, unit_tile), :])
            up = nt_dot(mlp_in[:block, :], w_gu_v[pl.ds(units + begin, unit_tile), :])
            hidden[at, pl.ds(begin, unit_tile)] = (
                (gate + gate * jnp.tanh(gate)) * up
            ).astype(jnp.bfloat16)
            return carry

        lax.fori_loop(0, unit_tiles, gate_up, 0)

    rows_in(0, half)
    for gather in gathers:
        gather.relay()
    rows_in(half, half + dec)
    for gather in gathers:
        gather.relay_far()
    for gather in gathers:
        gather.collect()

    spot = lax.broadcasted_iota(jnp.int32, (2 * group, 1), 0)
    owner = jnp.where(spot < group, 0, last)
    owned = jnp.where(owner == me, 1.0, 0.0).astype(jnp.float32)
    wide_v[2 * group :, :] = hidden[span:, :units]

    def dec_copy(offset):
        return pltpu.make_async_remote_copy(
            src_ref=dec_slots.at[me],
            dst_ref=dec_slots.at[me],
            send_sem=dec_send.at[offset],
            recv_sem=dec_recv.at[offset],
            device_id={"head": lax.rem(me + offset, head_count)},
            device_id_type=MESH,
        )

    def compute(index):
        spots = [
            pl.ds(pl.multiple_of(side * half + index * group, group), group) for side in range(2)
        ]
        for side in range(2):
            wide_v[side * group : (side + 1) * group, :] = hidden[spots[side], :units]

        def down(tile, carry):
            columns = pl.ds(pl.multiple_of(tile * out_tile, out_tile), out_tile)
            value = nt_dot(wide_v[...], w_down_v[columns, :])
            for side in range(2):
                mine = slice(side * group, (side + 1) * group)
                resid[spots[side], columns] = (
                    value[mine] + resid[spots[side], columns] * owned[mine]
                )

            @pl.when(index == 0)
            def _():
                dec_slots[me, :, columns] = value[2 * group :].astype(jnp.bfloat16)

            return carry

        lax.fori_loop(0, out_tiles, down, 0)

        @pl.when(index == 0)
        def _():
            for offset in range(1, head_count):
                dec_copy(offset).start()

    def out_rows(side, index):
        return out_ref.at[pl.ds(pl.multiple_of(side * half + index * CHUNK, CHUNK), CHUNK)]

    def next_of(side):
        return jnp.maximum(me - 1, 0) if side == 0 else jnp.minimum(me + 1, last)

    def before_of(side):
        return next_of(1 - side)

    def sum_copy(side, index):
        return pltpu.make_async_remote_copy(
            src_ref=slots.at[side, index],
            dst_ref=slots.at[side, index],
            send_sem=rs_send.at[side, index],
            recv_sem=rs_recv.at[side, index],
            device_id={"head": next_of(side)},
            device_id_type=MESH,
        )

    def final_copy(side, index, source):
        return pltpu.make_async_remote_copy(
            src_ref=source,
            dst_ref=out_rows(side, index),
            send_sem=ag_send.at[side, index],
            recv_sem=ag_recv.at[side, index],
            device_id={"head": before_of(side)},
            device_id_type=MESH,
        )

    def keep_copy(side, index):
        return pltpu.make_async_copy(
            slots.at[side, index], out_rows(side, index), keep_sem.at[side, index]
        )

    hops = [last - me, me]
    to_end = [me, last - me]

    def combine(side, index):
        mine = pl.ds(pl.multiple_of(side * half + index * CHUNK, CHUNK), CHUNK)

        @pl.when(hops[side] == 0)
        def _():
            slots[side, index] = resid[mine, :].astype(jnp.bfloat16)

        @pl.when(hops[side] > 0)
        def _():
            sum_copy(side, index).wait_recv()
            slots[side, index] = (
                resid[mine, :] + slots[side, index].astype(jnp.float32)
            ).astype(jnp.bfloat16)

        @pl.when(to_end[side] > 0)
        def _():
            sum_copy(side, index).start()

        @pl.when(to_end[side] == 0)
        def _():
            final_copy(side, index, slots.at[side, index]).start()
            keep_copy(side, index).start()

    def forward(side, index):
        final_copy(side, index, out_rows(side, index)).wait_recv()

        @pl.when(hops[side] > 0)
        def _():
            final_copy(side, index, out_rows(side, index)).start()

    every = group // CHUNK

    def tick(step, carry):
        @pl.when(jnp.logical_and(step < count, lax.rem(step, every) == 0))
        def _():
            compute(step // every)

        for side in range(2):
            index = step - LAG * hops[side]

            @pl.when(jnp.logical_and(index >= 0, index < count))
            def _():
                combine(side, index)

        for side in range(2):
            spread = step - LAG * (last + to_end[side])

            @pl.when(
                jnp.logical_and(
                    to_end[side] > 0, jnp.logical_and(spread >= 0, spread < count)
                )
            )
            def _():
                forward(side, spread)

        return carry

    lax.fori_loop(0, count + 2 * LAG * last, tick, 0)

    for offset in range(1, head_count):
        dec_copy(offset).wait()
    total = resid[span:, :]
    for index in range(head_count):
        total = total + dec_slots[index].astype(jnp.float32)
    dec_out_ref[...] = total.astype(jnp.bfloat16)

    for gather in gathers:
        gather.drain()

    def drain(index, carry):
        for side in range(2):

            @pl.when(to_end[side] > 0)
            def _():
                sum_copy(side, index).wait_send()

            @pl.when(to_end[side] == 0)
            def _():
                keep_copy(side, index).wait()

            @pl.when(hops[side] > 0)
            def _():
                final_copy(side, index, out_rows(side, index)).wait_send()

        return carry

    lax.fori_loop(0, count, drain, 0)


def mlp_layer(pre_order, att, rows, dec_att, dec_rows, gain, w_out, w_gu, w_down):
    head_count = lax.axis_size("head")
    tok_count = lax.axis_size("tok")
    span, width = att.shape
    units = w_gu.shape[0] // 2
    count = span // 2 // CHUNK
    dec = dec_att.shape[0]
    group = min(GROUP_ROWS, span // 2)
    any_space = pl.BlockSpec(memory_space=pl.ANY)
    in_vmem = pl.BlockSpec(memory_space=pltpu.VMEM)
    both = pltpu.SemaphoreType.DMA((2, count))
    gather_sems = pltpu.SemaphoreType.DMA((ROW_CHUNKS, PlaneGather.slots()))
    return pl.pallas_call(
        functools.partial(mlp_kernel, head_count),
        out_shape=(
            jax.ShapeDtypeStruct((span, width), jnp.bfloat16),
            jax.ShapeDtypeStruct((dec, width), jnp.bfloat16),
        ),
        in_specs=[pl.BlockSpec(memory_space=pltpu.SMEM), any_space]
        + [in_vmem] * 4
        + [any_space] * 3,
        out_specs=(any_space, in_vmem),
        scratch_shapes=[
            pltpu.VMEM((span + dec, max(width, units)), jnp.bfloat16),
            pltpu.VMEM(w_out.shape, jnp.bfloat16),
            pltpu.VMEM(w_gu.shape, jnp.bfloat16),
            pltpu.VMEM((tok_count * w_down.shape[0], units), jnp.bfloat16),
            pltpu.VMEM((span + dec, width), jnp.float32),
            pltpu.VMEM((span // 2 + dec, width), jnp.bfloat16),
            pltpu.VMEM((2 * group + dec, units), jnp.bfloat16),
            pltpu.VMEM((2, count, CHUNK, width), jnp.bfloat16),
            pltpu.VMEM((head_count, dec, width), jnp.bfloat16),
            pltpu.SemaphoreType.DMA((3,)),
            both,
            both,
            both,
            both,
            both,
            pltpu.SemaphoreType.DMA((head_count,)),
            pltpu.SemaphoreType.DMA((head_count,)),
            gather_sems,
            gather_sems,
            pltpu.SemaphoreType.DMA((ROW_CHUNKS,)),
        ],
        compiler_params=pltpu.CompilerParams(
            collective_id=3, has_side_effects=True, vmem_limit_bytes=60 * 1024 * 1024
        ),
        cost_estimate=pl.CostEstimate(
            flops=2 * span * width * (width + 3 * units),
            bytes_accessed=2 * (4 * span * width + w_out.size + w_gu.size + w_down.size),
            transcendentals=span * units,
        ),
        name="mlp_layer",
    )(pre_order, att, rows, dec_att, dec_rows, gain[None], w_out, w_gu, w_down)


def picked_rows(rows, order):
    count = rows.shape[0]
    picker = order[:, None] == jnp.arange(count, dtype=jnp.int32)[None, :]
    return jnp.dot(
        picker.astype(jnp.bfloat16), rows, preferred_element_type=jnp.float32
    ).astype(jnp.bfloat16)


def inverse_of(order):
    spots = jnp.arange(order.shape[0], dtype=jnp.int32)
    return jnp.sum(jnp.where(order[None, :] == spots[:, None], spots[None, :], 0), axis=1)


def on_device(
    pre_tokens,
    dec_tokens,
    attn_gain,
    mlp_gain,
    w_qkv,
    w_out,
    w_gate_up,
    w_down,
    pre_cache,
    dec_cache,
    pre_order,
    dec_order,
    pre_offsets,
    dec_lengths,
):
    tok_count = lax.axis_size("tok")
    tok_index = lax.axis_index("tok")
    head_count = lax.axis_size("head")
    span_rows, width = pre_tokens.shape
    piece_len = span_rows // tok_count
    dec_local = dec_tokens.shape[0]
    group_width, depth = w_qkv.shape[1:]
    units = w_gate_up.shape[1]

    blocks = pre_tokens.reshape(tok_count, piece_len, width)
    packed = dec_tokens.reshape(dec_local, width // depth, depth)
    packed = jnp.transpose(packed, (1, 0, 2)).reshape(dec_local * width // depth, depth)
    qkv, dec_qkv, dec_rows = project_layer(
        pre_order, blocks, packed, attn_gain, w_qkv.reshape(3 * group_width, depth)
    )
    w_out_rows = lax.all_gather(w_out, "head", axis=1, tiled=True)

    own_slots = lax.dynamic_slice_in_dim(dec_order, tok_index * dec_local, dec_local)
    dec_mine = jnp.stack([picked_rows(dec_qkv[which], own_slots) for which in range(3)])

    dec_all, attended, gate_up_full, out_full = attend_layer(
        qkv,
        pre_offsets[0],
        pre_cache,
        dec_lengths,
        decode_inputs(dec_mine, dec_lengths),
        dec_cache,
        w_gate_up.reshape(2 * units, depth),
        w_out_rows,
    )
    dec_spots = inverse_of(dec_order)
    dec_spots = dec_spots // dec_local * DEC_PAD + dec_spots % dec_local
    dec_all = picked_rows(dec_all, dec_spots)
    pre_out, dec_out = mlp_layer(
        pre_order,
        attended,
        blocks,
        dec_all,
        dec_rows,
        mlp_gain,
        out_full,
        gate_up_full,
        w_down,
    )
    pre_out = unpermuted(pre_out.reshape(tok_count, piece_len, width), pre_order)
    dec_out = lax.dynamic_slice_in_dim(dec_out, tok_index * dec_local, dec_local)
    return (pre_out.reshape(span_rows, width), dec_out)


def solution(mesh):
    placed = (
        P("tok", None),
        P("tok", None),
        P(),
        P(),
        P(None, "head", "tok"),
        P("tok", "head"),
        P(None, "head", "tok"),
        P("tok", "head"),
        P("tok", None, None, "head"),
        P("tok", None, None, "head"),
        P(),
        P(),
        P("tok"),
        P("tok"),
    )
    return jax.shard_map(
        on_device,
        mesh=mesh,
        in_specs=placed,
        out_specs=(P("tok", None), P("tok", None)),
        check_vma=False,
    )
```
